32 devices in a mesh: row: 4 (over y, x), col: 8 (over z, core).
Axes of the slice: x: 2, y: 2, z: 4, core: 2. Of those that a mesh axis runs over, the one named last changes fastest.
Arguments:
- tokens: bfloat16 [256, 8192], P('col', 'row'), may hold values from -500 to 500
- norm_gain: float32 [8192], P('row'), may hold values from 0.5 to 1.5
- cotangent: bfloat16 [256, 8192], P('col', 'row'), may hold values from -6 to 6
- gate_frozen_weight: bfloat16 [8192, 28672], P('row', 'col'), may hold values from -0.0625 to 0.0625
- up_frozen_weight: bfloat16 [8192, 28672], P('row', 'col'), may hold values from -0.0625 to 0.0625
- down_frozen_weight: bfloat16 [28672, 8192], P('col', 'row'), may hold values from -0.03125 to 0.03125
- gate_input_factor: bfloat16 [8192, 64], P('row'), may hold values from -0.0625 to 0.0625
- gate_output_factor: bfloat16 [64, 28672], P(None, 'col'), may hold values from -0.75 to 0.75
- up_input_factor: bfloat16 [8192, 64], P('row'), may hold values from -0.0625 to 0.0625
- up_output_factor: bfloat16 [64, 28672], P(None, 'col'), may hold values from -0.75 to 0.75
- down_input_factor: bfloat16 [28672, 64], P('col'), may hold values from -0.03125 to 0.03125
- down_b: bfloat16 [64, 8192], P(None, 'row'), may hold values from -0.75 to 0.75
- gate_input_factor_direction: bfloat16 [8192, 64], P('row'), may hold values from -0.0625 to 0.0625
- gate_output_factor_direction: bfloat16 [64, 28672], P(None, 'col'), may hold values from -0.75 to 0.75
- up_input_factor_direction: bfloat16 [8192, 64], P('row'), may hold values from -0.0625 to 0.0625
- up_output_factor_direction: bfloat16 [64, 28672], P(None, 'col'), may hold values from -0.75 to 0.75
- down_input_factor_direction: bfloat16 [28672, 64], P('col'), may hold values from -0.03125 to 0.03125
- down_b_dir: bfloat16 [64, 8192], P(None, 'row'), may hold values from -0.75 to 0.75
Outputs:
- normed_feature_adjoint: float32 [256, 8192], P('col', 'row')
- normed_feature_adjoint_direction: float32 [256, 8192], P('col', 'row')
- curvature_gate_input: float32 [8192, 64], P('row')
- curvature_gate_output: float32 [64, 28672], P(None, 'col')
- curvature_up_input: float32 [8192, 64], P('row')
- curvature_up_output: float32 [64, 28672], P(None, 'col')
- curvature_down_input: float32 [28672, 64], P('col')
- curvature_down_output: float32 [64, 8192], P(None, 'row')
The draws below stay inside these ranges and needn't reach their ends.
All inputs are finite; a program needn't handle non-finite values.
Results may differ from the reference program's by a relative error of at most 0.024.
Values may be sent and summed in bfloat16 or wider, within the bound.
A program may use at most 128 MiB of HBM per device.

```python
import jax
import jax.numpy as jnp
from jax import lax

D = 8192
FF = 28672
R = 64
TOKENS = 256


def draw_tokens(key, part):
    base_key = jax.random.fold_in(key, 11)
    noise_key, column_key, row_key = jax.random.split(base_key, 3)
    position = jnp.arange(D, dtype=jnp.float32) / D
    column_scale = jnp.power(10.0, 0.6 * position + 0.4 * jax.random.uniform(column_key, (D,), jnp.float32))
    values = jnp.clip(jax.random.normal(noise_key, (TOKENS, D), jnp.float32), -4.0, 4.0)
    row_scale = jnp.power(10.0, jax.random.uniform(row_key, (TOKENS, 1), jnp.float32))
    return (values * row_scale * column_scale).astype(jnp.bfloat16)


def shard_levels(stream_key, dims, cuts, least, top_value):
    factor_of = 1.0
    for axis_at, shards_of in cuts:
        heights = jax.random.uniform(jax.random.fold_in(jax.random.fold_in(stream_key, 6), axis_at), (shards_of,), jnp.float32, least / len(cuts), top_value / len(cuts))
        factor_of = factor_of * jnp.repeat(jnp.exp(heights), dims[axis_at] // shards_of).reshape((-1,) + (1,) * (len(dims) - 1 - axis_at))
    return factor_of


def scatter_about(key, shape, deviation, bound, cuts=(), held_as=jnp.bfloat16):
    values = deviation * jax.random.normal(key, shape, jnp.float32)
    if cuts:
        values = values * shard_levels(key, shape, cuts, -0.22, 0.18)
    return jnp.clip(values, -bound, bound).astype(held_as)


def setup_inputs(seed: int = 0) -> dict:
    key_of = jax.random.split(jax.random.key(seed), 19)
    return {
        "tokens": draw_tokens(jax.random.fold_in(key_of[18], 71), 0),
        "norm_gain": jnp.clip(1.0 + 0.1 * jax.random.normal(key_of[1], (D,), jnp.float32), 0.5, 1.5),
        "cotangent": scatter_about(key_of[2], (TOKENS, D), 1.0, 6.0, ((0, 8), (1, 4))),
        "gate_frozen_weight": scatter_about(key_of[3], (D, FF), D ** -0.5, 0.0625, ((0, 4), (1, 8))),
        "up_frozen_weight": scatter_about(key_of[4], (D, FF), D ** -0.5, 0.0625, ((0, 4), (1, 8))),
        "down_frozen_weight": scatter_about(key_of[5], (FF, D), FF ** -0.5, 0.03125, ((0, 8), (1, 4))),
        "gate_input_factor": scatter_about(key_of[6], (D, R), D ** -0.5, 0.0625, ((0, 4),)),
        "gate_output_factor": scatter_about(key_of[7], (R, FF), R ** -0.5, 0.75, ((1, 8),)),
        "up_input_factor": scatter_about(key_of[8], (D, R), D ** -0.5, 0.0625, ((0, 4),)),
        "up_output_factor": scatter_about(key_of[9], (R, FF), R ** -0.5, 0.75, ((1, 8),)),
        "down_input_factor": scatter_about(key_of[10], (FF, R), FF ** -0.5, 0.03125, ((0, 8),)),
        "down_b": scatter_about(key_of[11], (R, D), R ** -0.5, 0.75, ((1, 4),)),
        "gate_input_factor_direction": scatter_about(key_of[12], (D, R), D ** -0.5, 0.0625, ((0, 4),)),
        "gate_output_factor_direction": scatter_about(key_of[13], (R, FF), R ** -0.5, 0.75, ((1, 8),)),
        "up_input_factor_direction": scatter_about(key_of[14], (D, R), D ** -0.5, 0.0625, ((0, 4),)),
        "up_output_factor_direction": scatter_about(key_of[15], (R, FF), R ** -0.5, 0.75, ((1, 8),)),
        "down_input_factor_direction": scatter_about(key_of[16], (FF, R), FF ** -0.5, 0.03125, ((0, 8),)),
        "down_b_dir": scatter_about(key_of[17], (R, D), R ** -0.5, 0.75, ((1, 4),)),
    }


adapter_scale = 0.5
epsilon = 1e-05

def curvature_product(left, right):
    return jnp.dot(left, right, preferred_element_type=jnp.float32)

def cross_shard_total(left, right):
    return lax.dot_general(left, right, (((1,), (1,)), ((), ())), preferred_element_type=jnp.float32)

def summed_over_rows(left, right):
    return lax.dot_general(left, right, (((0,), (0,)), ((), ())), preferred_element_type=jnp.float32)

def exact_row_values(left, right):
    return lax.dot_general(left.astype(jnp.float32), right.astype(jnp.float32), (((0,), (0,)), ((), ())), precision=lax.Precision.HIGHEST)

def exact_cross_total(left, right):
    return lax.dot_general(left.astype(jnp.float32), right.astype(jnp.float32), (((1,), (1,)), ((), ())), precision=lax.Precision.HIGHEST)

def second_order(gate_preactivation, up_preactivation, hidden_adjoint, gate_tangent_rows, up_tangent_rows, adjoint_tangent_rows):
    sigma = jax.nn.sigmoid(gate_preactivation)
    silu_value = gate_preactivation * sigma
    slope = sigma * (1.0 + gate_preactivation * (1.0 - sigma))
    bend = sigma * (1.0 - sigma) * (2.0 + gate_preactivation * (1.0 - 2.0 * sigma))
    hidden_activation = (silu_value * up_preactivation).astype(jnp.bfloat16)
    hidden_direction = (slope * gate_tangent_rows * up_preactivation + silu_value * up_tangent_rows).astype(jnp.bfloat16)
    gate_derivative = (hidden_adjoint * up_preactivation * slope).astype(jnp.bfloat16)
    up_derivative = (hidden_adjoint * silu_value).astype(jnp.bfloat16)
    gate_derivative_direction = (adjoint_tangent_rows * up_preactivation * slope + hidden_adjoint * (up_tangent_rows * slope + up_preactivation * bend * gate_tangent_rows)).astype(jnp.bfloat16)
    up_derivative_direction = (adjoint_tangent_rows * silu_value + hidden_adjoint * slope * gate_tangent_rows).astype(jnp.bfloat16)
    return (hidden_activation, hidden_direction, gate_derivative, up_derivative, gate_derivative_direction, up_derivative_direction)

def reference(tokens, norm_gain, cotangent, gate_frozen_weight, up_frozen_weight, down_frozen_weight, gate_input_factor, gate_output_factor, up_input_factor, up_output_factor, down_input_factor, down_b, gate_input_factor_direction, gate_output_factor_direction, up_input_factor_direction, up_output_factor_direction, down_input_factor_direction, down_b_dir):
    tokens_f = tokens.astype(jnp.float32)
    inv_rms = lax.rsqrt(lax.optimization_barrier(jnp.sum(tokens_f * tokens_f, axis=1, keepdims=True)) / D + epsilon)
    normed_tokens = (tokens_f * inv_rms * norm_gain).astype(jnp.bfloat16)
    ranks = jnp.concatenate([curvature_product(normed_tokens, gate_input_factor), curvature_product(normed_tokens, up_input_factor), curvature_product(normed_tokens, gate_input_factor_direction), curvature_product(normed_tokens, up_input_factor_direction), cross_shard_total(cotangent, down_b), cross_shard_total(cotangent, down_b_dir)], axis=1).astype(jnp.bfloat16)
    gate_rank_rows = ranks[:, 0:R]
    up_rank_rows = ranks[:, R:2 * R]
    gate_rank_rows_direction = ranks[:, 2 * R:3 * R]
    up_rank_rows_direction = ranks[:, 3 * R:4 * R]
    adjoint_rank_rows = ranks[:, 4 * R:5 * R]
    adjoint_rank_rows_direction = ranks[:, 5 * R:6 * R]
    gate_preactivation = curvature_product(normed_tokens, gate_frozen_weight) + adapter_scale * curvature_product(gate_rank_rows, gate_output_factor)
    up_preactivation = curvature_product(normed_tokens, up_frozen_weight) + adapter_scale * curvature_product(up_rank_rows, up_output_factor)
    hidden_adjoint = cross_shard_total(cotangent, down_frozen_weight) + adapter_scale * cross_shard_total(adjoint_rank_rows, down_input_factor)
    gate_tangent_rows = adapter_scale * (curvature_product(gate_rank_rows_direction, gate_output_factor) + curvature_product(gate_rank_rows, gate_output_factor_direction))
    up_tangent_rows = adapter_scale * (curvature_product(up_rank_rows_direction, up_output_factor) + curvature_product(up_rank_rows, up_output_factor_direction))
    adjoint_tangent_rows = adapter_scale * (cross_shard_total(adjoint_rank_rows_direction, down_input_factor) + cross_shard_total(adjoint_rank_rows, down_input_factor_direction))
    hidden_activation, hidden_direction, gate_derivative, up_derivative, gate_derivative_direction, up_derivative_direction = second_order(gate_preactivation, up_preactivation, hidden_adjoint, gate_tangent_rows, up_tangent_rows, adjoint_tangent_rows)
    gate_quotient = cross_shard_total(gate_derivative, gate_output_factor)
    up_quotient = cross_shard_total(up_derivative, up_output_factor)
    gate_quotient_direction = cross_shard_total(gate_derivative_direction, gate_output_factor) + cross_shard_total(gate_derivative, gate_output_factor_direction)
    up_quotient_direction = cross_shard_total(up_derivative_direction, up_output_factor) + cross_shard_total(up_derivative, up_output_factor_direction)
    rank_direction = curvature_product(hidden_direction, down_input_factor) + curvature_product(hidden_activation, down_input_factor_direction)
    normed_feature_adjoint = cross_shard_total(gate_derivative, gate_frozen_weight) + cross_shard_total(up_derivative, up_frozen_weight) + adapter_scale * (exact_cross_total(gate_quotient, gate_input_factor) + exact_cross_total(up_quotient, up_input_factor))
    normed_feature_adjoint_direction = cross_shard_total(gate_derivative_direction, gate_frozen_weight) + cross_shard_total(up_derivative_direction, up_frozen_weight) + adapter_scale * (exact_cross_total(gate_quotient_direction, gate_input_factor) + exact_cross_total(gate_quotient, gate_input_factor_direction) + exact_cross_total(up_quotient_direction, up_input_factor) + exact_cross_total(up_quotient, up_input_factor_direction))
    curvature_gate_input = adapter_scale * exact_row_values(normed_tokens, gate_quotient_direction)
    curvature_up_input = adapter_scale * exact_row_values(normed_tokens, up_quotient_direction)
    curvature_gate_output = adapter_scale * (summed_over_rows(gate_rank_rows_direction, gate_derivative) + summed_over_rows(gate_rank_rows, gate_derivative_direction))
    curvature_up_output = adapter_scale * (summed_over_rows(up_rank_rows_direction, up_derivative) + summed_over_rows(up_rank_rows, up_derivative_direction))
    curvature_down_input = adapter_scale * (summed_over_rows(hidden_direction, adjoint_rank_rows) + summed_over_rows(hidden_activation, adjoint_rank_rows_direction))
    curvature_down_output = adapter_scale * exact_row_values(rank_direction, cotangent)
    return (normed_feature_adjoint, normed_feature_adjoint_direction, curvature_gate_input, curvature_gate_output, curvature_up_input, curvature_up_output, curvature_down_input, curvature_down_output)
```

```python
import functools

import jax
import jax.numpy as jnp
from jax import lax
from jax.experimental import pallas as pl
from jax.experimental.pallas import tpu as pltpu
from jax.sharding import PartitionSpec as P

adapter_scale = 0.5
epsilon = 1e-05
MESH = pl.DeviceIdType.MESH


def total_kernel(axis, n, x_ref, o_ref, inbox, whole, send1, recv1, send2, recv2):
    me = lax.axis_index(axis)
    barrier = pltpu.get_barrier_semaphore()

    @pl.loop(1, n)
    def _(k):
        pl.semaphore_signal(
            barrier, inc=1, device_id={axis: lax.rem(me + k, n)}, device_id_type=MESH
        )

    pl.semaphore_wait(barrier, n - 1)

    def scatter(k):
        peer = lax.rem(me + k, n)
        return pltpu.make_async_remote_copy(
            src_ref=x_ref.at[peer],
            dst_ref=inbox.at[k],
            send_sem=send1.at[k],
            recv_sem=recv1.at[k],
            device_id={axis: peer},
            device_id_type=MESH,
        )

    def spread(k):
        peer = lax.rem(me + k, n)
        return pltpu.make_async_remote_copy(
            src_ref=whole.at[me],
            dst_ref=whole.at[me],
            send_sem=send2.at[k],
            recv_sem=recv2.at[k],
            device_id={axis: peer},
            device_id_type=MESH,
        )

    def arrival(k):
        origin = lax.rem(me - k + n, n)
        return pltpu.make_async_remote_copy(
            src_ref=whole.at[origin],
            dst_ref=whole.at[origin],
            send_sem=send2.at[k],
            recv_sem=recv2.at[k],
            device_id={axis: origin},
            device_id_type=MESH,
        )

    @pl.loop(1, n)
    def _(k):
        scatter(k).start()

    def add(k, total):
        scatter(k).wait_recv()
        return total + inbox[k].astype(jnp.float32)

    total = lax.fori_loop(1, n, add, x_ref[me].astype(jnp.float32))
    whole[me] = total.astype(whole.dtype)

    @pl.loop(1, n)
    def _(k):
        spread(k).start()

    @pl.loop(1, n)
    def _(k):
        arrival(k).wait_recv()

    @pl.loop(1, n)
    def _(k):
        scatter(k).wait_send()
        spread(k).wait_send()

    o_ref[...] = whole[...]


def shard_total(x, axis, collective_id):
    n = lax.axis_size(axis)
    rows, columns = x.shape
    block = (n, rows // n, columns)
    total = pl.pallas_call(
        functools.partial(total_kernel, axis, n),
        out_shape=jax.ShapeDtypeStruct(block, jnp.bfloat16),
        in_specs=[pl.BlockSpec(memory_space=pltpu.VMEM)],
        out_specs=pl.BlockSpec(memory_space=pltpu.VMEM),
        scratch_shapes=[
            pltpu.VMEM(block, x.dtype),
            pltpu.VMEM(block, jnp.bfloat16),
            pltpu.SemaphoreType.DMA((n,)),
            pltpu.SemaphoreType.DMA((n,)),
            pltpu.SemaphoreType.DMA((n,)),
            pltpu.SemaphoreType.DMA((n,)),
        ],
        compiler_params=pltpu.CompilerParams(collective_id=collective_id, has_side_effects=True),
        name=f"total_{axis}",
    )(x.reshape(block))
    return total.reshape(rows, columns)


def curvature_product(left, right):
    return jnp.dot(left, right, preferred_element_type=jnp.float32)


def cross_shard_total(left, right):
    return lax.dot_general(
        left, right, (((1,), (1,)), ((), ())), preferred_element_type=jnp.float32
    )


def summed_over_rows(left, right):
    return lax.dot_general(
        left, right, (((0,), (0,)), ((), ())), preferred_element_type=jnp.float32
    )


def second_order(
    gate_preactivation,
    up_preactivation,
    hidden_adjoint,
    gate_tangent_rows,
    up_tangent_rows,
    adjoint_tangent_rows,
):
    sigma = jax.nn.sigmoid(gate_preactivation)
    silu_value = gate_preactivation * sigma
    slope = sigma * (1.0 + gate_preactivation * (1.0 - sigma))
    bend = sigma * (1.0 - sigma) * (2.0 + gate_preactivation * (1.0 - 2.0 * sigma))
    hidden_activation = (silu_value * up_preactivation).astype(jnp.bfloat16)
    hidden_direction = (
        slope * gate_tangent_rows * up_preactivation + silu_value * up_tangent_rows
    ).astype(jnp.bfloat16)
    gate_derivative = (hidden_adjoint * up_preactivation * slope).astype(jnp.bfloat16)
    up_derivative = (hidden_adjoint * silu_value).astype(jnp.bfloat16)
    gate_derivative_direction = (
        adjoint_tangent_rows * up_preactivation * slope
        + hidden_adjoint * (up_tangent_rows * slope + up_preactivation * bend * gate_tangent_rows)
    ).astype(jnp.bfloat16)
    up_derivative_direction = (
        adjoint_tangent_rows * silu_value + hidden_adjoint * slope * gate_tangent_rows
    ).astype(jnp.bfloat16)
    return (
        hidden_activation,
        hidden_direction,
        gate_derivative,
        up_derivative,
        gate_derivative_direction,
        up_derivative_direction,
    )


def lora_kernel(
    lead,
    tokens,
    gain,
    cot,
    gate_hbm,
    up_hbm,
    down_hbm,
    gate_in,
    gate_in_dir,
    up_in,
    up_in_dir,
    down_b,
    down_b_dir,
    gate_out,
    gate_out_dir,
    up_out,
    up_out_dir,
    down_in,
    down_in_dir,
    primal_ref,
    dir_ref,
    gate_curve_in,
    gate_curve,
    up_curve_in,
    up_curve,
    down_curve,
    down_curve_out,
    x_buf,
    cot_buf,
    squares,
    rank_part,
    rank_in,
    rank_all,
    in_rows,
    out_rows,
    wide_buf,
    down_buf,
    own_parts,
    own_first,
    own_mid_out,
    own_mid_in,
    own_whole,
    rest_parts,
    rest_first,
    rest_mid_out,
    rest_mid_in,
    rest_whole,
    own_left,
    own_flip,
    rest_left,
    rest_flip,
    total,
    gate_q,
    up_q,
    low_q,
    pair_out,
    pair_in,
    pair_q_out,
    pair_q_in,
    line_out,
    line_in,
    line_q_out,
    line_q_in,
    last_out,
    last_in,
    last_q_out,
    last_q_in,
    q_all,
    factor_sem,
    wide_sem,
    down_sem,
    square_sem,
    rank_sem,
    far_send,
    far_recv,
    near_send,
    near_recv,
    rank_all_sem,
    own_send,
    own_recv,
    rest_send,
    rest_recv,
    pair_sem,
    line_sem,
    last_sem,
    q_sem,
):
    row, me = lax.axis_index("row"), lax.axis_index("col")
    rows, columns = 4, 8
    z, core = me // 2, lax.rem(me, 2)
    partner = me + 1 - 2 * core
    flip_low = row + 1 - 2 * lax.rem(row, 2)
    flip_high = row + 2 - 4 * (row // 2)
    flip_both = 3 - row
    own, depth = tokens.shape
    chip = 2 * own
    count = 8 * own
    chunks = own_parts.shape[0]
    width = down_buf.shape[1]
    half = width // 2
    rank = gate_in.shape[0]
    slots, sides = wide_buf.shape[0], down_buf.shape[0]
    steps = 2 * chunks
    big = 4 * steps
    f32, bf16 = jnp.float32, jnp.bfloat16

    def remote(src, dst, send, recv, where):
        return pltpu.make_async_remote_copy(
            src_ref=src,
            dst_ref=dst,
            send_sem=send,
            recv_sem=recv,
            device_id=where,
            device_id_type=MESH,
        )

    def slot_rows(slot):
        return pl.ds(pl.multiple_of(slot * own, own), own)

    def lanes(c):
        return pl.ds(pl.multiple_of(c * width, width), width)

    def chunk_at(s):
        return (
            s - lead * ((s + big - lead) // big) - (chunks - lead) * ((s + big - lead - chunks) // big)
        )

    def loads(s):
        c, slot, side = chunk_at(s), lax.rem(s, slots), lax.rem(s, sides)
        return [
            pltpu.make_async_copy(
                gate_hbm.at[:, lanes(c)], wide_buf.at[slot, 0], wide_sem.at[slot, 0]
            ),
            pltpu.make_async_copy(
                up_hbm.at[:, lanes(c)], wide_buf.at[slot, 1], wide_sem.at[slot, 1]
            ),
            pltpu.make_async_copy(down_hbm.at[lanes(c), :], down_buf.at[side], down_sem.at[side]),
        ]

    factor_loads = []
    for index, (src, dst) in enumerate(
        [
            (down_b, in_rows.at[2, 0:rank]),
            (down_b_dir, in_rows.at[2, rank : 2 * rank]),
            (gate_in, in_rows.at[0, 0:rank]),
            (gate_in_dir, in_rows.at[0, rank : 2 * rank]),
            (up_in, in_rows.at[1, 0:rank]),
            (up_in_dir, in_rows.at[1, rank : 2 * rank]),
            (gate_out, out_rows.at[0, 0:rank]),
            (gate_out_dir, out_rows.at[0, rank : 2 * rank]),
            (up_out, out_rows.at[1, 0:rank]),
            (up_out_dir, out_rows.at[1, rank : 2 * rank]),
            (down_in, out_rows.at[2, 0:rank]),
            (down_in_dir, out_rows.at[2, rank : 2 * rank]),
        ]
    ):
        factor_loads.append(pltpu.make_async_copy(src, dst, factor_sem.at[index]))

    for copy in factor_loads[:6]:
        copy.start()
    for s in range(2):
        for copy in loads(s):
            copy.start()
    for copy in factor_loads[6:]:
        copy.start()

    line_in[...] = jnp.zeros_like(line_in)
    line_q_in[...] = jnp.zeros_like(line_q_in)

    barrier = pltpu.get_barrier_semaphore()

    def row_peer(k):
        return {"row": lax.rem(row + k, rows)}

    def col_peer(k):
        return {"col": lax.rem(me + k, columns)}

    @pl.loop(1, rows)
    def _(k):
        pl.semaphore_signal(barrier, inc=1, device_id=row_peer(k), device_id_type=MESH)

    @pl.loop(1, columns)
    def _(k):
        pl.semaphore_signal(barrier, inc=1, device_id=col_peer(k), device_id_type=MESH)

    values = tokens[...].astype(f32)
    squares[0] = jnp.broadcast_to(
        jnp.sum(values * values, axis=1, keepdims=True), squares.shape[1:]
    )
    cot_buf[slot_rows(core), :] = cot[...]
    pl.semaphore_wait(barrier, rows + columns - 2)

    def square(k):
        return remote(
            squares.at[0], squares.at[k], square_sem.at[0, k], square_sem.at[1, k], row_peer(k)
        )

    buffers = (cot_buf, x_buf)
    right, left = {"col": me + 2}, {"col": me - 2}

    def far(which, side, k):
        buffer = buffers[which]
        src = 2 * lax.rem(4 - k, 4) + core if side == 0 else 2 * k + core
        dst = 2 * (3 - k) + core if side == 0 else 2 * (k + 1) + core
        landing = 3 - k if side == 0 else k + 1
        return remote(
            buffer.at[slot_rows(src)],
            buffer.at[slot_rows(dst)],
            far_send.at[which, side, k],
            far_recv.at[which, landing],
            right if side == 0 else left,
        )

    def far_valid(side, k):
        if side == 0:
            return (z < 3) & (z >= k)
        return (z > 0) & (z + k <= 3)

    def far_arrival(which, slot):
        buffer = buffers[which]
        at = buffer.at[slot_rows(2 * slot + core)]
        return remote(at, at, far_send.at[which, 0, 0], far_recv.at[which, slot], {"col": partner})

    def near(which, slot):
        buffer = buffers[which]
        at = buffer.at[slot_rows(2 * slot + core)]
        return remote(
            at, at, near_send.at[which, slot], near_recv.at[which, slot], {"col": partner}
        )

    def near_arrival(which, slot):
        buffer = buffers[which]
        at = buffer.at[slot_rows(2 * slot + 1 - core)]
        return remote(
            at, at, near_send.at[which, slot], near_recv.at[which, slot], {"col": partner}
        )

    def launch(which):
        for side in range(2):

            @pl.when(far_valid(side, 0))
            def _(side=side):
                far(which, side, 0).start()

        near(which, 0).start()

    def pass_on(which, k):
        @pl.when(z >= k)
        def _():
            far_arrival(which, 4 - k).wait_recv()
            if k < 3:

                @pl.when(far_valid(0, k))
                def _():
                    far(which, 0, k).start()

            near(which, 4 - k).start()

        @pl.when(z + k <= 3)
        def _():
            far_arrival(which, k).wait_recv()
            if k < 3:

                @pl.when(far_valid(1, k))
                def _():
                    far(which, 1, k).start()

            near(which, k).start()

    for k in range(1, rows):
        square(k).start()
    launch(0)
    for copy in factor_loads[:6]:
        copy.wait()
    rank_part[:, 4 * rank :] = cross_shard_total(cot[...], in_rows[2]).astype(bf16)
    sum_squares = squares[0]
    for k in range(1, rows):
        square(k).wait_recv()
        sum_squares = sum_squares + squares[k]
    scale = lax.rsqrt(sum_squares[:, :1] / (rows * depth) + epsilon)
    x_buf[slot_rows(core), :] = (tokens[...].astype(f32) * scale * gain[...]).astype(bf16)
    launch(1)
    own_x = x_buf[slot_rows(core), :]
    rank_part[:, : 2 * rank] = cross_shard_total(own_x, in_rows[0]).astype(bf16)
    rank_part[:, 2 * rank : 4 * rank] = cross_shard_total(own_x, in_rows[1]).astype(bf16)

    def rank_row(k):
        return remote(
            rank_part, rank_in.at[k], rank_sem.at[0, k], rank_sem.at[1, k], row_peer(k)
        )

    for k in range(1, rows):
        rank_row(k).start()

    total[...] = jnp.zeros_like(total)
    for ref in (gate_q, up_q, low_q, gate_curve, up_curve, down_curve):
        ref[...] = jnp.zeros_like(ref)

    def slot_there(k):
        there = lax.rem(me + k, columns) // 2
        return 2 * lax.rem(z - there + 4, 4) + core

    def slot_from(k):
        origin = lax.rem(me - k + columns, columns)
        return 2 * lax.rem(origin // 2 - z + 4, 4) + lax.rem(origin, 2)

    def spread(buffer, sem, k):
        return remote(
            buffer.at[slot_rows(core)],
            buffer.at[slot_rows(slot_there(k))],
            sem.at[0, k],
            sem.at[1, k],
            col_peer(k),
        )

    def spread_arrival(buffer, sem, k):
        at = buffer.at[slot_rows(slot_from(k))]
        return remote(at, at, sem.at[0, k], sem.at[1, k], col_peer(k))

    def share_ranks():
        summed = rank_part[...].astype(f32)
        for k in range(1, rows):
            rank_row(k).wait_recv()
            summed = summed + rank_in[k].astype(f32)
        rank_all[slot_rows(core), :] = summed.astype(bf16)

        @pl.loop(1, columns)
        def _(k):
            spread(rank_all, rank_all_sem, k).start()

    partner_step = 7 - 6 * core

    class Group:
        pass

    mine, others = Group(), Group()
    mine.first, mine.size = 0, chip
    mine.parts, mine.inbox, mine.mid_out, mine.mid_in, mine.whole = (
        own_parts,
        own_first,
        own_mid_out,
        own_mid_in,
        own_whole,
    )
    mine.left, mine.flip, mine.send, mine.recv = own_left, own_flip, own_send, own_recv
    others.first, others.size = chip, count - chip
    others.parts, others.inbox, others.mid_out, others.mid_in, others.whole = (
        rest_parts,
        rest_first,
        rest_mid_out,
        rest_mid_in,
        rest_whole,
    )
    others.left, others.flip, others.send, others.recv = (
        rest_left,
        rest_flip,
        rest_send,
        rest_recv,
    )

    def prepare(g):
        low = rank_all[g.first : g.first + g.size, :].astype(f32)
        for index in range(3):
            block = low[:, index * 2 * rank : (index + 1) * 2 * rank] * adapter_scale
            lane = lax.broadcasted_iota(jnp.int32, block.shape, 1)
            turned = pltpu.roll(block, rank, 1)
            g.left[index, 0 : g.size, :] = jnp.where(lane < rank, block, 0.0).astype(bf16)
            g.left[index, g.size :, :] = turned.astype(bf16)
            g.flip[index] = turned.T.astype(bf16)

    def ends(path):
        return (flip_low, flip_high) if path == 0 else (flip_high, flip_low)

    def send(g, src, dst, c, path, k, peer):
        return remote(src, dst, g.send.at[c, path, k], g.recv.at[c, path, k], {"row": peer})

    def sends(g, c, path, ks):
        near_end, far_end = ends(path)
        table = [
            (g.parts.at[c, path, near_end], g.inbox.at[c, path, 0], near_end),
            (g.parts.at[c, path, flip_both], g.inbox.at[c, path, 1], near_end),
            (g.mid_out.at[c, path], g.mid_in.at[c, path], far_end),
            (g.whole.at[c, path, row], g.whole.at[c, path, row], far_end),
            (g.whole.at[c, path, row], g.whole.at[c, path, row], near_end),
            (g.whole.at[c, path, far_end], g.whole.at[c, path, far_end], near_end),
        ]
        return [send(g, table[k][0], table[k][1], c, path, k, table[k][2]) for k in ks]

    def arrivals(g, c, path, ks):
        near_end, far_end = ends(path)
        table = [
            (g.parts.at[c, path, row], g.inbox.at[c, path, 0], near_end),
            (g.parts.at[c, path, far_end], g.inbox.at[c, path, 1], near_end),
            (g.mid_out.at[c, path], g.mid_in.at[c, path], far_end),
            (g.whole.at[c, path, far_end], g.whole.at[c, path, far_end], far_end),
            (g.whole.at[c, path, near_end], g.whole.at[c, path, near_end], near_end),
            (g.whole.at[c, path, flip_both], g.whole.at[c, path, flip_both], near_end),
        ]
        return [send(g, table[k][0], table[k][1], c, path, k, table[k][2]) for k in ks]

    def project(g, c, s):
        for copy in loads(s):
            copy.wait()

        @pl.when(s + 2 < steps)
        def _():
            for copy in loads(s + 2):
                copy.start()

        slot = lax.rem(s, slots)
        span = slice(g.first, g.first + g.size)
        quarter = g.size // 4

        def put(path, at, value):
            g.parts[c, path, :, :, at : at + value.shape[1]] = value.reshape(
                4, quarter, value.shape[1]
            )

        gate = curvature_product(x_buf[span, :], wide_buf[slot, 0]).astype(bf16)
        put(0, 0, gate)
        up = curvature_product(x_buf[span, :], wide_buf[slot, 1]).astype(bf16)
        put(0, width, up[:, :half])
        put(1, 0, up[:, half:])
        for copy in sends(g, c, 0, (0, 1)):
            copy.start()
        down = cross_shard_total(cot_buf[span, :], down_buf[lax.rem(s, sides)]).astype(bf16)
        put(1, half, down)
        for copy in sends(g, c, 1, (0, 1)):
            copy.start()

    def relay(g, c, s):
        for path in range(2):
            near_end, far_end = ends(path)
            for copy in arrivals(g, c, path, (0, 1)):
                copy.wait_recv()
            g.mid_out[c, path] = (
                g.parts[c, path, far_end].astype(f32) + g.inbox[c, path, 1].astype(f32)
            ).astype(bf16)
            sends(g, c, path, (2,))[0].start()

    def settle(g, c, s):
        for path in range(2):
            arrivals(g, c, path, (2,))[0].wait_recv()
            g.whole[c, path, row] = (
                g.parts[c, path, row].astype(f32)
                + g.inbox[c, path, 0].astype(f32)
                + g.mid_in[c, path].astype(f32)
            ).astype(bf16)
            for copy in sends(g, c, path, (3, 4)):
                copy.start()

    def forward(g, c, s):
        for path in range(2):
            arrivals(g, c, path, (3,))[0].wait_recv()
            sends(g, c, path, (5,))[0].start()

    def differentiate(g, c, s):
        for path in range(2):
            for copy in arrivals(g, c, path, (4, 5)):
                copy.wait_recv()
        size = g.size

        def got(path, at, wide):
            return g.whole[c, path, :, :, at : at + wide].reshape(size, wide).astype(f32)

        gate_w, up_w, down_w = out_rows[0, :, lanes(c)], out_rows[1, :, lanes(c)], out_rows[2, :, lanes(c)]
        gate_low = curvature_product(g.left[0], gate_w)
        up_low = curvature_product(g.left[1], up_w)
        adj_low = curvature_product(g.left[2], down_w)
        hidden, hidden_dir, d_gate, d_up, d_gate_dir, d_up_dir = second_order(
            got(0, 0, width) + gate_low[:size],
            jnp.concatenate([got(0, width, half), got(1, 0, half)], axis=1) + up_low[:size],
            got(1, half, width) + adj_low[:size],
            gate_low[size:],
            up_low[size:],
            adj_low[size:],
        )
        gate_d = jnp.concatenate([d_gate, d_gate_dir], axis=0)
        up_d = jnp.concatenate([d_up, d_up_dir], axis=0)
        hidden_d = jnp.concatenate([hidden_dir, hidden], axis=0)
        span = slice(g.first, g.first + size)
        gate_curve[:, lanes(c)] += curvature_product(
            g.flip[0, :rank], d_gate
        ) + curvature_product(g.flip[0, rank:], d_gate_dir)
        up_curve[:, lanes(c)] += curvature_product(g.flip[1, :rank], d_up) + curvature_product(
            g.flip[1, rank:], d_up_dir
        )
        down_curve[:, lanes(c)] += curvature_product(
            g.flip[2, rank:], hidden_dir
        ) + curvature_product(g.flip[2, :rank], hidden)
        for ref, value, weight in (
            (gate_q, gate_d, gate_w),
            (up_q, up_d, up_w),
            (low_q, hidden_d, down_w),
        ):
            product = cross_shard_total(value, weight)
            ref[0, span, :] += product[:size]
            ref[1, span, :] += product[size:]
        slot = lax.rem(s, slots)
        piece = 512 if depth % 512 == 0 else depth
        for start in range(0, depth, piece):
            at = slice(start, start + piece)
            product = cross_shard_total(gate_d, wide_buf[slot, 0, at, :]) + cross_shard_total(
                up_d, wide_buf[slot, 1, at, :]
            )
            total[0, span, at] += product[:size]
            total[1, span, at] += product[size:]

    def q_rows(slot):
        at = slot_rows(slot)
        lane = lax.broadcasted_iota(jnp.int32, (own, 2 * rank), 1)
        low_half = lane < rank
        gate = gate_q[0, at, :] + jnp.where(low_half, 0.0, pltpu.roll(gate_q[1, at, :], rank, 1))
        up = up_q[0, at, :] + jnp.where(low_half, 0.0, pltpu.roll(up_q[1, at, :], rank, 1))
        low = jnp.where(low_half, low_q[0, at, :] + pltpu.roll(low_q[1, at, :], rank, 1), 0.0)
        return jnp.concatenate([gate, up, low], axis=1)

    def pair(src, dst, at):
        return remote(src, dst, pair_sem.at[0, at], pair_sem.at[1, at], {"col": partner})

    def pairs():
        return [pair(pair_out, pair_in, 0), pair(pair_q_out, pair_q_in, 1)]

    def exchange():
        for k in range(1, 4):
            slot = 2 * k + 1 - core
            for kind in range(2):
                pair_out[k - 1, kind] = total[kind, slot_rows(slot), :].astype(bf16)
            pair_q_out[k - 1] = q_rows(slot).astype(bf16)
        for copy in pairs():
            copy.start()

    def line(side, k, kind):
        out = k - 1 if side == 0 else 3 - k
        src, dst = (line_out, line_in) if kind == 0 else (line_q_out, line_q_in)
        return remote(
            src.at[out],
            dst.at[side, k - 1],
            line_sem.at[0, side, k - 1, kind],
            line_sem.at[1, side, k - 1, kind],
            right if side == 0 else left,
        )

    def line_arrival(side, k, kind):
        src, dst = (line_out, line_in) if kind == 0 else (line_q_out, line_q_in)
        return remote(
            src.at[0],
            dst.at[side, k],
            line_sem.at[0, side, k, kind],
            line_sem.at[1, side, k, kind],
            {"col": partner},
        )

    def line_valid(side, k):
        return z + k <= 3 if side == 0 else z - k >= 0

    def line_fed(side):
        return z >= 1 if side == 0 else z <= 2

    def line_stage(i):
        if i == 1:
            for copy in pairs():
                copy.wait_recv()
        k = 4 - i
        for side in range(2):

            @pl.when(line_valid(side, k))
            def _(side=side):
                if k < 3:

                    @pl.when(line_fed(side))
                    def _():
                        for kind in range(2):
                            line_arrival(side, k, kind).wait_recv()

                at = k if side == 0 else 4 - k
                slot = 2 * at + core
                for kind in range(2):
                    value = total[kind, slot_rows(slot), :] + pair_in[at - 1, kind].astype(f32)
                    if k < 3:
                        value = value + line_in[side, k, kind].astype(f32)
                    line_out[at - 1, kind] = value.astype(bf16)
                value = q_rows(slot) + pair_q_in[at - 1].astype(f32)
                if k < 3:
                    value = value + line_q_in[side, k].astype(f32)
                line_q_out[at - 1] = value.astype(bf16)
                for kind in range(2):
                    line(side, k, kind).start()

    def line_end():
        for side in range(2):

            @pl.when(line_fed(side))
            def _(side=side):
                for kind in range(2):
                    line_arrival(side, 0, kind).wait_recv()

    rest_end = lead + chunks + 3
    late = [exchange] + [functools.partial(line_stage, i) for i in (1, 2, 3)]
    stride = 2
    late_at = [rest_end] + [rest_end + 1 + stride * i for i in range(3)]
    relays = [(which, k) for k in (1, 2, 3) for which in (0, 1)]
    early = max(lead - 1, 0)

    for which in range(2):
        near_arrival(which, 0).wait_recv()

    def arrive():
        for which, k in relays[early:]:
            pass_on(which, k)
        for which in range(2):
            for k in range(1, 4):
                near_arrival(which, k).wait_recv()

    last_step = steps + 4

    @pl.loop(0, last_step)
    def _(t):
        @pl.when(t == lead)
        def _():
            arrive()

        for lag, stage in enumerate((project, relay, settle, forward, differentiate)):
            s = t - lag
            turn = lead + chunks
            if lag == 4:

                @pl.when(t == 4)
                def _():
                    for copy in factor_loads[6:]:
                        copy.wait()
                    spread_arrival(rank_all, rank_all_sem, partner_step).wait_recv()
                    prepare(mine)

                @pl.when(t == lead + 4)
                def _():
                    @pl.loop(1, columns)
                    def _(k):
                        @pl.when(k != partner_step)
                        def _():
                            spread_arrival(rank_all, rank_all_sem, k).wait_recv()

                    prepare(others)

            @pl.when(((s >= 0) & (s < lead)) | ((s >= turn) & (s < steps)))
            def _(s=s, stage=stage):
                stage(mine, chunk_at(s), s)

            @pl.when((s >= lead) & (s < turn))
            def _(s=s, stage=stage):
                stage(others, s - lead, s)

        @pl.when(t == 0)
        def _():
            share_ranks()

        for index, (which, k) in enumerate(relays[:early]):

            @pl.when(t == index)
            def _(which=which, k=k):
                pass_on(which, k)

        for at, action in zip(late_at, late):
            if at < last_step:

                @pl.when(t == at)
                def _(action=action):
                    action()

    for at, action in zip(late_at, late):
        if at >= last_step:
            action()

    def lasts():
        return [
            remote(last_out, last_in, last_sem.at[0, 0], last_sem.at[1, 0], {"col": partner}),
            remote(last_q_out, last_q_in, last_sem.at[0, 1], last_sem.at[1, 1], {"col": partner}),
        ]

    last_q_out[...] = q_rows(1 - core).astype(bf16)
    lasts()[1].start()
    for kind in range(2):
        last_out[kind] = total[kind, slot_rows(1 - core), :].astype(bf16)
    lasts()[0].start()
    line_end()
    lasts()[1].wait_recv()
    q_own = (
        q_rows(core)
        + last_q_in[...].astype(f32)
        + line_q_in[0, 0].astype(f32)
        + line_q_in[1, 0].astype(f32)
    )
    q_all[slot_rows(core), :] = q_own.astype(bf16)

    @pl.loop(1, columns)
    def _(k):
        spread(q_all, q_sem, k).start()

    lasts()[0].wait_recv()
    lane = lax.broadcasted_iota(jnp.int32, (own, 2 * rank), 1)
    feature = [
        total[kind, slot_rows(core), :]
        + last_in[kind].astype(f32)
        + line_in[0, 0, kind].astype(f32)
        + line_in[1, 0, kind].astype(f32)
        for kind in range(2)
    ]
    for index in range(2):
        block = q_own[:, index * 2 * rank : (index + 1) * 2 * rank] * adapter_scale
        straight = jnp.where(lane < rank, block, 0.0).astype(bf16)
        turned = pltpu.roll(block, rank, 1).astype(bf16)
        feature[0] = feature[0] + curvature_product(straight, in_rows[index])
        feature[1] = feature[1] + curvature_product(turned, in_rows[index])
    primal_ref[...] = feature[0]
    dir_ref[...] = feature[1]

    @pl.loop(1, columns)
    def _(k):
        spread_arrival(q_all, q_sem, k).wait_recv()

    every = q_all[...].astype(f32) * adapter_scale
    lane = lax.broadcasted_iota(jnp.int32, (count, 2 * rank), 1)
    both = jnp.where(
        lane < rank, pltpu.roll(every[:, : 2 * rank], rank, 1), every[:, 2 * rank : 4 * rank]
    )
    both_t = both.T.astype(bf16)
    low_t = every[:, 4 * rank :].T.astype(bf16)
    gate_curve_in[...] = curvature_product(both_t[:rank], x_buf[...])
    up_curve_in[...] = curvature_product(both_t[rank:], x_buf[...])
    down_curve_out[...] = curvature_product(low_t[:rank], cot_buf[...])

    for k in range(1, rows):
        square(k).wait_send()
        rank_row(k).wait_send()
    for which in range(2):
        for side in range(2):
            for k in range(3):

                @pl.when(far_valid(side, k))
                def _(which=which, side=side, k=k):
                    far(which, side, k).wait_send()

        for k in range(4):
            near(which, k).wait_send()

    @pl.loop(1, columns)
    def _(k):
        spread(rank_all, rank_all_sem, k).wait_send()
        spread(q_all, q_sem, k).wait_send()

    @pl.loop(0, chunks)
    def _(c):
        for g in (mine, others):
            for path in range(2):
                for copy in sends(g, c, path, range(6)):
                    copy.wait_send()

    for copy in pairs() + lasts():
        copy.wait_send()
    for side in range(2):
        for k in range(1, 4):

            @pl.when(line_valid(side, k))
            def _(side=side, k=k):
                for kind in range(2):
                    line(side, k, kind).wait_send()


def fused(
    tokens,
    norm_gain,
    cotangent,
    gate_frozen_weight,
    up_frozen_weight,
    down_frozen_weight,
    gate_input_factor,
    gate_output_factor,
    up_input_factor,
    up_output_factor,
    down_input_factor,
    down_b,
    gate_input_factor_direction,
    gate_output_factor_direction,
    up_input_factor_direction,
    up_output_factor_direction,
    down_input_factor_direction,
    down_b_dir,
    width,
):
    own, depth = tokens.shape
    hidden = gate_frozen_weight.shape[1]
    rank = gate_output_factor.shape[0]
    chunks = hidden // width
    chip, rest, count = 2 * own, 6 * own, 8 * own
    lead = (3 * chunks) // 7
    half_panel = 3 * width // 2
    f32, bf16 = jnp.float32, jnp.bfloat16
    vmem = pl.BlockSpec(memory_space=pltpu.VMEM)
    anywhere = pl.BlockSpec(memory_space=pl.ANY)

    def reduce_buffers(size):
        quarter = size // 4
        return [
            pltpu.VMEM((chunks, 2, 4, quarter, half_panel), bf16),
            pltpu.VMEM((chunks, 2, 2, quarter, half_panel), bf16),
            pltpu.VMEM((chunks, 2, quarter, half_panel), bf16),
            pltpu.VMEM((chunks, 2, quarter, half_panel), bf16),
            pltpu.VMEM((chunks, 2, 4, quarter, half_panel), bf16),
        ]

    dma = pltpu.SemaphoreType.DMA
    slots, sides = 7, 3
    results = pl.pallas_call(
        functools.partial(lora_kernel, lead),
        out_shape=[
            jax.ShapeDtypeStruct((own, depth), f32),
            jax.ShapeDtypeStruct((own, depth), f32),
            jax.ShapeDtypeStruct((rank, depth), f32),
            jax.ShapeDtypeStruct((rank, hidden), f32),
            jax.ShapeDtypeStruct((rank, depth), f32),
            jax.ShapeDtypeStruct((rank, hidden), f32),
            jax.ShapeDtypeStruct((rank, hidden), f32),
            jax.ShapeDtypeStruct((rank, depth), f32),
        ],
        in_specs=[vmem] * 3 + [anywhere] * 15,
        out_specs=[vmem] * 8,
        scratch_shapes=[
            pltpu.VMEM((count, depth), bf16),
            pltpu.VMEM((count, depth), bf16),
            pltpu.VMEM((4, own, 128), f32),
            pltpu.VMEM((own, 6 * rank), bf16),
            pltpu.VMEM((4, own, 6 * rank), bf16),
            pltpu.VMEM((count, 6 * rank), bf16),
            pltpu.VMEM((3, 2 * rank, depth), bf16),
            pltpu.VMEM((3, 2 * rank, hidden), bf16),
            pltpu.VMEM((slots, 2, depth, width), bf16),
            pltpu.VMEM((sides, width, depth), bf16),
        ]
        + reduce_buffers(chip)
        + reduce_buffers(rest)
        + [
            pltpu.VMEM((3, 2 * chip, 2 * rank), bf16),
            pltpu.VMEM((3, 2 * rank, chip), bf16),
            pltpu.VMEM((3, 2 * rest, 2 * rank), bf16),
            pltpu.VMEM((3, 2 * rank, rest), bf16),
            pltpu.VMEM((2, count, depth), f32),
            pltpu.VMEM((2, count, 2 * rank), f32),
            pltpu.VMEM((2, count, 2 * rank), f32),
            pltpu.VMEM((2, count, 2 * rank), f32),
            pltpu.VMEM((3, 2, own, depth), bf16),
            pltpu.VMEM((3, 2, own, depth), bf16),
            pltpu.VMEM((3, own, 6 * rank), bf16),
            pltpu.VMEM((3, own, 6 * rank), bf16),
            pltpu.VMEM((3, 2, own, depth), bf16),
            pltpu.VMEM((2, 3, 2, own, depth), bf16),
            pltpu.VMEM((3, own, 6 * rank), bf16),
            pltpu.VMEM((2, 3, own, 6 * rank), bf16),
            pltpu.VMEM((2, own, depth), bf16),
            pltpu.VMEM((2, own, depth), bf16),
            pltpu.VMEM((own, 6 * rank), bf16),
            pltpu.VMEM((own, 6 * rank), bf16),
            pltpu.VMEM((count, 6 * rank), bf16),
            dma((12,)),
            dma((slots, 2)),
            dma((sides,)),
            dma((2, 4)),
            dma((2, 4)),
            dma((2, 2, 3)),
            dma((2, 4)),
            dma((2, 4)),
            dma((2, 4)),
            dma((2, 8)),
            dma((chunks, 2, 6)),
            dma((chunks, 2, 6)),
            dma((chunks, 2, 6)),
            dma((chunks, 2, 6)),
            dma((2, 2)),
            dma((2, 2, 3, 2)),
            dma((2, 2)),
            dma((2, 8)),
        ],
        compiler_params=pltpu.CompilerParams(
            collective_id=2, has_side_effects=True, vmem_limit_bytes=63 * 1024 * 1024
        ),
        name="lora",
    )(
        tokens,
        norm_gain.reshape(1, depth),
        cotangent,
        gate_frozen_weight,
        up_frozen_weight,
        down_frozen_weight,
        gate_input_factor.T,
        gate_input_factor_direction.T,
        up_input_factor.T,
        up_input_factor_direction.T,
        down_b,
        down_b_dir,
        gate_output_factor,
        gate_output_factor_direction,
        up_output_factor,
        up_output_factor_direction,
        down_input_factor.T,
        down_input_factor_direction.T,
    )
    primal, direction, gate_input, gate_output, up_input, up_output, down_input, down_output = (
        results
    )
    return (
        primal,
        direction,
        gate_input.T,
        gate_output,
        up_input.T,
        up_output,
        down_input.T,
        down_output,
    )


def gather_kernel(
    tokens,
    gain,
    cot,
    x_all,
    cot_all,
    x_buf,
    cot_buf,
    squares,
    square_send,
    square_recv,
    far_send,
    far_recv,
    near_send,
    near_recv,
):
    rows, columns = lax.axis_size("row"), lax.axis_size("col")
    chips = columns // 2
    my_row, me = lax.axis_index("row"), lax.axis_index("col")
    partner = me + 1 - 2 * lax.rem(me, 2)
    features = rows * tokens.shape[1]
    barrier = pltpu.get_barrier_semaphore()

    def row_peer(k):
        return {"row": lax.rem(my_row + k, rows)}

    def far_peer(k):
        return {"col": lax.rem(me + 2 * k, columns)}

    @pl.loop(1, rows)
    def _(k):
        pl.semaphore_signal(barrier, inc=1, device_id=row_peer(k), device_id_type=MESH)

    @pl.loop(1, chips)
    def _(k):
        pl.semaphore_signal(barrier, inc=1, device_id=far_peer(k), device_id_type=MESH)

    pl.semaphore_signal(barrier, inc=1, device_id={"col": partner}, device_id_type=MESH)

    buffers = (cot_buf, x_buf)

    def origin(k):
        return lax.rem(me - 2 * k + columns, columns)

    def square(k):
        return pltpu.make_async_remote_copy(
            src_ref=squares.at[0],
            dst_ref=squares.at[k],
            send_sem=square_send.at[k],
            recv_sem=square_recv.at[k],
            device_id=row_peer(k),
            device_id_type=MESH,
        )

    def far(which, k, slot):
        return pltpu.make_async_remote_copy(
            src_ref=buffers[which].at[slot],
            dst_ref=buffers[which].at[slot],
            send_sem=far_send.at[which, k],
            recv_sem=far_recv.at[which, k],
            device_id=far_peer(k),
            device_id_type=MESH,
        )

    def near(which, k, slot):
        return pltpu.make_async_remote_copy(
            src_ref=buffers[which].at[slot],
            dst_ref=buffers[which].at[slot],
            send_sem=near_send.at[which, k],
            recv_sem=near_recv.at[which, k],
            device_id={"col": partner},
            device_id_type=MESH,
        )

    def launch(which):
        @pl.loop(1, chips)
        def _(k):
            far(which, k, me).start()

        near(which, 0, me).start()

    values = tokens[...].astype(jnp.float32)
    squares[0] = jnp.broadcast_to(
        jnp.sum(values * values, axis=1, keepdims=True), squares.shape[1:]
    )
    cot_buf[me] = cot[...]
    pl.semaphore_wait(barrier, rows + chips - 1)

    @pl.loop(1, rows)
    def _(k):
        square(k).start()

    launch(0)

    def add(k, total):
        square(k).wait_recv()
        return total + squares[k]

    total = lax.fori_loop(1, rows, add, squares[0])
    scale = lax.rsqrt(total[:, :1] / features + epsilon)
    x_buf[me] = (tokens[...].astype(jnp.float32) * scale * gain[...]).astype(jnp.bfloat16)
    launch(1)
    for which in range(2):

        @pl.loop(1, chips)
        def _(k, which=which):
            far(which, k, origin(k)).wait_recv()
            near(which, k, origin(k)).start()

    for which in range(2):

        @pl.loop(0, chips)
        def _(k, which=which):
            near(which, k, lax.rem(partner - 2 * k + columns, columns)).wait_recv()

    @pl.loop(1, rows)
    def _(k):
        square(k).wait_send()

    for which in range(2):

        @pl.loop(1, chips)
        def _(k, which=which):
            far(which, k, me).wait_send()

        @pl.loop(0, chips)
        def _(k, which=which):
            near(which, k, origin(k)).wait_send()

    cot_all[...] = cot_buf[...]
    x_all[...] = x_buf[...]


def gathered(tokens, gain, cot):
    rows, columns = lax.axis_size("row"), lax.axis_size("col")
    own, depth = tokens.shape
    whole = (columns, own, depth)
    vmem = pl.BlockSpec(memory_space=pltpu.VMEM)
    x, panel = pl.pallas_call(
        gather_kernel,
        out_shape=[jax.ShapeDtypeStruct(whole, jnp.bfloat16)] * 2,
        in_specs=[vmem] * 3,
        out_specs=[vmem] * 2,
        scratch_shapes=[
            pltpu.VMEM(whole, jnp.bfloat16),
            pltpu.VMEM(whole, jnp.bfloat16),
            pltpu.VMEM((rows, own, 128), jnp.float32),
            pltpu.SemaphoreType.DMA((rows,)),
            pltpu.SemaphoreType.DMA((rows,)),
            pltpu.SemaphoreType.DMA((2, columns // 2)),
            pltpu.SemaphoreType.DMA((2, columns // 2)),
            pltpu.SemaphoreType.DMA((2, columns // 2)),
            pltpu.SemaphoreType.DMA((2, columns // 2)),
        ],
        compiler_params=pltpu.CompilerParams(collective_id=3, has_side_effects=True),
        name="gather",
    )(tokens, gain.reshape(1, depth), cot)
    return x.reshape(columns * own, depth), panel.reshape(columns * own, depth)


def chunk_count(width):
    for count in (4, 2):
        if width % (128 * count) == 0:
            return count
    return 1


def on_device(
    tokens,
    norm_gain,
    cotangent,
    gate_frozen_weight,
    up_frozen_weight,
    down_frozen_weight,
    gate_input_factor,
    gate_output_factor,
    up_input_factor,
    up_output_factor,
    down_input_factor,
    down_b,
    gate_input_factor_direction,
    gate_output_factor_direction,
    up_input_factor_direction,
    up_output_factor_direction,
    down_input_factor_direction,
    down_b_dir,
):
    width = 256
    if (
        lax.axis_size("row") == 4
        and lax.axis_size("col") == 8
        and gate_frozen_weight.shape[1] % (7 * width) == 0
        and gate_frozen_weight.shape[0] % 128 == 0
        and gate_input_factor.shape[1] == 64
        and tokens.shape[0] % 32 == 0
    ):
        return fused(
            tokens,
            norm_gain,
            cotangent,
            gate_frozen_weight,
            up_frozen_weight,
            down_frozen_weight,
            gate_input_factor,
            gate_output_factor,
            up_input_factor,
            up_output_factor,
            down_input_factor,
            down_b,
            gate_input_factor_direction,
            gate_output_factor_direction,
            up_input_factor_direction,
            up_output_factor_direction,
            down_input_factor_direction,
            down_b_dir,
            width,
        )
    rank = gate_input_factor.shape[1]
    width_rows, width_columns = gate_frozen_weight.shape
    own_count = tokens.shape[0]
    normed_tokens, cot_panel = gathered(tokens, norm_gain, cotangent)
    count = normed_tokens.shape[0]
    in_factors = jnp.concatenate(
        [
            gate_input_factor,
            up_input_factor,
            gate_input_factor_direction,
            up_input_factor_direction,
        ],
        axis=1,
    )
    out_factors = jnp.concatenate([down_b, down_b_dir], axis=0)

    projected = jnp.concatenate(
        [curvature_product(normed_tokens, in_factors), cross_shard_total(cot_panel, out_factors)],
        axis=1,
    )
    ranks = shard_total(projected, "row", 0)
    gate_out = jnp.concatenate([gate_output_factor, gate_output_factor_direction], axis=0)
    up_out = jnp.concatenate([up_output_factor, up_output_factor_direction], axis=0)
    down_in = jnp.concatenate([down_input_factor, down_input_factor_direction], axis=1)

    chunks = chunk_count(width_columns)
    wide = width_columns // chunks
    spans = [slice(index * wide, (index + 1) * wide) for index in range(chunks)]

    summed_chunks = []
    for span in spans:
        partial = (
            curvature_product(normed_tokens, gate_frozen_weight[:, span]).astype(jnp.bfloat16),
            curvature_product(normed_tokens, up_frozen_weight[:, span]).astype(jnp.bfloat16),
            cross_shard_total(cot_panel, down_frozen_weight[span]).astype(jnp.bfloat16),
        )
        if summed_chunks:
            partial, summed_chunks[-1] = lax.optimization_barrier((partial, summed_chunks[-1]))
        summed_chunks.append(lax.psum(partial, "row"))

    gate_low, up_low, gate_low_dir, up_low_dir, adj_low, adj_low_dir = [
        ranks[:, index * rank : (index + 1) * rank] for index in range(6)
    ]
    gate_pair = jnp.concatenate([gate_low_dir, gate_low], axis=1)
    up_pair = jnp.concatenate([up_low_dir, up_low], axis=1)
    adj_pair = jnp.concatenate([adj_low_dir, adj_low], axis=1)
    gate_stack = jnp.concatenate([gate_low_dir, gate_low], axis=0)
    up_stack = jnp.concatenate([up_low_dir, up_low], axis=0)
    adj_stack = jnp.concatenate([adj_low, adj_low_dir], axis=0)
    feature = 0.0
    gate_q = 0.0
    up_q = 0.0
    low_dir = 0.0
    gate_output, up_output, down_input = [], [], []
    for span, total in zip(spans, summed_chunks):
        gate_sum, up_sum, adj_sum = [value.astype(jnp.float32) for value in total]
        gate_pre = gate_sum + adapter_scale * curvature_product(
            gate_low, gate_output_factor[:, span]
        )
        up_pre = up_sum + adapter_scale * curvature_product(
            up_low, up_output_factor[:, span]
        )
        hidden_adj = adj_sum + adapter_scale * cross_shard_total(
            adj_low, down_input_factor[span]
        )
        gate_tan = adapter_scale * curvature_product(gate_pair, gate_out[:, span])
        up_tan = adapter_scale * curvature_product(up_pair, up_out[:, span])
        adj_tan = adapter_scale * cross_shard_total(adj_pair, down_in[span])
        hidden, hidden_dir, d_gate, d_up, d_gate_dir, d_up_dir = second_order(
            gate_pre, up_pre, hidden_adj, gate_tan, up_tan, adj_tan
        )
        gate_d = jnp.concatenate([d_gate, d_gate_dir], axis=0)
        up_d = jnp.concatenate([d_up, d_up_dir], axis=0)
        hidden_d = jnp.concatenate([hidden_dir, hidden], axis=0)
        gate_output.append(adapter_scale * summed_over_rows(gate_stack, gate_d))
        up_output.append(adapter_scale * summed_over_rows(up_stack, up_d))
        down_input.append(adapter_scale * summed_over_rows(hidden_d, adj_stack))
        gate_q = gate_q + cross_shard_total(gate_d, gate_out[:, span])
        up_q = up_q + cross_shard_total(up_d, up_out[:, span])
        low_dir = (
            low_dir
            + curvature_product(hidden_dir, down_input_factor[span])
            + curvature_product(hidden, down_input_factor_direction[span])
        )
        feature = (
            feature
            + cross_shard_total(gate_d, gate_frozen_weight[:, span])
            + cross_shard_total(up_d, up_frozen_weight[:, span])
        )
    gate_output = jnp.concatenate(gate_output, axis=1)
    up_output = jnp.concatenate(up_output, axis=1)
    down_input = jnp.concatenate(down_input, axis=0)

    summed = lax.psum_scatter(
        feature.astype(jnp.bfloat16).reshape(2, count, width_rows),
        "col",
        scatter_dimension=1,
        tiled=True,
    ).astype(jnp.float32)
    adjoints = shard_total(
        jnp.concatenate(
            [
                gate_q[:count, :rank],
                up_q[:count, :rank],
                gate_q[count:, :rank] + gate_q[:count, rank:],
                up_q[count:, :rank] + up_q[:count, rank:],
                low_dir,
            ],
            axis=1,
        ).astype(jnp.bfloat16),
        "col",
        1,
    )
    piece = lax.dynamic_slice_in_dim(adjoints, lax.axis_index("col") * own_count, own_count, 0)
    normed_feature_adjoint = summed[0] + adapter_scale * cross_shard_total(
        piece[:, : 2 * rank], in_factors[:, : 2 * rank]
    )
    normed_feature_adjoint_direction = summed[1] + adapter_scale * cross_shard_total(
        jnp.concatenate([piece[:, 2 * rank : 4 * rank], piece[:, : 2 * rank]], axis=1), in_factors
    )
    gate_input = adapter_scale * summed_over_rows(
        normed_tokens, adjoints[:, 2 * rank : 3 * rank]
    )
    up_input = adapter_scale * summed_over_rows(normed_tokens, adjoints[:, 3 * rank : 4 * rank])
    down_output = adapter_scale * summed_over_rows(adjoints[:, 4 * rank :], cot_panel)
    return (
        normed_feature_adjoint,
        normed_feature_adjoint_direction,
        gate_input,
        gate_output,
        up_input,
        up_output,
        down_input,
        down_output,
    )


def solution(mesh):
    in_specs = (
        P("col", "row"),
        P("row"),
        P("col", "row"),
        P("row", "col"),
        P("row", "col"),
        P("col", "row"),
        P("row", None),
        P(None, "col"),
        P("row", None),
        P(None, "col"),
        P("col", None),
        P(None, "row"),
        P("row", None),
        P(None, "col"),
        P("row", None),
        P(None, "col"),
        P("col", None),
        P(None, "row"),
    )
    out_specs = (
        P("col", "row"),
        P("col", "row"),
        P("row", None),
        P(None, "col"),
        P("row", None),
        P(None, "col"),
        P("col", None),
        P(None, "row"),
    )
    return jax.shard_map(
        on_device, mesh=mesh, in_specs=in_specs, out_specs=out_specs, check_vma=False
    )
```

```python
import functools

import jax
import jax.numpy as jnp
from jax import lax
from jax.experimental import pallas as pl
from jax.experimental.pallas import tpu as pltpu
from jax.sharding import PartitionSpec as P

adapter_scale = 0.5
epsilon = 1e-05
MESH = pl.DeviceIdType.MESH


def total_kernel(axis, n, x_ref, o_ref, inbox, whole, send1, recv1, send2, recv2):
    me = lax.axis_index(axis)
    barrier = pltpu.get_barrier_semaphore()

    @pl.loop(1, n)
    def _(k):
        pl.semaphore_signal(
            barrier, inc=1, device_id={axis: lax.rem(me + k, n)}, device_id_type=MESH
        )

    pl.semaphore_wait(barrier, n - 1)

    def scatter(k):
        peer = lax.rem(me + k, n)
        return pltpu.make_async_remote_copy(
            src_ref=x_ref.at[peer],
            dst_ref=inbox.at[k],
            send_sem=send1.at[k],
            recv_sem=recv1.at[k],
            device_id={axis: peer},
            device_id_type=MESH,
        )

    def spread(k):
        peer = lax.rem(me + k, n)
        return pltpu.make_async_remote_copy(
            src_ref=whole.at[me],
            dst_ref=whole.at[me],
            send_sem=send2.at[k],
            recv_sem=recv2.at[k],
            device_id={axis: peer},
            device_id_type=MESH,
        )

    def arrival(k):
        origin = lax.rem(me - k + n, n)
        return pltpu.make_async_remote_copy(
            src_ref=whole.at[origin],
            dst_ref=whole.at[origin],
            send_sem=send2.at[k],
            recv_sem=recv2.at[k],
            device_id={axis: origin},
            device_id_type=MESH,
        )

    @pl.loop(1, n)
    def _(k):
        scatter(k).start()

    def add(k, total):
        scatter(k).wait_recv()
        return total + inbox[k].astype(jnp.float32)

    total = lax.fori_loop(1, n, add, x_ref[me].astype(jnp.float32))
    whole[me] = total.astype(whole.dtype)

    @pl.loop(1, n)
    def _(k):
        spread(k).start()

    @pl.loop(1, n)
    def _(k):
        arrival(k).wait_recv()

    @pl.loop(1, n)
    def _(k):
        scatter(k).wait_send()
        spread(k).wait_send()

    o_ref[...] = whole[...]


def shard_total(x, axis, collective_id):
    n = lax.axis_size(axis)
    rows, columns = x.shape
    block = (n, rows // n, columns)
    total = pl.pallas_call(
        functools.partial(total_kernel, axis, n),
        out_shape=jax.ShapeDtypeStruct(block, jnp.bfloat16),
        in_specs=[pl.BlockSpec(memory_space=pltpu.VMEM)],
        out_specs=pl.BlockSpec(memory_space=pltpu.VMEM),
        scratch_shapes=[
            pltpu.VMEM(block, x.dtype),
            pltpu.VMEM(block, jnp.bfloat16),
            pltpu.SemaphoreType.DMA((n,)),
            pltpu.SemaphoreType.DMA((n,)),
            pltpu.SemaphoreType.DMA((n,)),
            pltpu.SemaphoreType.DMA((n,)),
        ],
        compiler_params=pltpu.CompilerParams(collective_id=collective_id, has_side_effects=True),
        name=f"total_{axis}",
    )(x.reshape(block))
    return total.reshape(rows, columns)


def curvature_product(left, right):
    return jnp.dot(left, right, preferred_element_type=jnp.float32)


def cross_shard_total(left, right):
    return lax.dot_general(
        left, right, (((1,), (1,)), ((), ())), preferred_element_type=jnp.float32
    )


def summed_over_rows(left, right):
    return lax.dot_general(
        left, right, (((0,), (0,)), ((), ())), preferred_element_type=jnp.float32
    )


def second_order(
    gate_preactivation,
    up_preactivation,
    hidden_adjoint,
    gate_tangent_rows,
    up_tangent_rows,
    adjoint_tangent_rows,
):
    sigma = jax.nn.sigmoid(gate_preactivation)
    silu_value = gate_preactivation * sigma
    slope = sigma * (1.0 + gate_preactivation * (1.0 - sigma))
    bend = sigma * (1.0 - sigma) * (2.0 + gate_preactivation * (1.0 - 2.0 * sigma))
    hidden_activation = (silu_value * up_preactivation).astype(jnp.bfloat16)
    hidden_direction = (
        slope * gate_tangent_rows * up_preactivation + silu_value * up_tangent_rows
    ).astype(jnp.bfloat16)
    gate_derivative = (hidden_adjoint * up_preactivation * slope).astype(jnp.bfloat16)
    up_derivative = (hidden_adjoint * silu_value).astype(jnp.bfloat16)
    gate_derivative_direction = (
        adjoint_tangent_rows * up_preactivation * slope
        + hidden_adjoint * (up_tangent_rows * slope + up_preactivation * bend * gate_tangent_rows)
    ).astype(jnp.bfloat16)
    up_derivative_direction = (
        adjoint_tangent_rows * silu_value + hidden_adjoint * slope * gate_tangent_rows
    ).astype(jnp.bfloat16)
    return (
        hidden_activation,
        hidden_direction,
        gate_derivative,
        up_derivative,
        gate_derivative_direction,
        up_derivative_direction,
    )


def lora_kernel(
    lead,
    gap,
    tokens,
    gain,
    cot,
    gate_hbm,
    up_hbm,
    down_hbm,
    gate_in,
    gate_in_dir,
    up_in,
    up_in_dir,
    down_b,
    down_b_dir,
    gate_out,
    gate_out_dir,
    up_out,
    up_out_dir,
    down_in,
    down_in_dir,
    primal_out,
    dir_out,
    gate_curve_in_out,
    gate_curve_hbm,
    up_curve_in_out,
    up_curve_hbm,
    down_curve_hbm,
    down_curve_out_out,
    primal_ref,
    dir_ref,
    gate_curve_in,
    gate_curve,
    up_curve_in,
    up_curve,
    down_curve,
    down_curve_out,
    x_buf,
    cot_buf,
    squares,
    rank_part,
    rank_in,
    rank_all,
    inv_all,
    in_rows,
    out_rows,
    wide_buf,
    down_buf,
    own_parts,
    own_first,
    own_whole,
    rest_parts,
    rest_first,
    rest_mid_out,
    rest_mid_in,
    rest_whole,
    own_left,
    own_flip,
    rest_left,
    rest_flip,
    total,
    gate_q,
    up_q,
    low_q,
    pair_out,
    pair_in,
    pair_q_out,
    pair_q_in,
    line_out,
    line_in,
    line_q_out,
    line_q_in,
    last_out,
    last_in,
    last_q_out,
    last_q_in,
    q_all,
    factor_sem,
    wide_sem,
    down_sem,
    square_sem,
    rank_sem,
    far_send,
    far_recv,
    near_send,
    near_recv,
    rank_all_sem,
    inv_sem,
    own_send,
    own_recv,
    rest_send,
    rest_recv,
    pair_sem,
    line_sem,
    last_sem,
    q_sem,
    out_sem,
):
    row, me = lax.axis_index("row"), lax.axis_index("col")
    rows, columns = 4, 8
    z, core = me // 2, lax.rem(me, 2)
    partner = me + 1 - 2 * core
    flip_low = row + 1 - 2 * lax.rem(row, 2)
    flip_high = row + 2 - 4 * (row // 2)
    flip_both = 3 - row
    own, depth = tokens.shape
    chip = 2 * own
    count = 8 * own
    chunks = own_parts.shape[0]
    width = down_buf.shape[1]
    half = width // 2
    rank = gate_in.shape[0]
    slots, sides = wide_buf.shape[0], down_buf.shape[0]
    steps = 2 * chunks
    big = 4 * steps
    f32, bf16 = jnp.float32, jnp.bfloat16

    def remote(src, dst, send, recv, where):
        return pltpu.make_async_remote_copy(
            src_ref=src,
            dst_ref=dst,
            send_sem=send,
            recv_sem=recv,
            device_id=where,
            device_id_type=MESH,
        )

    def slot_rows(slot):
        return pl.ds(pl.multiple_of(slot * own, own), own)

    def lanes(c):
        return pl.ds(pl.multiple_of(c * width, width), width)

    def chunk_at(s):
        return (
            s - lead * ((s + big - lead) // big) - (chunks - lead) * ((s + big - lead - chunks) // big)
        )

    def loads(s):
        c, slot, side = chunk_at(s), lax.rem(s, slots), lax.rem(s, sides)
        return [
            pltpu.make_async_copy(
                gate_hbm.at[:, lanes(c)], wide_buf.at[slot, 0], wide_sem.at[slot, 0]
            ),
            pltpu.make_async_copy(
                up_hbm.at[:, lanes(c)], wide_buf.at[slot, 1], wide_sem.at[slot, 1]
            ),
            pltpu.make_async_copy(down_hbm.at[lanes(c), :], down_buf.at[side], down_sem.at[side]),
        ]

    barrier = pltpu.get_barrier_semaphore()

    def row_peer(k):
        return {"row": lax.rem(row + k, rows)}

    def col_peer(k):
        return {"col": lax.rem(me + k, columns)}

    @pl.loop(1, rows)
    def _(k):
        pl.semaphore_signal(barrier, inc=1, device_id=row_peer(k), device_id_type=MESH)

    @pl.loop(1, columns)
    def _(k):
        pl.semaphore_signal(barrier, inc=1, device_id=col_peer(k), device_id_type=MESH)

    factor_loads = []
    for index, (src, dst) in enumerate(
        [
            (down_b, in_rows.at[2, 0:rank]),
            (down_b_dir, in_rows.at[2, rank : 2 * rank]),
            (gate_in, in_rows.at[0, 0:rank]),
            (gate_in_dir, in_rows.at[0, rank : 2 * rank]),
            (up_in, in_rows.at[1, 0:rank]),
            (up_in_dir, in_rows.at[1, rank : 2 * rank]),
            (gate_out, out_rows.at[0, 0:rank]),
            (gate_out_dir, out_rows.at[0, rank : 2 * rank]),
            (up_out, out_rows.at[1, 0:rank]),
            (up_out_dir, out_rows.at[1, rank : 2 * rank]),
            (down_in, out_rows.at[2, 0:rank]),
            (down_in_dir, out_rows.at[2, rank : 2 * rank]),
        ]
    ):
        factor_loads.append(pltpu.make_async_copy(src, dst, factor_sem.at[index]))

    for copy in factor_loads[:6]:
        copy.start()
    for s in range(2):
        for copy in loads(s):
            copy.start()
    for copy in factor_loads[6:]:
        copy.start()

    values = tokens[...].astype(f32)
    squares[0] = jnp.broadcast_to(
        jnp.sum(values * values, axis=1, keepdims=True), squares.shape[1:]
    )
    cot_buf[slot_rows(core), :] = cot[...]
    x_buf[slot_rows(core), :] = (values * gain[...]).astype(bf16)
    line_in[...] = jnp.zeros_like(line_in)
    line_q_in[...] = jnp.zeros_like(line_q_in)
    pl.semaphore_wait(barrier, rows + columns - 2)

    def square(k):
        return remote(
            squares.at[0], squares.at[k], square_sem.at[0, k], square_sem.at[1, k], row_peer(k)
        )

    buffers = (cot_buf, x_buf)
    right, left = {"col": me + 2}, {"col": me - 2}

    def far(which, side, k):
        buffer = buffers[which]
        src = 2 * lax.rem(4 - k, 4) + core if side == 0 else 2 * k + core
        dst = 2 * (3 - k) + core if side == 0 else 2 * (k + 1) + core
        landing = 3 - k if side == 0 else k + 1
        return remote(
            buffer.at[slot_rows(src)],
            buffer.at[slot_rows(dst)],
            far_send.at[which, side, k],
            far_recv.at[which, landing],
            right if side == 0 else left,
        )

    def far_valid(side, k):
        if side == 0:
            return (z < 3) & (z >= k)
        return (z > 0) & (z + k <= 3)

    def far_arrival(which, slot):
        buffer = buffers[which]
        at = buffer.at[slot_rows(2 * slot + core)]
        return remote(at, at, far_send.at[which, 0, 0], far_recv.at[which, slot], {"col": partner})

    def near(which, slot):
        buffer = buffers[which]
        at = buffer.at[slot_rows(2 * slot + core)]
        return remote(
            at, at, near_send.at[which, slot], near_recv.at[which, slot], {"col": partner}
        )

    def near_arrival(which, slot):
        buffer = buffers[which]
        at = buffer.at[slot_rows(2 * slot + 1 - core)]
        return remote(
            at, at, near_send.at[which, slot], near_recv.at[which, slot], {"col": partner}
        )

    def launch(which):
        for side in range(2):

            @pl.when(far_valid(side, 0))
            def _(side=side):
                far(which, side, 0).start()

        near(which, 0).start()

    def pass_on(which, k):
        @pl.when(z >= k)
        def _():
            far_arrival(which, 4 - k).wait_recv()
            if k < 3:

                @pl.when(far_valid(0, k))
                def _():
                    far(which, 0, k).start()

            near(which, 4 - k).start()

        @pl.when(z + k <= 3)
        def _():
            far_arrival(which, k).wait_recv()
            if k < 3:

                @pl.when(far_valid(1, k))
                def _():
                    far(which, 1, k).start()

            near(which, k).start()

    launch(0)
    launch(1)
    for k in range(1, rows):
        square(k).start()
    for copy in factor_loads[:6]:
        copy.wait()
    rank_part[:, 4 * rank :] = cross_shard_total(cot[...], in_rows[2]).astype(bf16)
    own_x = x_buf[slot_rows(core), :]
    rank_part[:, : 2 * rank] = cross_shard_total(own_x, in_rows[0]).astype(bf16)
    rank_part[:, 2 * rank : 4 * rank] = cross_shard_total(own_x, in_rows[1]).astype(bf16)

    def rank_row(k):
        return remote(
            rank_part, rank_in.at[k], rank_sem.at[0, k], rank_sem.at[1, k], row_peer(k)
        )

    for k in range(1, rows):
        rank_row(k).start()

    pass_on(0, 1)

    def clear():
        total[...] = jnp.zeros_like(total)
        for ref in (gate_q, up_q, low_q, gate_curve, up_curve, down_curve):
            ref[...] = jnp.zeros_like(ref)

    def slot_there(k):
        there = lax.rem(me + k, columns) // 2
        return 2 * lax.rem(z - there + 4, 4) + core

    def slot_from(k):
        origin = lax.rem(me - k + columns, columns)
        return 2 * lax.rem(origin // 2 - z + 4, 4) + lax.rem(origin, 2)

    def spread(buffer, sem, k):
        return remote(
            buffer.at[slot_rows(core)],
            buffer.at[slot_rows(slot_there(k))],
            sem.at[0, k],
            sem.at[1, k],
            col_peer(k),
        )

    def spread_arrival(buffer, sem, k):
        at = buffer.at[slot_rows(slot_from(k))]
        return remote(at, at, sem.at[0, k], sem.at[1, k], col_peer(k))

    def share_ranks():
        sum_squares = squares[0]
        summed = rank_part[...].astype(f32)
        for k in range(1, rows):
            square(k).wait_recv()
            sum_squares = sum_squares + squares[k]
            rank_row(k).wait_recv()
            summed = summed + rank_in[k].astype(f32)
        inv = lax.rsqrt(sum_squares / (rows * depth) + epsilon)
        inv_all[slot_rows(core), :] = inv
        for index in range(3):
            at = slice(index * 2 * rank, (index + 1) * 2 * rank)
            block = summed[:, at]
            if index < 2:
                block = block * inv
            rank_all[slot_rows(core), at] = block.astype(bf16)

        @pl.loop(1, columns)
        def _(k):
            spread(rank_all, rank_all_sem, k).start()
            spread(inv_all, inv_sem, k).start()

    partner_step = 7 - 6 * core

    class Group:
        pass

    mine, others = Group(), Group()
    mine.first, mine.size = 0, chip
    mine.left, mine.flip = own_left, own_flip
    others.first, others.size = chip, count - chip
    others.left, others.flip = rest_left, rest_flip

    def prepare(g):
        low = rank_all[g.first : g.first + g.size, :].astype(f32)
        for index in range(3):
            block = low[:, index * 2 * rank : (index + 1) * 2 * rank] * adapter_scale
            lane = lax.broadcasted_iota(jnp.int32, block.shape, 1)
            turned = pltpu.roll(block, rank, 1)
            g.left[index, 0 : g.size, :] = jnp.where(lane < rank, block, 0.0).astype(bf16)
            g.left[index, g.size :, :] = turned.astype(bf16)
            g.flip[index] = turned.T.astype(bf16)

    friends = (flip_both, flip_low, flip_high)

    def own_sends(c, stage):
        return [
            remote(
                own_parts.at[c, peer] if stage == 0 else own_whole.at[c, row],
                own_first.at[c, index] if stage == 0 else own_whole.at[c, row],
                own_send.at[c, stage],
                own_recv.at[c, stage],
                {"row": peer},
            )
            for index, peer in enumerate(friends)
        ]

    def own_all(c, stage):
        return remote(
            own_first.at[c],
            own_first.at[c],
            own_send.at[c, stage],
            own_recv.at[c, stage],
            {"row": flip_both},
        )

    def ends(path):
        return (flip_low, flip_high) if path == 0 else (flip_high, flip_low)

    def send(src, dst, c, path, k, peer):
        away = rest_send.at[c, 1 if k in (2, 5) else 0]
        landed = rest_recv.at[c, 6] if k > 3 else rest_recv.at[c, 3 * path + max(k - 1, 0)]
        return remote(src, dst, away, landed, {"row": peer})

    def sends(c, path, ks):
        near_end, far_end = ends(path)
        table = [
            (rest_parts.at[c, path, near_end], rest_first.at[c, path, 0], near_end),
            (rest_parts.at[c, path, flip_both], rest_first.at[c, path, 1], near_end),
            (rest_mid_out.at[c, path], rest_mid_in.at[c, path], far_end),
            (rest_whole.at[c, path, row], rest_whole.at[c, path, row], far_end),
            (rest_whole.at[c, path, row], rest_whole.at[c, path, row], near_end),
            (rest_whole.at[c, path, far_end], rest_whole.at[c, path, far_end], near_end),
        ]
        return [send(table[k][0], table[k][1], c, path, k, table[k][2]) for k in ks]

    def landed_pair(c, path):
        at = rest_first.at[c, path]
        return remote(at, at, rest_send.at[c, 0], rest_recv.at[c, 3 * path], {"row": flip_low})

    def landed_one(c, path, k):
        at = rest_mid_in.at[c, path]
        return remote(
            at, at, rest_send.at[c, 0], rest_recv.at[c, 3 * path + k - 1], {"row": flip_low}
        )

    def landed_four(c):
        at = rest_first.at[c]
        return remote(at, at, rest_send.at[c, 1], rest_recv.at[c, 6], {"row": flip_low})

    def sent_eight(c):
        at = rest_parts.at[c]
        return remote(at, at, rest_send.at[c, 0], rest_recv.at[c, 6], {"row": flip_low})

    def project(g, c, s):
        for copy in loads(s):
            copy.wait()

        @pl.when(s + 2 < steps)
        def _():
            for copy in loads(s + 2):
                copy.start()

        slot = lax.rem(s, slots)
        span = slice(g.first, g.first + g.size)
        quarter = g.size // 4

        def put(at, value):
            for start in range(0, width, half):
                piece = value[:, start : start + half].reshape(4, quarter, half)
                lane = at * width + start
                if g is mine:
                    own_parts[c, :, :, lane : lane + half] = piece
                else:
                    path, lane = lane // (3 * half), lane % (3 * half)
                    rest_parts[c, path, :, :, lane : lane + half] = piece

        put(0, curvature_product(x_buf[span, :], wide_buf[slot, 0]).astype(bf16))
        put(1, curvature_product(x_buf[span, :], wide_buf[slot, 1]).astype(bf16))
        if g is others:
            for copy in sends(c, 0, (0, 1)):
                copy.start()
        put(2, cross_shard_total(cot_buf[span, :], down_buf[lax.rem(s, sides)]).astype(bf16))
        for copy in own_sends(c, 0) if g is mine else sends(c, 1, (0, 1)):
            copy.start()

    def reduce(g, c, s):
        own_all(c, 0).wait_recv()
        summed = own_parts[c, row].astype(f32)
        for index in range(3):
            summed = summed + own_first[c, index].astype(f32)
        own_whole[c, row] = summed.astype(bf16)
        for copy in own_sends(c, 1):
            copy.start()

    def relay(g, c, s):
        for path in range(2):
            near_end, far_end = ends(path)
            landed_pair(c, path).wait_recv()
            rest_mid_out[c, path] = (
                rest_parts[c, path, far_end].astype(f32) + rest_first[c, path, 1].astype(f32)
            ).astype(bf16)
            sends(c, path, (2,))[0].start()

    def settle(g, c, s):
        for path in range(2):
            landed_one(c, path, 2).wait_recv()
            rest_whole[c, path, row] = (
                rest_parts[c, path, row].astype(f32)
                + rest_first[c, path, 0].astype(f32)
                + rest_mid_in[c, path].astype(f32)
            ).astype(bf16)
            for copy in sends(c, path, (3, 4)):
                copy.start()

    def forward(g, c, s):
        for path in range(2):
            landed_one(c, path, 3).wait_recv()
            sends(c, path, (5,))[0].start()

    def differentiate(g, c, s):
        if g is mine:
            own_all(c, 1).wait_recv()
        else:
            landed_four(c).wait_recv()
        size = g.size

        def got(at):
            pieces = []
            for start in range(0, width, half):
                lane = at * width + start
                if g is mine:
                    piece = own_whole[c, :, :, lane : lane + half]
                else:
                    path, lane = lane // (3 * half), lane % (3 * half)
                    piece = rest_whole[c, path, :, :, lane : lane + half]
                piece = piece.reshape(size, half).astype(f32)
                if at < 2:
                    piece = piece * inv_all[g.first : g.first + size, :]
                pieces.append(piece)
            return jnp.concatenate(pieces, axis=1)

        gate_w, up_w, down_w = out_rows[0, :, lanes(c)], out_rows[1, :, lanes(c)], out_rows[2, :, lanes(c)]
        gate_low = curvature_product(g.left[0], gate_w)
        up_low = curvature_product(g.left[1], up_w)
        adj_low = curvature_product(g.left[2], down_w)
        hidden, hidden_dir, d_gate, d_up, d_gate_dir, d_up_dir = second_order(
            got(0) + gate_low[:size],
            got(1) + up_low[:size],
            got(2) + adj_low[:size],
            gate_low[size:],
            up_low[size:],
            adj_low[size:],
        )
        gate_d = jnp.concatenate([d_gate, d_gate_dir], axis=0)
        up_d = jnp.concatenate([d_up, d_up_dir], axis=0)
        hidden_d = jnp.concatenate([hidden_dir, hidden], axis=0)
        span = slice(g.first, g.first + size)
        gate_curve[:, lanes(c)] += curvature_product(
            g.flip[0, :rank], d_gate
        ) + curvature_product(g.flip[0, rank:], d_gate_dir)
        up_curve[:, lanes(c)] += curvature_product(g.flip[1, :rank], d_up) + curvature_product(
            g.flip[1, rank:], d_up_dir
        )
        down_curve[:, lanes(c)] += curvature_product(
            g.flip[2, rank:], hidden_dir
        ) + curvature_product(g.flip[2, :rank], hidden)
        for ref, value, weight in (
            (gate_q, gate_d, gate_w),
            (up_q, up_d, up_w),
            (low_q, hidden_d, down_w),
        ):
            product = cross_shard_total(value, weight)
            ref[0, span, :] += product[:size]
            ref[1, span, :] += product[size:]
        slot = lax.rem(s, slots)
        piece = 512 if depth % 512 == 0 else depth
        for start in range(0, depth, piece):
            at = slice(start, start + piece)
            product = cross_shard_total(gate_d, wide_buf[slot, 0, at, :]) + cross_shard_total(
                up_d, wide_buf[slot, 1, at, :]
            )
            total[0, span, at] += product[:size]
            total[1, span, at] += product[size:]

    def q_rows(slot):
        at = slot_rows(slot)
        lane = lax.broadcasted_iota(jnp.int32, (own, 2 * rank), 1)
        low_half = lane < rank
        gate = gate_q[0, at, :] + jnp.where(low_half, 0.0, pltpu.roll(gate_q[1, at, :], rank, 1))
        up = up_q[0, at, :] + jnp.where(low_half, 0.0, pltpu.roll(up_q[1, at, :], rank, 1))
        low = jnp.where(low_half, low_q[0, at, :] + pltpu.roll(low_q[1, at, :], rank, 1), 0.0)
        return jnp.concatenate([gate, up, low], axis=1)

    def pair(src, dst, at):
        return remote(src, dst, pair_sem.at[0, at], pair_sem.at[1, at], {"col": partner})

    def pairs():
        return [pair(pair_out, pair_in, 0), pair(pair_q_out, pair_q_in, 1)]

    def exchange():
        for k in range(1, 4):
            slot = 2 * k + 1 - core
            for kind in range(2):
                pair_out[k - 1, kind] = total[kind, slot_rows(slot), :].astype(bf16)
            pair_q_out[k - 1] = q_rows(slot).astype(bf16)
        for copy in pairs():
            copy.start()

    def line(side, k, kind):
        out = k - 1 if side == 0 else 3 - k
        src = line_out.at[out, kind] if kind < 2 else line_q_out.at[out]
        dst = line_in.at[side, k - 1, kind] if kind < 2 else line_q_in.at[side, k - 1]
        return remote(
            src,
            dst,
            line_sem.at[0, side, k - 1, kind],
            line_sem.at[1, side, k - 1, kind],
            right if side == 0 else left,
        )

    def line_arrival(side, k, kind):
        at = line_in.at[side, k, kind] if kind < 2 else line_q_in.at[side, k]
        return remote(
            at,
            at,
            line_sem.at[0, side, k, kind],
            line_sem.at[1, side, k, kind],
            {"col": partner},
        )

    def line_valid(side, k):
        return z + k <= 3 if side == 0 else z - k >= 0

    def line_fed(side):
        return z >= 1 if side == 0 else z <= 2

    def line_send(side, k, kinds):
        at = k if side == 0 else 4 - k
        slot = 2 * at + core
        for kind in kinds:
            if kind < 2:
                value = total[kind, slot_rows(slot), :] + pair_in[at - 1, kind].astype(f32)
                if k < 3:
                    value = value + line_in[side, k, kind].astype(f32)
                line_out[at - 1, kind] = value.astype(bf16)
            else:
                value = q_rows(slot) + pair_q_in[at - 1].astype(f32)
                if k < 3:
                    value = value + line_q_in[side, k].astype(f32)
                line_q_out[at - 1] = value.astype(bf16)
            line(side, k, kind).start()

    def line_open():
        for copy in pairs():
            copy.wait_recv()
        for side in range(2):
            for k in (3, 2, 1):

                @pl.when(line_valid(side, k) & ((z == 0) if side == 0 else (z == 3)))
                def _(side=side, k=k):
                    line_send(side, k, (0, 1, 2))

    def line_stage(k, kinds):
        for side in range(2):

            @pl.when(line_valid(side, k) & line_fed(side))
            def _(side=side):
                for kind in kinds:
                    line_arrival(side, k, kind).wait_recv()
                line_send(side, k, kinds)

    def line_end():
        for side in range(2):

            @pl.when(line_fed(side))
            def _(side=side):
                for kind in range(3):
                    line_arrival(side, 0, kind).wait_recv()

    turn = lead + chunks
    resume = turn + gap
    rest_end = turn + 3
    late = {
        rest_end: exchange,
        rest_end + 1: line_open,
        rest_end + 3: functools.partial(line_stage, 2, (0,)),
        rest_end + 4: functools.partial(line_stage, 2, (1, 2)),
        rest_end + 5: functools.partial(line_stage, 1, (0,)),
        rest_end + 6: functools.partial(line_stage, 1, (1, 2)),
    }
    relays = [(1, 1), (0, 2), (1, 2), (0, 3), (1, 3)]
    early = max(min(lead - 3, len(relays)), 0)

    def share():
        share_ranks()
        clear()

    def arrive():
        for which, k in relays[early:]:
            pass_on(which, k)
        for which in range(2):
            for k in range(1, 4):
                near_arrival(which, k).wait_recv()

    def first_ready():
        for copy in factor_loads[6:]:
            copy.wait()
        spread_arrival(rank_all, rank_all_sem, partner_step).wait_recv()
        spread_arrival(inv_all, inv_sem, partner_step).wait_recv()
        prepare(mine)

    def rest_ready():
        @pl.loop(1, columns)
        def _(k):
            @pl.when(k != partner_step)
            def _():
                spread_arrival(rank_all, rank_all_sem, k).wait_recv()
                spread_arrival(inv_all, inv_sem, k).wait_recv()

        prepare(others)

    for which in range(2):
        near_arrival(which, 0).wait_recv()

    last_step = steps + gap + 4

    @pl.loop(0, last_step)
    def _(t):
        def at_step(step, action):
            @pl.when(t == step)
            def _():
                action()

        def own_stage(lag, stage):
            u = t - lag
            after = (u + big - resume) // big
            s = u - gap * after

            @pl.when(((u >= 0) & (u < lead)) | ((u >= resume) & (u < steps + gap)))
            def _():
                stage(mine, s - chunks * after, s)

        def rest_stage(lag, stage):
            s = t - lag

            @pl.when((s >= lead) & (s < turn))
            def _():
                stage(others, s - lead, s)

        at_step(lead, arrive)
        at_step(4, first_ready)
        at_step(lead + 4, rest_ready)
        for lag, stage in enumerate((project, relay, settle, forward, differentiate)):
            rest_stage(lag, stage)
        for step, action in late.items():
            if step < last_step:
                at_step(step, action)
        own_stage(0, project)
        at_step(0, share)
        own_stage(2, reduce)
        own_stage(4, differentiate)
        for index, (which, k) in enumerate(relays[:early]):
            at_step(index + 1 + index // 3, functools.partial(pass_on, which, k))

    for step, action in late.items():
        if step >= last_step:
            action()

    def outputs(index):
        src, dst = (
            (primal_ref, primal_out),
            (dir_ref, dir_out),
            (gate_curve_in, gate_curve_in_out),
            (gate_curve, gate_curve_hbm),
            (up_curve_in, up_curve_in_out),
            (up_curve, up_curve_hbm),
            (down_curve, down_curve_hbm),
            (down_curve_out, down_curve_out_out),
        )[index]
        return pltpu.make_async_copy(src, dst, out_sem.at[index])

    def lasts():
        return [
            remote(last_out, last_in, last_sem.at[0, 0], last_sem.at[1, 0], {"col": partner}),
            remote(last_q_out, last_q_in, last_sem.at[0, 1], last_sem.at[1, 1], {"col": partner}),
        ]

    last_feature, last_q = lasts()
    last_q_out[...] = q_rows(1 - core).astype(bf16)
    last_q.start()
    for kind in range(2):
        last_out[kind] = total[kind, slot_rows(1 - core), :].astype(bf16)
    last_feature.start()
    for index in (3, 5, 6):
        outputs(index).start()

    @pl.loop(0, chunks)
    def _(c):
        own_all(c, 0).wait_send()
        own_all(c, 1).wait_send()
        sent_eight(c).wait_send()
        landed_four(c).wait_send()

    line_end()
    last_q.wait_recv()
    q_own = (
        q_rows(core)
        + last_q_in[...].astype(f32)
        + line_q_in[0, 0].astype(f32)
        + line_q_in[1, 0].astype(f32)
    )
    q_all[slot_rows(core), :] = q_own.astype(bf16)

    @pl.loop(1, columns)
    def _(k):
        spread(q_all, q_sem, k).start()

    last_feature.wait_recv()
    lane = lax.broadcasted_iota(jnp.int32, (own, 2 * rank), 1)
    feature = [
        total[kind, slot_rows(core), :]
        + last_in[kind].astype(f32)
        + line_in[0, 0, kind].astype(f32)
        + line_in[1, 0, kind].astype(f32)
        for kind in range(2)
    ]
    for index in range(2):
        block = q_own[:, index * 2 * rank : (index + 1) * 2 * rank] * adapter_scale
        straight = jnp.where(lane < rank, block, 0.0).astype(bf16)
        turned = pltpu.roll(block, rank, 1).astype(bf16)
        feature[0] = feature[0] + curvature_product(straight, in_rows[index])
        feature[1] = feature[1] + curvature_product(turned, in_rows[index])
    primal_ref[...] = feature[0]
    dir_ref[...] = feature[1]
    for index in (0, 1):
        outputs(index).start()

    @pl.loop(1, columns)
    def _(k):
        spread_arrival(q_all, q_sem, k).wait_recv()

    every = q_all[...].astype(f32) * adapter_scale
    lane = lax.broadcasted_iota(jnp.int32, (count, 2 * rank), 1)
    both = jnp.where(
        lane < rank, pltpu.roll(every[:, : 2 * rank], rank, 1), every[:, 2 * rank : 4 * rank]
    )
    both = both * inv_all[...]
    both_t = both.T.astype(bf16)
    low_t = every[:, 4 * rank :].T.astype(bf16)
    down_curve_out[...] = curvature_product(low_t[:rank], cot_buf[...])
    outputs(7).start()
    product = curvature_product(both_t, x_buf[...])
    gate_curve_in[...] = product[:rank]
    up_curve_in[...] = product[rank:]
    for index in (2, 4):
        outputs(index).start()

    for k in range(1, rows):
        square(k).wait_send()
        rank_row(k).wait_send()
    for which in range(2):
        for side in range(2):
            for k in range(3):

                @pl.when(far_valid(side, k))
                def _(which=which, side=side, k=k):
                    far(which, side, k).wait_send()

        for k in range(4):
            near(which, k).wait_send()

    @pl.loop(1, columns)
    def _(k):
        spread(rank_all, rank_all_sem, k).wait_send()
        spread(inv_all, inv_sem, k).wait_send()
        spread(q_all, q_sem, k).wait_send()

    for copy in pairs() + [last_feature, last_q]:
        copy.wait_send()
    for side in range(2):
        for k in range(1, 4):

            @pl.when(line_valid(side, k))
            def _(side=side, k=k):
                for kind in range(3):
                    line(side, k, kind).wait_send()

    for index in range(8):
        outputs(index).wait()


def handover_kernel(*refs):
    sources, targets, held, sem = refs[:8], refs[8:16], refs[16:24], refs[24]
    fetch = [
        pltpu.make_async_copy(sources[i], held[i], sem.at[0, i]) for i in range(len(sources))
    ]
    place = [
        pltpu.make_async_copy(held[i], targets[i], sem.at[1, i]) for i in range(len(sources))
    ]
    for copy in fetch:
        copy.start()
    for arrive, leave in zip(fetch, place):
        arrive.wait()
        leave.start()
    for copy in place:
        copy.wait()


def fused(
    tokens,
    norm_gain,
    cotangent,
    gate_frozen_weight,
    up_frozen_weight,
    down_frozen_weight,
    gate_input_factor,
    gate_output_factor,
    up_input_factor,
    up_output_factor,
    down_input_factor,
    down_b,
    gate_input_factor_direction,
    gate_output_factor_direction,
    up_input_factor_direction,
    up_output_factor_direction,
    down_input_factor_direction,
    down_b_dir,
    width,
):
    own, depth = tokens.shape
    hidden = gate_frozen_weight.shape[1]
    rank = gate_output_factor.shape[0]
    chunks = hidden // width
    chip, rest, count = 2 * own, 6 * own, 8 * own
    lead, gap = chunks // 2, 2
    half_panel = 3 * width // 2
    f32, bf16 = jnp.float32, jnp.bfloat16
    vmem = pl.BlockSpec(memory_space=pltpu.VMEM)
    anywhere = pl.BlockSpec(memory_space=pl.ANY)

    def reduce_buffers(size):
        quarter = size // 4
        return [
            pltpu.VMEM((chunks, 2, 4, quarter, half_panel), bf16),
            pltpu.VMEM((chunks, 2, 2, quarter, half_panel), bf16),
            pltpu.VMEM((chunks, 2, quarter, half_panel), bf16),
            pltpu.VMEM((chunks, 2, quarter, half_panel), bf16),
            pltpu.VMEM((chunks, 2, 4, quarter, half_panel), bf16),
        ]

    dma = pltpu.SemaphoreType.DMA
    slots, sides = 7, 3
    shapes = [
        jax.ShapeDtypeStruct((own, depth), f32),
        jax.ShapeDtypeStruct((own, depth), f32),
        jax.ShapeDtypeStruct((rank, depth), f32),
        jax.ShapeDtypeStruct((rank, hidden), f32),
        jax.ShapeDtypeStruct((rank, depth), f32),
        jax.ShapeDtypeStruct((rank, hidden), f32),
        jax.ShapeDtypeStruct((rank, hidden), f32),
        jax.ShapeDtypeStruct((rank, depth), f32),
    ]
    results = pl.pallas_call(
        functools.partial(lora_kernel, lead, gap),
        out_shape=shapes,
        in_specs=[vmem] * 3 + [anywhere] * 15,
        out_specs=[anywhere] * 8,
        scratch_shapes=[pltpu.VMEM(shape.shape, f32) for shape in shapes]
        + [
            pltpu.VMEM((count, depth), bf16),
            pltpu.VMEM((count, depth), bf16),
            pltpu.VMEM((4, own, 2 * rank), f32),
            pltpu.VMEM((own, 6 * rank), bf16),
            pltpu.VMEM((4, own, 6 * rank), bf16),
            pltpu.VMEM((count, 6 * rank), bf16),
            pltpu.VMEM((count, 2 * rank), f32),
            pltpu.VMEM((3, 2 * rank, depth), bf16),
            pltpu.VMEM((3, 2 * rank, hidden), bf16),
            pltpu.VMEM((slots, 2, depth, width), bf16),
            pltpu.VMEM((sides, width, depth), bf16),
        ]
        + [
            pltpu.VMEM((chunks, 4, chip // 4, 3 * width), bf16),
            pltpu.VMEM((chunks, 3, chip // 4, 3 * width), bf16),
            pltpu.VMEM((chunks, 4, chip // 4, 3 * width), bf16),
        ]
        + reduce_buffers(rest)
        + [
            pltpu.VMEM((3, 2 * chip, 2 * rank), bf16),
            pltpu.VMEM((3, 2 * rank, chip), bf16),
            pltpu.VMEM((3, 2 * rest, 2 * rank), bf16),
            pltpu.VMEM((3, 2 * rank, rest), bf16),
            pltpu.VMEM((2, count, depth), f32),
            pltpu.VMEM((2, count, 2 * rank), f32),
            pltpu.VMEM((2, count, 2 * rank), f32),
            pltpu.VMEM((2, count, 2 * rank), f32),
            pltpu.VMEM((3, 2, own, depth), bf16),
            pltpu.VMEM((3, 2, own, depth), bf16),
            pltpu.VMEM((3, own, 6 * rank), bf16),
            pltpu.VMEM((3, own, 6 * rank), bf16),
            pltpu.VMEM((3, 2, own, depth), bf16),
            pltpu.VMEM((2, 3, 2, own, depth), bf16),
            pltpu.VMEM((3, own, 6 * rank), bf16),
            pltpu.VMEM((2, 3, own, 6 * rank), bf16),
            pltpu.VMEM((2, own, depth), bf16),
            pltpu.VMEM((2, own, depth), bf16),
            pltpu.VMEM((own, 6 * rank), bf16),
            pltpu.VMEM((own, 6 * rank), bf16),
            pltpu.VMEM((count, 6 * rank), bf16),
            dma((12,)),
            dma((slots, 2)),
            dma((sides,)),
            dma((2, 4)),
            dma((2, 4)),
            dma((2, 2, 3)),
            dma((2, 4)),
            dma((2, 4)),
            dma((2, 4)),
            dma((2, 8)),
            dma((2, 8)),
            dma((chunks, 2)),
            dma((chunks, 2)),
            dma((chunks, 2)),
            dma((chunks, 7)),
            dma((2, 2)),
            dma((2, 2, 3, 3)),
            dma((2, 2)),
            dma((2, 8)),
            dma((8,)),
        ],
        compiler_params=pltpu.CompilerParams(
            collective_id=2, has_side_effects=True, vmem_limit_bytes=63 * 1024 * 1024
        ),
        name="lora",
    )(
        tokens,
        norm_gain.reshape(1, depth),
        cotangent,
        gate_frozen_weight,
        up_frozen_weight,
        down_frozen_weight,
        gate_input_factor.T,
        gate_input_factor_direction.T,
        up_input_factor.T,
        up_input_factor_direction.T,
        down_b,
        down_b_dir,
        gate_output_factor,
        gate_output_factor_direction,
        up_output_factor,
        up_output_factor_direction,
        down_input_factor.T,
        down_input_factor_direction.T,
    )
    primal, direction, gate_input, gate_output, up_input, up_output, down_input, down_output = (
        pl.pallas_call(
            handover_kernel,
            out_shape=shapes,
            in_specs=[anywhere] * 8,
            out_specs=[anywhere] * 8,
            scratch_shapes=[pltpu.VMEM(shape.shape, f32) for shape in shapes] + [dma((2, 8))],
            name="handover",
        )(*results)
    )
    return (
        primal,
        direction,
        gate_input.T,
        gate_output,
        up_input.T,
        up_output,
        down_input.T,
        down_output,
    )


def gather_kernel(
    tokens,
    gain,
    cot,
    x_all,
    cot_all,
    x_buf,
    cot_buf,
    squares,
    square_send,
    square_recv,
    far_send,
    far_recv,
    near_send,
    near_recv,
):
    rows, columns = lax.axis_size("row"), lax.axis_size("col")
    chips = columns // 2
    my_row, me = lax.axis_index("row"), lax.axis_index("col")
    partner = me + 1 - 2 * lax.rem(me, 2)
    features = rows * tokens.shape[1]
    barrier = pltpu.get_barrier_semaphore()

    def row_peer(k):
        return {"row": lax.rem(my_row + k, rows)}

    def far_peer(k):
        return {"col": lax.rem(me + 2 * k, columns)}

    @pl.loop(1, rows)
    def _(k):
        pl.semaphore_signal(barrier, inc=1, device_id=row_peer(k), device_id_type=MESH)

    @pl.loop(1, chips)
    def _(k):
        pl.semaphore_signal(barrier, inc=1, device_id=far_peer(k), device_id_type=MESH)

    pl.semaphore_signal(barrier, inc=1, device_id={"col": partner}, device_id_type=MESH)

    buffers = (cot_buf, x_buf)

    def origin(k):
        return lax.rem(me - 2 * k + columns, columns)

    def square(k):
        return pltpu.make_async_remote_copy(
            src_ref=squares.at[0],
            dst_ref=squares.at[k],
            send_sem=square_send.at[k],
            recv_sem=square_recv.at[k],
            device_id=row_peer(k),
            device_id_type=MESH,
        )

    def far(which, k, slot):
        return pltpu.make_async_remote_copy(
            src_ref=buffers[which].at[slot],
            dst_ref=buffers[which].at[slot],
            send_sem=far_send.at[which, k],
            recv_sem=far_recv.at[which, k],
            device_id=far_peer(k),
            device_id_type=MESH,
        )

    def near(which, k, slot):
        return pltpu.make_async_remote_copy(
            src_ref=buffers[which].at[slot],
            dst_ref=buffers[which].at[slot],
            send_sem=near_send.at[which, k],
            recv_sem=near_recv.at[which, k],
            device_id={"col": partner},
            device_id_type=MESH,
        )

    def launch(which):
        @pl.loop(1, chips)
        def _(k):
            far(which, k, me).start()

        near(which, 0, me).start()

    values = tokens[...].astype(jnp.float32)
    squares[0] = jnp.broadcast_to(
        jnp.sum(values * values, axis=1, keepdims=True), squares.shape[1:]
    )
    cot_buf[me] = cot[...]
    pl.semaphore_wait(barrier, rows + chips - 1)

    @pl.loop(1, rows)
    def _(k):
        square(k).start()

    launch(0)

    def add(k, total):
        square(k).wait_recv()
        return total + squares[k]

    total = lax.fori_loop(1, rows, add, squares[0])
    scale = lax.rsqrt(total[:, :1] / features + epsilon)
    x_buf[me] = (tokens[...].astype(jnp.float32) * scale * gain[...]).astype(jnp.bfloat16)
    launch(1)
    for which in range(2):

        @pl.loop(1, chips)
        def _(k, which=which):
            far(which, k, origin(k)).wait_recv()
            near(which, k, origin(k)).start()

    for which in range(2):

        @pl.loop(0, chips)
        def _(k, which=which):
            near(which, k, lax.rem(partner - 2 * k + columns, columns)).wait_recv()

    @pl.loop(1, rows)
    def _(k):
        square(k).wait_send()

    for which in range(2):

        @pl.loop(1, chips)
        def _(k, which=which):
            far(which, k, me).wait_send()

        @pl.loop(0, chips)
        def _(k, which=which):
            near(which, k, origin(k)).wait_send()

    cot_all[...] = cot_buf[...]
    x_all[...] = x_buf[...]


def gathered(tokens, gain, cot):
    rows, columns = lax.axis_size("row"), lax.axis_size("col")
    own, depth = tokens.shape
    whole = (columns, own, depth)
    vmem = pl.BlockSpec(memory_space=pltpu.VMEM)
    x, panel = pl.pallas_call(
        gather_kernel,
        out_shape=[jax.ShapeDtypeStruct(whole, jnp.bfloat16)] * 2,
        in_specs=[vmem] * 3,
        out_specs=[vmem] * 2,
        scratch_shapes=[
            pltpu.VMEM(whole, jnp.bfloat16),
            pltpu.VMEM(whole, jnp.bfloat16),
            pltpu.VMEM((rows, own, 128), jnp.float32),
            pltpu.SemaphoreType.DMA((rows,)),
            pltpu.SemaphoreType.DMA((rows,)),
            pltpu.SemaphoreType.DMA((2, columns // 2)),
            pltpu.SemaphoreType.DMA((2, columns // 2)),
            pltpu.SemaphoreType.DMA((2, columns // 2)),
            pltpu.SemaphoreType.DMA((2, columns // 2)),
        ],
        compiler_params=pltpu.CompilerParams(collective_id=3, has_side_effects=True),
        name="gather",
    )(tokens, gain.reshape(1, depth), cot)
    return x.reshape(columns * own, depth), panel.reshape(columns * own, depth)


def chunk_count(width):
    for count in (4, 2):
        if width % (128 * count) == 0:
            return count
    return 1


def on_device(
    tokens,
    norm_gain,
    cotangent,
    gate_frozen_weight,
    up_frozen_weight,
    down_frozen_weight,
    gate_input_factor,
    gate_output_factor,
    up_input_factor,
    up_output_factor,
    down_input_factor,
    down_b,
    gate_input_factor_direction,
    gate_output_factor_direction,
    up_input_factor_direction,
    up_output_factor_direction,
    down_input_factor_direction,
    down_b_dir,
):
    width = 256
    if (
        lax.axis_size("row") == 4
        and lax.axis_size("col") == 8
        and gate_frozen_weight.shape[1] % (14 * width) == 0
        and gate_frozen_weight.shape[0] % 128 == 0
        and gate_input_factor.shape[1] == 64
        and tokens.shape[0] % 32 == 0
    ):
        return fused(
            tokens,
            norm_gain,
            cotangent,
            gate_frozen_weight,
            up_frozen_weight,
            down_frozen_weight,
            gate_input_factor,
            gate_output_factor,
            up_input_factor,
            up_output_factor,
            down_input_factor,
            down_b,
            gate_input_factor_direction,
            gate_output_factor_direction,
            up_input_factor_direction,
            up_output_factor_direction,
            down_input_factor_direction,
            down_b_dir,
            width,
        )
    rank = gate_input_factor.shape[1]
    width_rows, width_columns = gate_frozen_weight.shape
    own_count = tokens.shape[0]
    normed_tokens, cot_panel = gathered(tokens, norm_gain, cotangent)
    count = normed_tokens.shape[0]
    in_factors = jnp.concatenate(
        [
            gate_input_factor,
            up_input_factor,
            gate_input_factor_direction,
            up_input_factor_direction,
        ],
        axis=1,
    )
    out_factors = jnp.concatenate([down_b, down_b_dir], axis=0)

    projected = jnp.concatenate(
        [curvature_product(normed_tokens, in_factors), cross_shard_total(cot_panel, out_factors)],
        axis=1,
    )
    ranks = shard_total(projected, "row", 0)
    gate_out = jnp.concatenate([gate_output_factor, gate_output_factor_direction], axis=0)
    up_out = jnp.concatenate([up_output_factor, up_output_factor_direction], axis=0)
    down_in = jnp.concatenate([down_input_factor, down_input_factor_direction], axis=1)

    chunks = chunk_count(width_columns)
    wide = width_columns // chunks
    spans = [slice(index * wide, (index + 1) * wide) for index in range(chunks)]

    summed_chunks = []
    for span in spans:
        partial = (
            curvature_product(normed_tokens, gate_frozen_weight[:, span]).astype(jnp.bfloat16),
            curvature_product(normed_tokens, up_frozen_weight[:, span]).astype(jnp.bfloat16),
            cross_shard_total(cot_panel, down_frozen_weight[span]).astype(jnp.bfloat16),
        )
        if summed_chunks:
            partial, summed_chunks[-1] = lax.optimization_barrier((partial, summed_chunks[-1]))
        summed_chunks.append(lax.psum(partial, "row"))

    gate_low, up_low, gate_low_dir, up_low_dir, adj_low, adj_low_dir = [
        ranks[:, index * rank : (index + 1) * rank] for index in range(6)
    ]
    gate_pair = jnp.concatenate([gate_low_dir, gate_low], axis=1)
    up_pair = jnp.concatenate([up_low_dir, up_low], axis=1)
    adj_pair = jnp.concatenate([adj_low_dir, adj_low], axis=1)
    gate_stack = jnp.concatenate([gate_low_dir, gate_low], axis=0)
    up_stack = jnp.concatenate([up_low_dir, up_low], axis=0)
    adj_stack = jnp.concatenate([adj_low, adj_low_dir], axis=0)
    feature = 0.0
    gate_q = 0.0
    up_q = 0.0
    low_dir = 0.0
    gate_output, up_output, down_input = [], [], []
    for span, total in zip(spans, summed_chunks):
        gate_sum, up_sum, adj_sum = [value.astype(jnp.float32) for value in total]
        gate_pre = gate_sum + adapter_scale * curvature_product(
            gate_low, gate_output_factor[:, span]
        )
        up_pre = up_sum + adapter_scale * curvature_product(
            up_low, up_output_factor[:, span]
        )
        hidden_adj = adj_sum + adapter_scale * cross_shard_total(
            adj_low, down_input_factor[span]
        )
        gate_tan = adapter_scale * curvature_product(gate_pair, gate_out[:, span])
        up_tan = adapter_scale * curvature_product(up_pair, up_out[:, span])
        adj_tan = adapter_scale * cross_shard_total(adj_pair, down_in[span])
        hidden, hidden_dir, d_gate, d_up, d_gate_dir, d_up_dir = second_order(
            gate_pre, up_pre, hidden_adj, gate_tan, up_tan, adj_tan
        )
        gate_d = jnp.concatenate([d_gate, d_gate_dir], axis=0)
        up_d = jnp.concatenate([d_up, d_up_dir], axis=0)
        hidden_d = jnp.concatenate([hidden_dir, hidden], axis=0)
        gate_output.append(adapter_scale * summed_over_rows(gate_stack, gate_d))
        up_output.append(adapter_scale * summed_over_rows(up_stack, up_d))
        down_input.append(adapter_scale * summed_over_rows(hidden_d, adj_stack))
        gate_q = gate_q + cross_shard_total(gate_d, gate_out[:, span])
        up_q = up_q + cross_shard_total(up_d, up_out[:, span])
        low_dir = (
            low_dir
            + curvature_product(hidden_dir, down_input_factor[span])
            + curvature_product(hidden, down_input_factor_direction[span])
        )
        feature = (
            feature
            + cross_shard_total(gate_d, gate_frozen_weight[:, span])
            + cross_shard_total(up_d, up_frozen_weight[:, span])
        )
    gate_output = jnp.concatenate(gate_output, axis=1)
    up_output = jnp.concatenate(up_output, axis=1)
    down_input = jnp.concatenate(down_input, axis=0)

    summed = lax.psum_scatter(
        feature.astype(jnp.bfloat16).reshape(2, count, width_rows),
        "col",
        scatter_dimension=1,
        tiled=True,
    ).astype(jnp.float32)
    adjoints = shard_total(
        jnp.concatenate(
            [
                gate_q[:count, :rank],
                up_q[:count, :rank],
                gate_q[count:, :rank] + gate_q[:count, rank:],
                up_q[count:, :rank] + up_q[:count, rank:],
                low_dir,
            ],
            axis=1,
        ).astype(jnp.bfloat16),
        "col",
        1,
    )
    piece = lax.dynamic_slice_in_dim(adjoints, lax.axis_index("col") * own_count, own_count, 0)
    normed_feature_adjoint = summed[0] + adapter_scale * cross_shard_total(
        piece[:, : 2 * rank], in_factors[:, : 2 * rank]
    )
    normed_feature_adjoint_direction = summed[1] + adapter_scale * cross_shard_total(
        jnp.concatenate([piece[:, 2 * rank : 4 * rank], piece[:, : 2 * rank]], axis=1), in_factors
    )
    gate_input = adapter_scale * summed_over_rows(
        normed_tokens, adjoints[:, 2 * rank : 3 * rank]
    )
    up_input = adapter_scale * summed_over_rows(normed_tokens, adjoints[:, 3 * rank : 4 * rank])
    down_output = adapter_scale * summed_over_rows(adjoints[:, 4 * rank :], cot_panel)
    return (
        normed_feature_adjoint,
        normed_feature_adjoint_direction,
        gate_input,
        gate_output,
        up_input,
        up_output,
        down_input,
        down_output,
    )


def solution(mesh):
    in_specs = (
        P("col", "row"),
        P("row"),
        P("col", "row"),
        P("row", "col"),
        P("row", "col"),
        P("col", "row"),
        P("row", None),
        P(None, "col"),
        P("row", None),
        P(None, "col"),
        P("col", None),
        P(None, "row"),
        P("row", None),
        P(None, "col"),
        P("row", None),
        P(None, "col"),
        P("col", None),
        P(None, "row"),
    )
    out_specs = (
        P("col", "row"),
        P("col", "row"),
        P("row", None),
        P(None, "col"),
        P("row", None),
        P(None, "col"),
        P("col", None),
        P(None, "row"),
    )
    return jax.shard_map(
        on_device, mesh=mesh, in_specs=in_specs, out_specs=out_specs, check_vma=False
    )
```

```python
import functools

import jax
import jax.numpy as jnp
from jax import lax
from jax.experimental import pallas as pl
from jax.experimental.pallas import tpu as pltpu
from jax.sharding import PartitionSpec as P

adapter_scale = 0.5
epsilon = 1e-05
MESH = pl.DeviceIdType.MESH


def total_kernel(axis, n, x_ref, o_ref, inbox, whole, send1, recv1, send2, recv2):
    me = lax.axis_index(axis)
    barrier = pltpu.get_barrier_semaphore()

    @pl.loop(1, n)
    def _(k):
        pl.semaphore_signal(
            barrier, inc=1, device_id={axis: lax.rem(me + k, n)}, device_id_type=MESH
        )

    pl.semaphore_wait(barrier, n - 1)

    def scatter(k):
        peer = lax.rem(me + k, n)
        return pltpu.make_async_remote_copy(
            src_ref=x_ref.at[peer],
            dst_ref=inbox.at[k],
            send_sem=send1.at[k],
            recv_sem=recv1.at[k],
            device_id={axis: peer},
            device_id_type=MESH,
        )

    def spread(k):
        peer = lax.rem(me + k, n)
        return pltpu.make_async_remote_copy(
            src_ref=whole.at[me],
            dst_ref=whole.at[me],
            send_sem=send2.at[k],
            recv_sem=recv2.at[k],
            device_id={axis: peer},
            device_id_type=MESH,
        )

    def arrival(k):
        origin = lax.rem(me - k + n, n)
        return pltpu.make_async_remote_copy(
            src_ref=whole.at[origin],
            dst_ref=whole.at[origin],
            send_sem=send2.at[k],
            recv_sem=recv2.at[k],
            device_id={axis: origin},
            device_id_type=MESH,
        )

    @pl.loop(1, n)
    def _(k):
        scatter(k).start()

    def add(k, total):
        scatter(k).wait_recv()
        return total + inbox[k].astype(jnp.float32)

    total = lax.fori_loop(1, n, add, x_ref[me].astype(jnp.float32))
    whole[me] = total.astype(whole.dtype)

    @pl.loop(1, n)
    def _(k):
        spread(k).start()

    @pl.loop(1, n)
    def _(k):
        arrival(k).wait_recv()

    @pl.loop(1, n)
    def _(k):
        scatter(k).wait_send()
        spread(k).wait_send()

    o_ref[...] = whole[...]


def shard_total(x, axis, collective_id):
    n = lax.axis_size(axis)
    rows, columns = x.shape
    block = (n, rows // n, columns)
    total = pl.pallas_call(
        functools.partial(total_kernel, axis, n),
        out_shape=jax.ShapeDtypeStruct(block, jnp.bfloat16),
        in_specs=[pl.BlockSpec(memory_space=pltpu.VMEM)],
        out_specs=pl.BlockSpec(memory_space=pltpu.VMEM),
        scratch_shapes=[
            pltpu.VMEM(block, x.dtype),
            pltpu.VMEM(block, jnp.bfloat16),
            pltpu.SemaphoreType.DMA((n,)),
            pltpu.SemaphoreType.DMA((n,)),
            pltpu.SemaphoreType.DMA((n,)),
            pltpu.SemaphoreType.DMA((n,)),
        ],
        compiler_params=pltpu.CompilerParams(collective_id=collective_id, has_side_effects=True),
        name=f"total_{axis}",
    )(x.reshape(block))
    return total.reshape(rows, columns)


def curvature_product(left, right):
    return jnp.dot(left, right, preferred_element_type=jnp.float32)


def cross_shard_total(left, right):
    return lax.dot_general(
        left, right, (((1,), (1,)), ((), ())), preferred_element_type=jnp.float32
    )


def summed_over_rows(left, right):
    return lax.dot_general(
        left, right, (((0,), (0,)), ((), ())), preferred_element_type=jnp.float32
    )


def second_order(
    gate_preactivation,
    up_preactivation,
    hidden_adjoint,
    gate_tangent_rows,
    up_tangent_rows,
    adjoint_tangent_rows,
):
    sigma = jax.nn.sigmoid(gate_preactivation)
    silu_value = gate_preactivation * sigma
    slope = sigma * (1.0 + gate_preactivation * (1.0 - sigma))
    bend = sigma * (1.0 - sigma) * (2.0 + gate_preactivation * (1.0 - 2.0 * sigma))
    hidden_activation = (silu_value * up_preactivation).astype(jnp.bfloat16)
    hidden_direction = (
        slope * gate_tangent_rows * up_preactivation + silu_value * up_tangent_rows
    ).astype(jnp.bfloat16)
    gate_derivative = (hidden_adjoint * up_preactivation * slope).astype(jnp.bfloat16)
    up_derivative = (hidden_adjoint * silu_value).astype(jnp.bfloat16)
    gate_derivative_direction = (
        adjoint_tangent_rows * up_preactivation * slope
        + hidden_adjoint * (up_tangent_rows * slope + up_preactivation * bend * gate_tangent_rows)
    ).astype(jnp.bfloat16)
    up_derivative_direction = (
        adjoint_tangent_rows * silu_value + hidden_adjoint * slope * gate_tangent_rows
    ).astype(jnp.bfloat16)
    return (
        hidden_activation,
        hidden_direction,
        gate_derivative,
        up_derivative,
        gate_derivative_direction,
        up_derivative_direction,
    )


def lora_kernel(
    lead,
    gap,
    tokens,
    gain,
    cot,
    gate_hbm,
    up_hbm,
    down_hbm,
    gate_in,
    gate_in_dir,
    up_in,
    up_in_dir,
    down_b,
    down_b_dir,
    gate_out,
    gate_out_dir,
    up_out,
    up_out_dir,
    down_in,
    down_in_dir,
    primal_out,
    dir_out,
    gate_curve_in_out,
    gate_curve_hbm,
    up_curve_in_out,
    up_curve_hbm,
    down_curve_hbm,
    down_curve_out_out,
    primal_ref,
    dir_ref,
    gate_curve_in,
    gate_curve,
    up_curve_in,
    up_curve,
    down_curve,
    down_curve_out,
    x_buf,
    cot_buf,
    squares,
    rank_part,
    rank_in,
    rank_all,
    inv_all,
    in_rows,
    out_rows,
    wide_buf,
    down_buf,
    own_parts,
    own_first,
    own_whole,
    rest_parts,
    rest_first,
    rest_mid_out,
    rest_mid_in,
    rest_whole,
    own_left,
    own_flip,
    rest_left,
    rest_flip,
    total,
    gate_q,
    up_q,
    low_q,
    pair_out,
    pair_in,
    pair_q_out,
    pair_q_in,
    line_out,
    line_in,
    line_q_out,
    line_q_in,
    last_out,
    last_in,
    last_q_out,
    last_q_in,
    q_all,
    factor_sem,
    wide_sem,
    down_sem,
    square_sem,
    rank_sem,
    far_send,
    far_recv,
    near_send,
    near_recv,
    rank_all_sem,
    inv_sem,
    own_send,
    own_recv,
    rest_send,
    rest_recv,
    pair_sem,
    line_sem,
    last_sem,
    q_sem,
    out_sem,
):
    row, me = lax.axis_index("row"), lax.axis_index("col")
    rows, columns = 4, 8
    z, core = me // 2, lax.rem(me, 2)
    partner = me + 1 - 2 * core
    flip_low = row + 1 - 2 * lax.rem(row, 2)
    flip_high = row + 2 - 4 * (row // 2)
    flip_both = 3 - row
    own, depth = tokens.shape
    chip = 2 * own
    count = 8 * own
    chunks = own_parts.shape[0]
    width = down_buf.shape[1]
    half = width // 2
    rank = gate_in.shape[0]
    slots, sides = wide_buf.shape[0], down_buf.shape[0]
    steps = 2 * chunks
    big = 4 * steps
    f32, bf16 = jnp.float32, jnp.bfloat16

    def remote(src, dst, send, recv, where):
        return pltpu.make_async_remote_copy(
            src_ref=src,
            dst_ref=dst,
            send_sem=send,
            recv_sem=recv,
            device_id=where,
            device_id_type=MESH,
        )

    def slot_rows(slot):
        return pl.ds(pl.multiple_of(slot * own, own), own)

    def lanes(c):
        return pl.ds(pl.multiple_of(c * width, width), width)

    def chunk_at(s):
        return (
            s - lead * ((s + big - lead) // big) - (chunks - lead) * ((s + big - lead - chunks) // big)
        )

    def loads(s):
        c, slot, side = chunk_at(s), lax.rem(s, slots), lax.rem(s, sides)
        return [
            pltpu.make_async_copy(
                gate_hbm.at[:, lanes(c)], wide_buf.at[slot, 0], wide_sem.at[slot, 0]
            ),
            pltpu.make_async_copy(
                up_hbm.at[:, lanes(c)], wide_buf.at[slot, 1], wide_sem.at[slot, 1]
            ),
            pltpu.make_async_copy(down_hbm.at[lanes(c), :], down_buf.at[side], down_sem.at[side]),
        ]

    barrier = pltpu.get_barrier_semaphore()

    def row_peer(k):
        return {"row": lax.rem(row + k, rows)}

    def col_peer(k):
        return {"col": lax.rem(me + k, columns)}

    @pl.loop(1, rows)
    def _(k):
        pl.semaphore_signal(barrier, inc=1, device_id=row_peer(k), device_id_type=MESH)

    @pl.loop(1, columns)
    def _(k):
        pl.semaphore_signal(barrier, inc=1, device_id=col_peer(k), device_id_type=MESH)

    factor_loads = []
    for index, (src, dst) in enumerate(
        [
            (down_b, in_rows.at[2, 0:rank]),
            (down_b_dir, in_rows.at[2, rank : 2 * rank]),
            (gate_in, in_rows.at[0, 0:rank]),
            (gate_in_dir, in_rows.at[0, rank : 2 * rank]),
            (up_in, in_rows.at[1, 0:rank]),
            (up_in_dir, in_rows.at[1, rank : 2 * rank]),
            (gate_out, out_rows.at[0, 0:rank]),
            (gate_out_dir, out_rows.at[0, rank : 2 * rank]),
            (up_out, out_rows.at[1, 0:rank]),
            (up_out_dir, out_rows.at[1, rank : 2 * rank]),
            (down_in, out_rows.at[2, 0:rank]),
            (down_in_dir, out_rows.at[2, rank : 2 * rank]),
        ]
    ):
        factor_loads.append(pltpu.make_async_copy(src, dst, factor_sem.at[index]))

    for copy in factor_loads[:6]:
        copy.start()
    for s in range(2):
        for copy in loads(s):
            copy.start()
    for copy in factor_loads[6:]:
        copy.start()

    values = tokens[...].astype(f32)
    squares[0] = jnp.broadcast_to(
        jnp.sum(values * values, axis=1, keepdims=True), squares.shape[1:]
    )
    cot_buf[slot_rows(core), :] = cot[...]
    x_buf[slot_rows(core), :] = (values * gain[...]).astype(bf16)
    line_in[...] = jnp.zeros_like(line_in)
    line_q_in[...] = jnp.zeros_like(line_q_in)
    pl.semaphore_wait(barrier, rows + columns - 2)

    def square(k):
        return remote(
            squares.at[0], squares.at[k], square_sem.at[0, k], square_sem.at[1, k], row_peer(k)
        )

    buffers = (cot_buf, x_buf)
    right, left = {"col": me + 2}, {"col": me - 2}

    def far(which, side, k):
        buffer = buffers[which]
        src = 2 * lax.rem(4 - k, 4) + core if side == 0 else 2 * k + core
        dst = 2 * (3 - k) + core if side == 0 else 2 * (k + 1) + core
        landing = 3 - k if side == 0 else k + 1
        return remote(
            buffer.at[slot_rows(src)],
            buffer.at[slot_rows(dst)],
            far_send.at[which, side, k],
            far_recv.at[which, landing],
            right if side == 0 else left,
        )

    def far_valid(side, k):
        if side == 0:
            return (z < 3) & (z >= k)
        return (z > 0) & (z + k <= 3)

    def far_arrival(which, slot):
        buffer = buffers[which]
        at = buffer.at[slot_rows(2 * slot + core)]
        return remote(at, at, far_send.at[which, 0, 0], far_recv.at[which, slot], {"col": partner})

    def near(which, slot):
        buffer = buffers[which]
        at = buffer.at[slot_rows(2 * slot + core)]
        return remote(
            at, at, near_send.at[which, slot], near_recv.at[which, slot], {"col": partner}
        )

    def near_arrival(which, slot):
        buffer = buffers[which]
        at = buffer.at[slot_rows(2 * slot + 1 - core)]
        return remote(
            at, at, near_send.at[which, slot], near_recv.at[which, slot], {"col": partner}
        )

    def launch(which):
        for side in range(2):

            @pl.when(far_valid(side, 0))
            def _(side=side):
                far(which, side, 0).start()

        near(which, 0).start()

    def pass_on(which, k):
        @pl.when(z >= k)
        def _():
            far_arrival(which, 4 - k).wait_recv()
            if k < 3:

                @pl.when(far_valid(0, k))
                def _():
                    far(which, 0, k).start()

            near(which, 4 - k).start()

        @pl.when(z + k <= 3)
        def _():
            far_arrival(which, k).wait_recv()
            if k < 3:

                @pl.when(far_valid(1, k))
                def _():
                    far(which, 1, k).start()

            near(which, k).start()

    launch(0)
    launch(1)
    for k in range(1, rows):
        square(k).start()
    for copy in factor_loads[:6]:
        copy.wait()
    rank_part[:, 4 * rank :] = cross_shard_total(cot[...], in_rows[2]).astype(bf16)
    own_x = x_buf[slot_rows(core), :]
    rank_part[:, : 2 * rank] = cross_shard_total(own_x, in_rows[0]).astype(bf16)
    rank_part[:, 2 * rank : 4 * rank] = cross_shard_total(own_x, in_rows[1]).astype(bf16)

    def rank_row(k):
        return remote(
            rank_part, rank_in.at[k], rank_sem.at[0, k], rank_sem.at[1, k], row_peer(k)
        )

    for k in range(1, rows):
        rank_row(k).start()

    def clear():
        total[...] = jnp.zeros_like(total)
        for ref in (gate_q, up_q, low_q, gate_curve, up_curve, down_curve):
            ref[...] = jnp.zeros_like(ref)

    def slot_there(k):
        there = lax.rem(me + k, columns) // 2
        return 2 * lax.rem(z - there + 4, 4) + core

    def slot_from(k):
        origin = lax.rem(me - k + columns, columns)
        return 2 * lax.rem(origin // 2 - z + 4, 4) + lax.rem(origin, 2)

    def spread(buffer, sem, k):
        return remote(
            buffer.at[slot_rows(core)],
            buffer.at[slot_rows(slot_there(k))],
            sem.at[0, k],
            sem.at[1, k],
            col_peer(k),
        )

    def spread_arrival(buffer, sem, k):
        at = buffer.at[slot_rows(slot_from(k))]
        return remote(at, at, sem.at[0, k], sem.at[1, k], col_peer(k))

    partner_step = 7 - 6 * core
    partner_ahead = 1 + 6 * core

    def share_ranks():
        sum_squares = squares[0]
        summed = rank_part[...].astype(f32)
        for k in range(1, rows):
            square(k).wait_recv()
            sum_squares = sum_squares + squares[k]
            rank_row(k).wait_recv()
            summed = summed + rank_in[k].astype(f32)
        inv = lax.rsqrt(sum_squares / (rows * depth) + epsilon)
        inv_all[slot_rows(core), :] = inv
        for index in range(3):
            at = slice(index * 2 * rank, (index + 1) * 2 * rank)
            block = summed[:, at]
            if index < 2:
                block = block * inv
            rank_all[slot_rows(core), at] = block.astype(bf16)

        spread(rank_all, rank_all_sem, partner_ahead).start()
        spread(inv_all, inv_sem, partner_ahead).start()

    def spread_ranks():
        @pl.loop(1, columns)
        def _(k):
            @pl.when(k != partner_ahead)
            def _():
                spread(rank_all, rank_all_sem, k).start()
                spread(inv_all, inv_sem, k).start()


    class Group:
        pass

    mine, others = Group(), Group()
    mine.first, mine.size = 0, chip
    mine.left, mine.flip = own_left, own_flip
    others.first, others.size = chip, count - chip
    others.left, others.flip = rest_left, rest_flip

    def prepare(g):
        low = rank_all[g.first : g.first + g.size, :].astype(f32)
        for index in range(3):
            block = low[:, index * 2 * rank : (index + 1) * 2 * rank] * adapter_scale
            lane = lax.broadcasted_iota(jnp.int32, block.shape, 1)
            turned = pltpu.roll(block, rank, 1)
            g.left[index, 0 : g.size, :] = jnp.where(lane < rank, block, 0.0).astype(bf16)
            g.left[index, g.size :, :] = turned.astype(bf16)
            g.flip[index] = turned.T.astype(bf16)

    friends = (flip_both, flip_low, flip_high)

    def own_sends(c, stage):
        return [
            remote(
                own_parts.at[c, peer] if stage == 0 else own_whole.at[c, row],
                own_first.at[c, index] if stage == 0 else own_whole.at[c, row],
                own_send.at[c, stage],
                own_recv.at[c, stage],
                {"row": peer},
            )
            for index, peer in enumerate(friends)
        ]

    def own_all(c, stage):
        return remote(
            own_first.at[c],
            own_first.at[c],
            own_send.at[c, stage],
            own_recv.at[c, stage],
            {"row": flip_both},
        )

    def ends(path):
        return (flip_low, flip_high) if path == 0 else (flip_high, flip_low)

    def send(src, dst, c, path, k, peer):
        away = rest_send.at[c, 1 if k in (2, 5) else 0]
        landed = rest_recv.at[c, 6] if k > 3 else rest_recv.at[c, 3 * path + max(k - 1, 0)]
        return remote(src, dst, away, landed, {"row": peer})

    def sends(c, path, ks):
        near_end, far_end = ends(path)
        table = [
            (rest_parts.at[c, path, near_end], rest_first.at[c, path, 0], near_end),
            (rest_parts.at[c, path, flip_both], rest_first.at[c, path, 1], near_end),
            (rest_mid_out.at[c, path], rest_mid_in.at[c, path], far_end),
            (rest_whole.at[c, path, row], rest_whole.at[c, path, row], far_end),
            (rest_whole.at[c, path, row], rest_whole.at[c, path, row], near_end),
            (rest_whole.at[c, path, far_end], rest_whole.at[c, path, far_end], near_end),
        ]
        return [send(table[k][0], table[k][1], c, path, k, table[k][2]) for k in ks]

    def landed_pair(c, path):
        at = rest_first.at[c, path]
        return remote(at, at, rest_send.at[c, 0], rest_recv.at[c, 3 * path], {"row": flip_low})

    def landed_one(c, path, k):
        at = rest_mid_in.at[c, path]
        return remote(
            at, at, rest_send.at[c, 0], rest_recv.at[c, 3 * path + k - 1], {"row": flip_low}
        )

    def landed_four(c):
        at = rest_first.at[c]
        return remote(at, at, rest_send.at[c, 1], rest_recv.at[c, 6], {"row": flip_low})

    def sent_eight(c):
        at = rest_parts.at[c]
        return remote(at, at, rest_send.at[c, 0], rest_recv.at[c, 6], {"row": flip_low})

    def project(g, c, s):
        for copy in loads(s):
            copy.wait()

        @pl.when(s + 2 < steps)
        def _():
            for copy in loads(s + 2):
                copy.start()

        slot = lax.rem(s, slots)
        span = slice(g.first, g.first + g.size)
        quarter = g.size // 4

        def put(at, value):
            for start in range(0, width, half):
                piece = value[:, start : start + half].reshape(4, quarter, half)
                lane = at * width + start
                if g is mine:
                    own_parts[c, :, :, lane : lane + half] = piece
                else:
                    path, lane = lane // (3 * half), lane % (3 * half)
                    rest_parts[c, path, :, :, lane : lane + half] = piece

        put(0, curvature_product(x_buf[span, :], wide_buf[slot, 0]).astype(bf16))
        put(1, curvature_product(x_buf[span, :], wide_buf[slot, 1]).astype(bf16))
        if g is others:
            for copy in sends(c, 0, (0, 1)):
                copy.start()
        put(2, cross_shard_total(cot_buf[span, :], down_buf[lax.rem(s, sides)]).astype(bf16))
        for copy in own_sends(c, 0) if g is mine else sends(c, 1, (0, 1)):
            copy.start()

    def reduce(g, c, s):
        own_all(c, 0).wait_recv()
        summed = own_parts[c, row].astype(f32)
        for index in range(3):
            summed = summed + own_first[c, index].astype(f32)
        own_whole[c, row] = summed.astype(bf16)
        for copy in own_sends(c, 1):
            copy.start()

    def relay(g, c, s):
        for path in range(2):
            near_end, far_end = ends(path)
            landed_pair(c, path).wait_recv()
            rest_mid_out[c, path] = (
                rest_parts[c, path, far_end].astype(f32) + rest_first[c, path, 1].astype(f32)
            ).astype(bf16)
            sends(c, path, (2,))[0].start()

    def settle(g, c, s):
        for path in range(2):
            landed_one(c, path, 2).wait_recv()
            rest_whole[c, path, row] = (
                rest_parts[c, path, row].astype(f32)
                + rest_first[c, path, 0].astype(f32)
                + rest_mid_in[c, path].astype(f32)
            ).astype(bf16)
            for copy in sends(c, path, (3, 4)):
                copy.start()

    def forward(g, c, s):
        for path in range(2):
            landed_one(c, path, 3).wait_recv()
            sends(c, path, (5,))[0].start()

    def differentiate(g, c, s):
        if g is mine:
            own_all(c, 1).wait_recv()
        else:
            landed_four(c).wait_recv()
        size = g.size

        def got(at):
            pieces = []
            for start in range(0, width, half):
                lane = at * width + start
                if g is mine:
                    piece = own_whole[c, :, :, lane : lane + half]
                else:
                    path, lane = lane // (3 * half), lane % (3 * half)
                    piece = rest_whole[c, path, :, :, lane : lane + half]
                piece = piece.reshape(size, half).astype(f32)
                if at < 2:
                    piece = piece * inv_all[g.first : g.first + size, :]
                pieces.append(piece)
            return jnp.concatenate(pieces, axis=1)

        gate_w, up_w, down_w = out_rows[0, :, lanes(c)], out_rows[1, :, lanes(c)], out_rows[2, :, lanes(c)]
        gate_low = curvature_product(g.left[0], gate_w)
        up_low = curvature_product(g.left[1], up_w)
        adj_low = curvature_product(g.left[2], down_w)
        hidden, hidden_dir, d_gate, d_up, d_gate_dir, d_up_dir = second_order(
            got(0) + gate_low[:size],
            got(1) + up_low[:size],
            got(2) + adj_low[:size],
            gate_low[size:],
            up_low[size:],
            adj_low[size:],
        )
        gate_d = jnp.concatenate([d_gate, d_gate_dir], axis=0)
        up_d = jnp.concatenate([d_up, d_up_dir], axis=0)
        hidden_d = jnp.concatenate([hidden_dir, hidden], axis=0)
        span = slice(g.first, g.first + size)
        gate_curve[:, lanes(c)] += curvature_product(
            g.flip[0, :rank], d_gate
        ) + curvature_product(g.flip[0, rank:], d_gate_dir)
        up_curve[:, lanes(c)] += curvature_product(g.flip[1, :rank], d_up) + curvature_product(
            g.flip[1, rank:], d_up_dir
        )
        down_curve[:, lanes(c)] += curvature_product(
            g.flip[2, rank:], hidden_dir
        ) + curvature_product(g.flip[2, :rank], hidden)
        for ref, value, weight in (
            (gate_q, gate_d, gate_w),
            (up_q, up_d, up_w),
            (low_q, hidden_d, down_w),
        ):
            product = cross_shard_total(value, weight)
            ref[0, span, :] += product[:size]
            ref[1, span, :] += product[size:]
        slot = lax.rem(s, slots)
        piece = 512 if depth % 512 == 0 else depth
        for start in range(0, depth, piece):
            at = slice(start, start + piece)
            product = cross_shard_total(gate_d, wide_buf[slot, 0, at, :]) + cross_shard_total(
                up_d, wide_buf[slot, 1, at, :]
            )
            total[0, span, at] += product[:size]
            total[1, span, at] += product[size:]

    def q_rows(slot):
        at = slot_rows(slot)
        lane = lax.broadcasted_iota(jnp.int32, (own, 2 * rank), 1)
        low_half = lane < rank
        gate = gate_q[0, at, :] + jnp.where(low_half, 0.0, pltpu.roll(gate_q[1, at, :], rank, 1))
        up = up_q[0, at, :] + jnp.where(low_half, 0.0, pltpu.roll(up_q[1, at, :], rank, 1))
        low = jnp.where(low_half, low_q[0, at, :] + pltpu.roll(low_q[1, at, :], rank, 1), 0.0)
        return jnp.concatenate([gate, up, low], axis=1)

    def pair(src, dst, at):
        return remote(src, dst, pair_sem.at[0, at], pair_sem.at[1, at], {"col": partner})

    def pairs():
        return [pair(pair_out, pair_in, 0), pair(pair_q_out, pair_q_in, 1)]

    def exchange():
        for k in range(1, 4):
            slot = 2 * k + 1 - core
            for kind in range(2):
                pair_out[k - 1, kind] = total[kind, slot_rows(slot), :].astype(bf16)
            pair_q_out[k - 1] = q_rows(slot).astype(bf16)
        for copy in pairs():
            copy.start()

    def line(side, k, kind):
        out = k - 1 if side == 0 else 3 - k
        src = line_out.at[out, kind] if kind < 2 else line_q_out.at[out]
        dst = line_in.at[side, k - 1, kind] if kind < 2 else line_q_in.at[side, k - 1]
        return remote(
            src,
            dst,
            line_sem.at[0, side, k - 1, kind],
            line_sem.at[1, side, k - 1, kind],
            right if side == 0 else left,
        )

    def line_arrival(side, k, kind):
        at = line_in.at[side, k, kind] if kind < 2 else line_q_in.at[side, k]
        return remote(
            at,
            at,
            line_sem.at[0, side, k, kind],
            line_sem.at[1, side, k, kind],
            {"col": partner},
        )

    def line_valid(side, k):
        return z + k <= 3 if side == 0 else z - k >= 0

    def line_fed(side):
        return z >= 1 if side == 0 else z <= 2

    def line_send(side, k, kinds):
        at = k if side == 0 else 4 - k
        slot = 2 * at + core
        for kind in kinds:
            if kind < 2:
                value = total[kind, slot_rows(slot), :] + pair_in[at - 1, kind].astype(f32)
                if k < 3:
                    value = value + line_in[side, k, kind].astype(f32)
                line_out[at - 1, kind] = value.astype(bf16)
            else:
                value = q_rows(slot) + pair_q_in[at - 1].astype(f32)
                if k < 3:
                    value = value + line_q_in[side, k].astype(f32)
                line_q_out[at - 1] = value.astype(bf16)
            line(side, k, kind).start()

    def line_open():
        for copy in pairs():
            copy.wait_recv()
        for side in range(2):
            for k in (3, 2, 1):

                @pl.when(line_valid(side, k) & ((z == 0) if side == 0 else (z == 3)))
                def _(side=side, k=k):
                    line_send(side, k, (2, 0, 1))

    def line_stage(k, kinds):
        for side in range(2):

            @pl.when(line_valid(side, k) & line_fed(side))
            def _(side=side):
                for kind in kinds:
                    line_arrival(side, k, kind).wait_recv()
                line_send(side, k, kinds)

    def line_end(kinds):
        for side in range(2):

            @pl.when(line_fed(side))
            def _(side=side):
                for kind in kinds:
                    line_arrival(side, 0, kind).wait_recv()

    turn = lead + chunks
    resume = turn + gap
    own_lags = (0, 2, 4)
    rest_lags = (0, 1, 2, 3, 4)
    rest_end = turn - 1 + rest_lags[4]
    late = {
        rest_end: exchange,
        rest_end + 1: line_open,
        rest_end + 4: functools.partial(line_stage, 2, (2, 0)),
        rest_end + 5: functools.partial(line_stage, 2, (1,)),
        rest_end + 6: functools.partial(line_stage, 1, (2, 0)),
        rest_end + 8: functools.partial(line_stage, 1, (1,)),
    }
    relays = [(0, 1), (1, 1), (0, 2), (1, 2), (0, 3), (1, 3)]
    relay_at = [1, 3, 4, 5, 6, lead - 1]
    early = sum(step < lead for step in relay_at)

    def share():
        share_ranks()
        clear()

    def arrive():
        for which, k in relays[early:]:
            pass_on(which, k)
        for which in range(2):
            for k in range(1, 4):
                near_arrival(which, k).wait_recv()

    def first_ready():
        for copy in factor_loads[6:]:
            copy.wait()
        spread_arrival(rank_all, rank_all_sem, partner_step).wait_recv()
        spread_arrival(inv_all, inv_sem, partner_step).wait_recv()
        prepare(mine)

    def rest_ready():
        @pl.loop(1, columns)
        def _(k):
            @pl.when(k != partner_step)
            def _():
                spread_arrival(rank_all, rank_all_sem, k).wait_recv()
                spread_arrival(inv_all, inv_sem, k).wait_recv()

        prepare(others)

    for which in range(2):
        near_arrival(which, 0).wait_recv()

    last_step = steps + gap + own_lags[2]

    @pl.loop(0, last_step)
    def _(t):
        def at_step(step, action):
            @pl.when(t == step)
            def _():
                action()

        def own_stage(lag, stage):
            u = t - lag
            after = (u + big - resume) // big
            s = u - gap * after

            @pl.when(((u >= 0) & (u < lead)) | ((u >= resume) & (u < steps + gap)))
            def _():
                stage(mine, s - chunks * after, s)

        def rest_stage(lag, stage):
            s = t - lag

            @pl.when((s >= lead) & (s < turn))
            def _():
                stage(others, s - lead, s)

        at_step(lead, arrive)
        at_step(own_lags[2], first_ready)
        at_step(lead + 1, spread_ranks)
        at_step(lead + rest_lags[4], rest_ready)
        for lag, stage in zip(rest_lags, (project, relay, settle, forward, differentiate)):
            rest_stage(lag, stage)
        for step, action in late.items():
            if step < last_step:
                at_step(step, action)
        own_stage(0, project)
        at_step(2, share)
        own_stage(own_lags[1], reduce)
        own_stage(own_lags[2], differentiate)
        for index, (which, k) in enumerate(relays[:early]):
            at_step(relay_at[index], functools.partial(pass_on, which, k))

    for step, action in late.items():
        if step >= last_step:
            action()

    def outputs(index):
        src, dst = (
            (primal_ref, primal_out),
            (dir_ref, dir_out),
            (gate_curve_in, gate_curve_in_out),
            (gate_curve, gate_curve_hbm),
            (up_curve_in, up_curve_in_out),
            (up_curve, up_curve_hbm),
            (down_curve, down_curve_hbm),
            (down_curve_out, down_curve_out_out),
        )[index]
        return pltpu.make_async_copy(src, dst, out_sem.at[index])

    def lasts():
        return [
            remote(last_out, last_in, last_sem.at[0, 0], last_sem.at[1, 0], {"col": partner}),
            remote(last_q_out, last_q_in, last_sem.at[0, 1], last_sem.at[1, 1], {"col": partner}),
        ]

    last_feature, last_q = lasts()
    last_q_out[...] = q_rows(1 - core).astype(bf16)
    last_q.start()
    for kind in range(2):
        last_out[kind] = total[kind, slot_rows(1 - core), :].astype(bf16)
    last_feature.start()
    for index in (3, 5, 6):
        outputs(index).start()

    @pl.loop(0, chunks)
    def _(c):
        own_all(c, 0).wait_send()
        own_all(c, 1).wait_send()
        sent_eight(c).wait_send()
        landed_four(c).wait_send()

    line_end((2,))
    last_q.wait_recv()
    q_own = (
        q_rows(core)
        + last_q_in[...].astype(f32)
        + line_q_in[0, 0].astype(f32)
        + line_q_in[1, 0].astype(f32)
    )
    lane = lax.broadcasted_iota(jnp.int32, (own, 2 * rank), 1)
    both = jnp.where(
        lane < rank, pltpu.roll(q_own[:, : 2 * rank], rank, 1), q_own[:, 2 * rank : 4 * rank]
    )
    q_all[slot_rows(core), : 2 * rank] = (
        both * inv_all[slot_rows(core), :] * adapter_scale
    ).astype(bf16)
    q_all[slot_rows(core), 2 * rank :] = (q_own[:, 4 * rank :] * adapter_scale).astype(bf16)

    @pl.loop(1, columns)
    def _(k):
        spread(q_all, q_sem, k).start()

    line_end((0, 1))
    last_feature.wait_recv()
    feature = [
        total[kind, slot_rows(core), :]
        + last_in[kind].astype(f32)
        + line_in[0, 0, kind].astype(f32)
        + line_in[1, 0, kind].astype(f32)
        for kind in range(2)
    ]
    for index in range(2):
        block = q_own[:, index * 2 * rank : (index + 1) * 2 * rank] * adapter_scale
        straight = jnp.where(lane < rank, block, 0.0).astype(bf16)
        turned = pltpu.roll(block, rank, 1).astype(bf16)
        feature[0] = feature[0] + curvature_product(straight, in_rows[index])
        feature[1] = feature[1] + curvature_product(turned, in_rows[index])
    primal_ref[...] = feature[0]
    dir_ref[...] = feature[1]
    for index in (0, 1):
        outputs(index).start()

    @pl.loop(1, columns)
    def _(k):
        spread_arrival(q_all, q_sem, k).wait_recv()

    every = q_all[...].astype(f32)
    both_t = every[:, : 2 * rank].T.astype(bf16)
    low_t = every[:, 2 * rank :].T.astype(bf16)
    down_curve_out[...] = curvature_product(low_t[:rank], cot_buf[...])
    outputs(7).start()
    product = curvature_product(both_t, x_buf[...])
    gate_curve_in[...] = product[:rank]
    up_curve_in[...] = product[rank:]
    for index in (2, 4):
        outputs(index).start()

    for k in range(1, rows):
        square(k).wait_send()
        rank_row(k).wait_send()
    for which in range(2):
        for side in range(2):
            for k in range(3):

                @pl.when(far_valid(side, k))
                def _(which=which, side=side, k=k):
                    far(which, side, k).wait_send()

        for k in range(4):
            near(which, k).wait_send()

    @pl.loop(1, columns)
    def _(k):
        spread(rank_all, rank_all_sem, k).wait_send()
        spread(inv_all, inv_sem, k).wait_send()
        spread(q_all, q_sem, k).wait_send()

    for copy in pairs() + [last_feature, last_q]:
        copy.wait_send()
    for side in range(2):
        for k in range(1, 4):

            @pl.when(line_valid(side, k))
            def _(side=side, k=k):
                for kind in range(3):
                    line(side, k, kind).wait_send()

    for index in range(8):
        outputs(index).wait()


def handover_kernel(*refs):
    sources, targets, held, sem = refs[:8], refs[8:16], refs[16:24], refs[24]
    fetch = [
        pltpu.make_async_copy(sources[i], held[i], sem.at[0, i]) for i in range(len(sources))
    ]
    place = [
        pltpu.make_async_copy(held[i], targets[i], sem.at[1, i]) for i in range(len(sources))
    ]
    for copy in fetch:
        copy.start()
    for arrive, leave in zip(fetch, place):
        arrive.wait()
        leave.start()
    for copy in place:
        copy.wait()


def fused(
    tokens,
    norm_gain,
    cotangent,
    gate_frozen_weight,
    up_frozen_weight,
    down_frozen_weight,
    gate_input_factor,
    gate_output_factor,
    up_input_factor,
    up_output_factor,
    down_input_factor,
    down_b,
    gate_input_factor_direction,
    gate_output_factor_direction,
    up_input_factor_direction,
    up_output_factor_direction,
    down_input_factor_direction,
    down_b_dir,
    width,
):
    own, depth = tokens.shape
    hidden = gate_frozen_weight.shape[1]
    rank = gate_output_factor.shape[0]
    chunks = hidden // width
    chip, rest, count = 2 * own, 6 * own, 8 * own
    lead, gap = (8 * chunks) // 14, 3
    half_panel = 3 * width // 2
    f32, bf16 = jnp.float32, jnp.bfloat16
    vmem = pl.BlockSpec(memory_space=pltpu.VMEM)
    anywhere = pl.BlockSpec(memory_space=pl.ANY)

    def reduce_buffers(size):
        quarter = size // 4
        return [
            pltpu.VMEM((chunks, 2, 4, quarter, half_panel), bf16),
            pltpu.VMEM((chunks, 2, 2, quarter, half_panel), bf16),
            pltpu.VMEM((chunks, 2, quarter, half_panel), bf16),
            pltpu.VMEM((chunks, 2, quarter, half_panel), bf16),
            pltpu.VMEM((chunks, 2, 4, quarter, half_panel), bf16),
        ]

    dma = pltpu.SemaphoreType.DMA
    slots, sides = 7, 3
    shapes = [
        jax.ShapeDtypeStruct((own, depth), f32),
        jax.ShapeDtypeStruct((own, depth), f32),
        jax.ShapeDtypeStruct((rank, depth), f32),
        jax.ShapeDtypeStruct((rank, hidden), f32),
        jax.ShapeDtypeStruct((rank, depth), f32),
        jax.ShapeDtypeStruct((rank, hidden), f32),
        jax.ShapeDtypeStruct((rank, hidden), f32),
        jax.ShapeDtypeStruct((rank, depth), f32),
    ]
    results = pl.pallas_call(
        functools.partial(lora_kernel, lead, gap),
        out_shape=shapes,
        in_specs=[vmem] * 3 + [anywhere] * 15,
        out_specs=[anywhere] * 8,
        scratch_shapes=[pltpu.VMEM(shape.shape, f32) for shape in shapes]
        + [
            pltpu.VMEM((count, depth), bf16),
            pltpu.VMEM((count, depth), bf16),
            pltpu.VMEM((4, own, 2 * rank), f32),
            pltpu.VMEM((own, 6 * rank), bf16),
            pltpu.VMEM((4, own, 6 * rank), bf16),
            pltpu.VMEM((count, 6 * rank), bf16),
            pltpu.VMEM((count, 2 * rank), f32),
            pltpu.VMEM((3, 2 * rank, depth), bf16),
            pltpu.VMEM((3, 2 * rank, hidden), bf16),
            pltpu.VMEM((slots, 2, depth, width), bf16),
            pltpu.VMEM((sides, width, depth), bf16),
        ]
        + [
            pltpu.VMEM((chunks, 4, chip // 4, 3 * width), bf16),
            pltpu.VMEM((chunks, 3, chip // 4, 3 * width), bf16),
            pltpu.VMEM((chunks, 4, chip // 4, 3 * width), bf16),
        ]
        + reduce_buffers(rest)
        + [
            pltpu.VMEM((3, 2 * chip, 2 * rank), bf16),
            pltpu.VMEM((3, 2 * rank, chip), bf16),
            pltpu.VMEM((3, 2 * rest, 2 * rank), bf16),
            pltpu.VMEM((3, 2 * rank, rest), bf16),
            pltpu.VMEM((2, count, depth), f32),
            pltpu.VMEM((2, count, 2 * rank), f32),
            pltpu.VMEM((2, count, 2 * rank), f32),
            pltpu.VMEM((2, count, 2 * rank), f32),
            pltpu.VMEM((3, 2, own, depth), bf16),
            pltpu.VMEM((3, 2, own, depth), bf16),
            pltpu.VMEM((3, own, 6 * rank), bf16),
            pltpu.VMEM((3, own, 6 * rank), bf16),
            pltpu.VMEM((3, 2, own, depth), bf16),
            pltpu.VMEM((2, 3, 2, own, depth), bf16),
            pltpu.VMEM((3, own, 6 * rank), bf16),
            pltpu.VMEM((2, 3, own, 6 * rank), bf16),
            pltpu.VMEM((2, own, depth), bf16),
            pltpu.VMEM((2, own, depth), bf16),
            pltpu.VMEM((own, 6 * rank), bf16),
            pltpu.VMEM((own, 6 * rank), bf16),
            pltpu.VMEM((count, 4 * rank), bf16),
            dma((12,)),
            dma((slots, 2)),
            dma((sides,)),
            dma((2, 4)),
            dma((2, 4)),
            dma((2, 2, 3)),
            dma((2, 4)),
            dma((2, 4)),
            dma((2, 4)),
            dma((2, 8)),
            dma((2, 8)),
            dma((chunks, 2)),
            dma((chunks, 2)),
            dma((chunks, 2)),
            dma((chunks, 7)),
            dma((2, 2)),
            dma((2, 2, 3, 3)),
            dma((2, 2)),
            dma((2, 8)),
            dma((8,)),
        ],
        compiler_params=pltpu.CompilerParams(
            collective_id=2, has_side_effects=True, vmem_limit_bytes=63 * 1024 * 1024
        ),
        name="lora",
    )(
        tokens,
        norm_gain.reshape(1, depth),
        cotangent,
        gate_frozen_weight,
        up_frozen_weight,
        down_frozen_weight,
        gate_input_factor.T,
        gate_input_factor_direction.T,
        up_input_factor.T,
        up_input_factor_direction.T,
        down_b,
        down_b_dir,
        gate_output_factor,
        gate_output_factor_direction,
        up_output_factor,
        up_output_factor_direction,
        down_input_factor.T,
        down_input_factor_direction.T,
    )
    primal, direction, gate_input, gate_output, up_input, up_output, down_input, down_output = (
        pl.pallas_call(
            handover_kernel,
            out_shape=shapes,
            in_specs=[anywhere] * 8,
            out_specs=[anywhere] * 8,
            scratch_shapes=[pltpu.VMEM(shape.shape, f32) for shape in shapes] + [dma((2, 8))],
            name="handover",
        )(*results)
    )
    return (
        primal,
        direction,
        gate_input.T,
        gate_output,
        up_input.T,
        up_output,
        down_input.T,
        down_output,
    )


def gather_kernel(
    tokens,
    gain,
    cot,
    x_all,
    cot_all,
    x_buf,
    cot_buf,
    squares,
    square_send,
    square_recv,
    far_send,
    far_recv,
    near_send,
    near_recv,
):
    rows, columns = lax.axis_size("row"), lax.axis_size("col")
    chips = columns // 2
    my_row, me = lax.axis_index("row"), lax.axis_index("col")
    partner = me + 1 - 2 * lax.rem(me, 2)
    features = rows * tokens.shape[1]
    barrier = pltpu.get_barrier_semaphore()

    def row_peer(k):
        return {"row": lax.rem(my_row + k, rows)}

    def far_peer(k):
        return {"col": lax.rem(me + 2 * k, columns)}

    @pl.loop(1, rows)
    def _(k):
        pl.semaphore_signal(barrier, inc=1, device_id=row_peer(k), device_id_type=MESH)

    @pl.loop(1, chips)
    def _(k):
        pl.semaphore_signal(barrier, inc=1, device_id=far_peer(k), device_id_type=MESH)

    pl.semaphore_signal(barrier, inc=1, device_id={"col": partner}, device_id_type=MESH)

    buffers = (cot_buf, x_buf)

    def origin(k):
        return lax.rem(me - 2 * k + columns, columns)

    def square(k):
        return pltpu.make_async_remote_copy(
            src_ref=squares.at[0],
            dst_ref=squares.at[k],
            send_sem=square_send.at[k],
            recv_sem=square_recv.at[k],
            device_id=row_peer(k),
            device_id_type=MESH,
        )

    def far(which, k, slot):
        return pltpu.make_async_remote_copy(
            src_ref=buffers[which].at[slot],
            dst_ref=buffers[which].at[slot],
            send_sem=far_send.at[which, k],
            recv_sem=far_recv.at[which, k],
            device_id=far_peer(k),
            device_id_type=MESH,
        )

    def near(which, k, slot):
        return pltpu.make_async_remote_copy(
            src_ref=buffers[which].at[slot],
            dst_ref=buffers[which].at[slot],
            send_sem=near_send.at[which, k],
            recv_sem=near_recv.at[which, k],
            device_id={"col": partner},
            device_id_type=MESH,
        )

    def launch(which):
        @pl.loop(1, chips)
        def _(k):
            far(which, k, me).start()

        near(which, 0, me).start()

    values = tokens[...].astype(jnp.float32)
    squares[0] = jnp.broadcast_to(
        jnp.sum(values * values, axis=1, keepdims=True), squares.shape[1:]
    )
    cot_buf[me] = cot[...]
    pl.semaphore_wait(barrier, rows + chips - 1)

    @pl.loop(1, rows)
    def _(k):
        square(k).start()

    launch(0)

    def add(k, total):
        square(k).wait_recv()
        return total + squares[k]

    total = lax.fori_loop(1, rows, add, squares[0])
    scale = lax.rsqrt(total[:, :1] / features + epsilon)
    x_buf[me] = (tokens[...].astype(jnp.float32) * scale * gain[...]).astype(jnp.bfloat16)
    launch(1)
    for which in range(2):

        @pl.loop(1, chips)
        def _(k, which=which):
            far(which, k, origin(k)).wait_recv()
            near(which, k, origin(k)).start()

    for which in range(2):

        @pl.loop(0, chips)
        def _(k, which=which):
            near(which, k, lax.rem(partner - 2 * k + columns, columns)).wait_recv()

    @pl.loop(1, rows)
    def _(k):
        square(k).wait_send()

    for which in range(2):

        @pl.loop(1, chips)
        def _(k, which=which):
            far(which, k, me).wait_send()

        @pl.loop(0, chips)
        def _(k, which=which):
            near(which, k, origin(k)).wait_send()

    cot_all[...] = cot_buf[...]
    x_all[...] = x_buf[...]


def gathered(tokens, gain, cot):
    rows, columns = lax.axis_size("row"), lax.axis_size("col")
    own, depth = tokens.shape
    whole = (columns, own, depth)
    vmem = pl.BlockSpec(memory_space=pltpu.VMEM)
    x, panel = pl.pallas_call(
        gather_kernel,
        out_shape=[jax.ShapeDtypeStruct(whole, jnp.bfloat16)] * 2,
        in_specs=[vmem] * 3,
        out_specs=[vmem] * 2,
        scratch_shapes=[
            pltpu.VMEM(whole, jnp.bfloat16),
            pltpu.VMEM(whole, jnp.bfloat16),
            pltpu.VMEM((rows, own, 128), jnp.float32),
            pltpu.SemaphoreType.DMA((rows,)),
            pltpu.SemaphoreType.DMA((rows,)),
            pltpu.SemaphoreType.DMA((2, columns // 2)),
            pltpu.SemaphoreType.DMA((2, columns // 2)),
            pltpu.SemaphoreType.DMA((2, columns // 2)),
            pltpu.SemaphoreType.DMA((2, columns // 2)),
        ],
        compiler_params=pltpu.CompilerParams(collective_id=3, has_side_effects=True),
        name="gather",
    )(tokens, gain.reshape(1, depth), cot)
    return x.reshape(columns * own, depth), panel.reshape(columns * own, depth)


def chunk_count(width):
    for count in (4, 2):
        if width % (128 * count) == 0:
            return count
    return 1


def on_device(
    tokens,
    norm_gain,
    cotangent,
    gate_frozen_weight,
    up_frozen_weight,
    down_frozen_weight,
    gate_input_factor,
    gate_output_factor,
    up_input_factor,
    up_output_factor,
    down_input_factor,
    down_b,
    gate_input_factor_direction,
    gate_output_factor_direction,
    up_input_factor_direction,
    up_output_factor_direction,
    down_input_factor_direction,
    down_b_dir,
):
    width = 256
    if (
        lax.axis_size("row") == 4
        and lax.axis_size("col") == 8
        and gate_frozen_weight.shape[1] % (14 * width) == 0
        and gate_frozen_weight.shape[0] % 128 == 0
        and gate_input_factor.shape[1] == 64
        and tokens.shape[0] % 32 == 0
    ):
        return fused(
            tokens,
            norm_gain,
            cotangent,
            gate_frozen_weight,
            up_frozen_weight,
            down_frozen_weight,
            gate_input_factor,
            gate_output_factor,
            up_input_factor,
            up_output_factor,
            down_input_factor,
            down_b,
            gate_input_factor_direction,
            gate_output_factor_direction,
            up_input_factor_direction,
            up_output_factor_direction,
            down_input_factor_direction,
            down_b_dir,
            width,
        )
    rank = gate_input_factor.shape[1]
    width_rows, width_columns = gate_frozen_weight.shape
    own_count = tokens.shape[0]
    normed_tokens, cot_panel = gathered(tokens, norm_gain, cotangent)
    count = normed_tokens.shape[0]
    in_factors = jnp.concatenate(
        [
            gate_input_factor,
            up_input_factor,
            gate_input_factor_direction,
            up_input_factor_direction,
        ],
        axis=1,
    )
    out_factors = jnp.concatenate([down_b, down_b_dir], axis=0)

    projected = jnp.concatenate(
        [curvature_product(normed_tokens, in_factors), cross_shard_total(cot_panel, out_factors)],
        axis=1,
    )
    ranks = shard_total(projected, "row", 0)
    gate_out = jnp.concatenate([gate_output_factor, gate_output_factor_direction], axis=0)
    up_out = jnp.concatenate([up_output_factor, up_output_factor_direction], axis=0)
    down_in = jnp.concatenate([down_input_factor, down_input_factor_direction], axis=1)

    chunks = chunk_count(width_columns)
    wide = width_columns // chunks
    spans = [slice(index * wide, (index + 1) * wide) for index in range(chunks)]

    summed_chunks = []
    for span in spans:
        partial = (
            curvature_product(normed_tokens, gate_frozen_weight[:, span]).astype(jnp.bfloat16),
            curvature_product(normed_tokens, up_frozen_weight[:, span]).astype(jnp.bfloat16),
            cross_shard_total(cot_panel, down_frozen_weight[span]).astype(jnp.bfloat16),
        )
        if summed_chunks:
            partial, summed_chunks[-1] = lax.optimization_barrier((partial, summed_chunks[-1]))
        summed_chunks.append(lax.psum(partial, "row"))

    gate_low, up_low, gate_low_dir, up_low_dir, adj_low, adj_low_dir = [
        ranks[:, index * rank : (index + 1) * rank] for index in range(6)
    ]
    gate_pair = jnp.concatenate([gate_low_dir, gate_low], axis=1)
    up_pair = jnp.concatenate([up_low_dir, up_low], axis=1)
    adj_pair = jnp.concatenate([adj_low_dir, adj_low], axis=1)
    gate_stack = jnp.concatenate([gate_low_dir, gate_low], axis=0)
    up_stack = jnp.concatenate([up_low_dir, up_low], axis=0)
    adj_stack = jnp.concatenate([adj_low, adj_low_dir], axis=0)
    feature = 0.0
    gate_q = 0.0
    up_q = 0.0
    low_dir = 0.0
    gate_output, up_output, down_input = [], [], []
    for span, total in zip(spans, summed_chunks):
        gate_sum, up_sum, adj_sum = [value.astype(jnp.float32) for value in total]
        gate_pre = gate_sum + adapter_scale * curvature_product(
            gate_low, gate_output_factor[:, span]
        )
        up_pre = up_sum + adapter_scale * curvature_product(
            up_low, up_output_factor[:, span]
        )
        hidden_adj = adj_sum + adapter_scale * cross_shard_total(
            adj_low, down_input_factor[span]
        )
        gate_tan = adapter_scale * curvature_product(gate_pair, gate_out[:, span])
        up_tan = adapter_scale * curvature_product(up_pair, up_out[:, span])
        adj_tan = adapter_scale * cross_shard_total(adj_pair, down_in[span])
        hidden, hidden_dir, d_gate, d_up, d_gate_dir, d_up_dir = second_order(
            gate_pre, up_pre, hidden_adj, gate_tan, up_tan, adj_tan
        )
        gate_d = jnp.concatenate([d_gate, d_gate_dir], axis=0)
        up_d = jnp.concatenate([d_up, d_up_dir], axis=0)
        hidden_d = jnp.concatenate([hidden_dir, hidden], axis=0)
        gate_output.append(adapter_scale * summed_over_rows(gate_stack, gate_d))
        up_output.append(adapter_scale * summed_over_rows(up_stack, up_d))
        down_input.append(adapter_scale * summed_over_rows(hidden_d, adj_stack))
        gate_q = gate_q + cross_shard_total(gate_d, gate_out[:, span])
        up_q = up_q + cross_shard_total(up_d, up_out[:, span])
        low_dir = (
            low_dir
            + curvature_product(hidden_dir, down_input_factor[span])
            + curvature_product(hidden, down_input_factor_direction[span])
        )
        feature = (
            feature
            + cross_shard_total(gate_d, gate_frozen_weight[:, span])
            + cross_shard_total(up_d, up_frozen_weight[:, span])
        )
    gate_output = jnp.concatenate(gate_output, axis=1)
    up_output = jnp.concatenate(up_output, axis=1)
    down_input = jnp.concatenate(down_input, axis=0)

    summed = lax.psum_scatter(
        feature.astype(jnp.bfloat16).reshape(2, count, width_rows),
        "col",
        scatter_dimension=1,
        tiled=True,
    ).astype(jnp.float32)
    adjoints = shard_total(
        jnp.concatenate(
            [
                gate_q[:count, :rank],
                up_q[:count, :rank],
                gate_q[count:, :rank] + gate_q[:count, rank:],
                up_q[count:, :rank] + up_q[:count, rank:],
                low_dir,
            ],
            axis=1,
        ).astype(jnp.bfloat16),
        "col",
        1,
    )
    piece = lax.dynamic_slice_in_dim(adjoints, lax.axis_index("col") * own_count, own_count, 0)
    normed_feature_adjoint = summed[0] + adapter_scale * cross_shard_total(
        piece[:, : 2 * rank], in_factors[:, : 2 * rank]
    )
    normed_feature_adjoint_direction = summed[1] + adapter_scale * cross_shard_total(
        jnp.concatenate([piece[:, 2 * rank : 4 * rank], piece[:, : 2 * rank]], axis=1), in_factors
    )
    gate_input = adapter_scale * summed_over_rows(
        normed_tokens, adjoints[:, 2 * rank : 3 * rank]
    )
    up_input = adapter_scale * summed_over_rows(normed_tokens, adjoints[:, 3 * rank : 4 * rank])
    down_output = adapter_scale * summed_over_rows(adjoints[:, 4 * rank :], cot_panel)
    return (
        normed_feature_adjoint,
        normed_feature_adjoint_direction,
        gate_input,
        gate_output,
        up_input,
        up_output,
        down_input,
        down_output,
    )


def solution(mesh):
    in_specs = (
        P("col", "row"),
        P("row"),
        P("col", "row"),
        P("row", "col"),
        P("row", "col"),
        P("col", "row"),
        P("row", None),
        P(None, "col"),
        P("row", None),
        P(None, "col"),
        P("col", None),
        P(None, "row"),
        P("row", None),
        P(None, "col"),
        P("row", None),
        P(None, "col"),
        P("col", None),
        P(None, "row"),
    )
    out_specs = (
        P("col", "row"),
        P("col", "row"),
        P("row", None),
        P(None, "col"),
        P("row", None),
        P(None, "col"),
        P("col", None),
        P(None, "row"),
    )
    return jax.shard_map(
        on_device, mesh=mesh, in_specs=in_specs, out_specs=out_specs, check_vma=False
    )
```

```python
import functools

import jax
import jax.numpy as jnp
from jax import lax
from jax.experimental import pallas as pl
from jax.experimental.pallas import tpu as pltpu
from jax.sharding import PartitionSpec as P

adapter_scale = 0.5
epsilon = 1e-05
MESH = pl.DeviceIdType.MESH


def total_kernel(axis, n, x_ref, o_ref, inbox, whole, send1, recv1, send2, recv2):
    me = lax.axis_index(axis)
    barrier = pltpu.get_barrier_semaphore()

    @pl.loop(1, n)
    def _(k):
        pl.semaphore_signal(
            barrier, inc=1, device_id={axis: lax.rem(me + k, n)}, device_id_type=MESH
        )

    pl.semaphore_wait(barrier, n - 1)

    def scatter(k):
        peer = lax.rem(me + k, n)
        return pltpu.make_async_remote_copy(
            src_ref=x_ref.at[peer],
            dst_ref=inbox.at[k],
            send_sem=send1.at[k],
            recv_sem=recv1.at[k],
            device_id={axis: peer},
            device_id_type=MESH,
        )

    def spread(k):
        peer = lax.rem(me + k, n)
        return pltpu.make_async_remote_copy(
            src_ref=whole.at[me],
            dst_ref=whole.at[me],
            send_sem=send2.at[k],
            recv_sem=recv2.at[k],
            device_id={axis: peer},
            device_id_type=MESH,
        )

    def arrival(k):
        origin = lax.rem(me - k + n, n)
        return pltpu.make_async_remote_copy(
            src_ref=whole.at[origin],
            dst_ref=whole.at[origin],
            send_sem=send2.at[k],
            recv_sem=recv2.at[k],
            device_id={axis: origin},
            device_id_type=MESH,
        )

    @pl.loop(1, n)
    def _(k):
        scatter(k).start()

    def add(k, total):
        scatter(k).wait_recv()
        return total + inbox[k].astype(jnp.float32)

    total = lax.fori_loop(1, n, add, x_ref[me].astype(jnp.float32))
    whole[me] = total.astype(whole.dtype)

    @pl.loop(1, n)
    def _(k):
        spread(k).start()

    @pl.loop(1, n)
    def _(k):
        arrival(k).wait_recv()

    @pl.loop(1, n)
    def _(k):
        scatter(k).wait_send()
        spread(k).wait_send()

    o_ref[...] = whole[...]


def shard_total(x, axis, collective_id):
    n = lax.axis_size(axis)
    rows, columns = x.shape
    block = (n, rows // n, columns)
    total = pl.pallas_call(
        functools.partial(total_kernel, axis, n),
        out_shape=jax.ShapeDtypeStruct(block, jnp.bfloat16),
        in_specs=[pl.BlockSpec(memory_space=pltpu.VMEM)],
        out_specs=pl.BlockSpec(memory_space=pltpu.VMEM),
        scratch_shapes=[
            pltpu.VMEM(block, x.dtype),
            pltpu.VMEM(block, jnp.bfloat16),
            pltpu.SemaphoreType.DMA((n,)),
            pltpu.SemaphoreType.DMA((n,)),
            pltpu.SemaphoreType.DMA((n,)),
            pltpu.SemaphoreType.DMA((n,)),
        ],
        compiler_params=pltpu.CompilerParams(collective_id=collective_id, has_side_effects=True),
        name=f"total_{axis}",
    )(x.reshape(block))
    return total.reshape(rows, columns)


def curvature_product(left, right):
    return jnp.dot(left, right, preferred_element_type=jnp.float32)


def cross_shard_total(left, right):
    return lax.dot_general(
        left, right, (((1,), (1,)), ((), ())), preferred_element_type=jnp.float32
    )


def summed_over_rows(left, right):
    return lax.dot_general(
        left, right, (((0,), (0,)), ((), ())), preferred_element_type=jnp.float32
    )


def second_order(
    gate_preactivation,
    up_preactivation,
    hidden_adjoint,
    gate_tangent_rows,
    up_tangent_rows,
    adjoint_tangent_rows,
):
    sigma = jax.nn.sigmoid(gate_preactivation)
    silu_value = gate_preactivation * sigma
    slope = sigma * (1.0 + gate_preactivation * (1.0 - sigma))
    bend = sigma * (1.0 - sigma) * (2.0 + gate_preactivation * (1.0 - 2.0 * sigma))
    hidden_activation = (silu_value * up_preactivation).astype(jnp.bfloat16)
    hidden_direction = (
        slope * gate_tangent_rows * up_preactivation + silu_value * up_tangent_rows
    ).astype(jnp.bfloat16)
    gate_derivative = (hidden_adjoint * up_preactivation * slope).astype(jnp.bfloat16)
    up_derivative = (hidden_adjoint * silu_value).astype(jnp.bfloat16)
    gate_derivative_direction = (
        adjoint_tangent_rows * up_preactivation * slope
        + hidden_adjoint * (up_tangent_rows * slope + up_preactivation * bend * gate_tangent_rows)
    ).astype(jnp.bfloat16)
    up_derivative_direction = (
        adjoint_tangent_rows * silu_value + hidden_adjoint * slope * gate_tangent_rows
    ).astype(jnp.bfloat16)
    return (
        hidden_activation,
        hidden_direction,
        gate_derivative,
        up_derivative,
        gate_derivative_direction,
        up_derivative_direction,
    )


def lora_kernel(
    lead,
    gap,
    tokens,
    gain,
    cot,
    gate_hbm,
    up_hbm,
    down_hbm,
    gate_in,
    gate_in_dir,
    up_in,
    up_in_dir,
    down_b,
    down_b_dir,
    gate_out,
    gate_out_dir,
    up_out,
    up_out_dir,
    down_in,
    down_in_dir,
    primal_out,
    dir_out,
    gate_curve_in_out,
    gate_curve_hbm,
    up_curve_in_out,
    up_curve_hbm,
    down_curve_hbm,
    down_curve_out_out,
    primal_ref,
    dir_ref,
    gate_curve_in,
    gate_curve,
    up_curve_in,
    up_curve,
    down_curve,
    down_curve_out,
    x_buf,
    cot_buf,
    squares,
    rank_part,
    rank_in,
    rank_all,
    inv_all,
    in_rows,
    out_rows,
    wide_buf,
    down_buf,
    own_parts,
    own_first,
    own_whole,
    rest_parts,
    rest_first,
    rest_mid_out,
    rest_mid_in,
    rest_whole,
    own_left,
    own_flip,
    rest_left,
    rest_flip,
    total,
    gate_q,
    up_q,
    low_q,
    pair_out,
    pair_in,
    pair_q_out,
    pair_q_in,
    line_out,
    line_in,
    line_q_out,
    line_q_in,
    last_out,
    last_in,
    last_q_out,
    last_q_in,
    q_all,
    factor_sem,
    wide_sem,
    down_sem,
    square_sem,
    rank_sem,
    far_send,
    far_recv,
    near_send,
    near_recv,
    rank_all_sem,
    inv_sem,
    own_send,
    own_recv,
    rest_send,
    rest_recv,
    pair_sem,
    line_sem,
    last_sem,
    q_sem,
    out_sem,
):
    row, me = lax.axis_index("row"), lax.axis_index("col")
    rows, columns = 4, 8
    z, core = me // 2, lax.rem(me, 2)
    partner = me + 1 - 2 * core
    flip_low = row + 1 - 2 * lax.rem(row, 2)
    flip_high = row + 2 - 4 * (row // 2)
    flip_both = 3 - row
    own, depth = tokens.shape
    chip = 2 * own
    count = 8 * own
    chunks = own_parts.shape[0]
    width = down_buf.shape[1]
    half = width // 2
    rank = gate_in.shape[0]
    slots, sides = wide_buf.shape[0], down_buf.shape[0]
    steps = 2 * chunks
    big = 4 * steps
    f32, bf16 = jnp.float32, jnp.bfloat16

    def remote(src, dst, send, recv, where):
        return pltpu.make_async_remote_copy(
            src_ref=src,
            dst_ref=dst,
            send_sem=send,
            recv_sem=recv,
            device_id=where,
            device_id_type=MESH,
        )

    def slot_rows(slot):
        return pl.ds(pl.multiple_of(slot * own, own), own)

    def lanes(c):
        return pl.ds(pl.multiple_of(c * width, width), width)

    def chunk_at(s):
        return (
            s - lead * ((s + big - lead) // big) - (chunks - lead) * ((s + big - lead - chunks) // big)
        )

    def loads(s):
        c, slot, side = chunk_at(s), lax.rem(s, slots), lax.rem(s, sides)
        return [
            pltpu.make_async_copy(
                gate_hbm.at[:, lanes(c)], wide_buf.at[slot, 0], wide_sem.at[slot, 0]
            ),
            pltpu.make_async_copy(
                up_hbm.at[:, lanes(c)], wide_buf.at[slot, 1], wide_sem.at[slot, 1]
            ),
            pltpu.make_async_copy(down_hbm.at[lanes(c), :], down_buf.at[side], down_sem.at[side]),
        ]

    barrier = pltpu.get_barrier_semaphore()

    def row_peer(k):
        return {"row": lax.rem(row + k, rows)}

    def col_peer(k):
        return {"col": lax.rem(me + k, columns)}

    @pl.loop(1, rows)
    def _(k):
        pl.semaphore_signal(barrier, inc=1, device_id=row_peer(k), device_id_type=MESH)

    @pl.loop(1, columns)
    def _(k):
        pl.semaphore_signal(barrier, inc=1, device_id=col_peer(k), device_id_type=MESH)

    factor_loads = []
    for index, (src, dst) in enumerate(
        [
            (down_b, in_rows.at[2, 0:rank]),
            (down_b_dir, in_rows.at[2, rank : 2 * rank]),
            (gate_in, in_rows.at[0, 0:rank]),
            (gate_in_dir, in_rows.at[0, rank : 2 * rank]),
            (up_in, in_rows.at[1, 0:rank]),
            (up_in_dir, in_rows.at[1, rank : 2 * rank]),
            (gate_out, out_rows.at[0, 0:rank]),
            (gate_out_dir, out_rows.at[0, rank : 2 * rank]),
            (up_out, out_rows.at[1, 0:rank]),
            (up_out_dir, out_rows.at[1, rank : 2 * rank]),
            (down_in, out_rows.at[2, 0:rank]),
            (down_in_dir, out_rows.at[2, rank : 2 * rank]),
        ]
    ):
        factor_loads.append(pltpu.make_async_copy(src, dst, factor_sem.at[index]))

    for copy in factor_loads[:6]:
        copy.start()
    for s in range(2):
        for copy in loads(s):
            copy.start()
    for copy in factor_loads[6:]:
        copy.start()

    values = tokens[...].astype(f32)
    squares[0] = jnp.broadcast_to(
        jnp.sum(values * values, axis=1, keepdims=True), squares.shape[1:]
    )
    cot_buf[slot_rows(core), :] = cot[...]
    x_buf[slot_rows(core), :] = (values * gain[...]).astype(bf16)
    line_in[...] = jnp.zeros_like(line_in)
    line_q_in[...] = jnp.zeros_like(line_q_in)
    pl.semaphore_wait(barrier, rows + columns - 2)

    def square(k):
        return remote(
            squares.at[0], squares.at[k], square_sem.at[0, k], square_sem.at[1, k], row_peer(k)
        )

    buffers = (cot_buf, x_buf)
    right, left = {"col": me + 2}, {"col": me - 2}

    def far(which, side, k):
        buffer = buffers[which]
        src = 2 * lax.rem(4 - k, 4) + core if side == 0 else 2 * k + core
        dst = 2 * (3 - k) + core if side == 0 else 2 * (k + 1) + core
        landing = 3 - k if side == 0 else k + 1
        return remote(
            buffer.at[slot_rows(src)],
            buffer.at[slot_rows(dst)],
            far_send.at[which, side, k],
            far_recv.at[which, landing],
            right if side == 0 else left,
        )

    def far_valid(side, k):
        if side == 0:
            return (z < 3) & (z >= k)
        return (z > 0) & (z + k <= 3)

    def far_arrival(which, slot):
        buffer = buffers[which]
        at = buffer.at[slot_rows(2 * slot + core)]
        return remote(at, at, far_send.at[which, 0, 0], far_recv.at[which, slot], {"col": partner})

    def near(which, slot):
        buffer = buffers[which]
        at = buffer.at[slot_rows(2 * slot + core)]
        return remote(
            at, at, near_send.at[which, slot], near_recv.at[which, slot], {"col": partner}
        )

    def near_arrival(which, slot):
        buffer = buffers[which]
        at = buffer.at[slot_rows(2 * slot + 1 - core)]
        return remote(
            at, at, near_send.at[which, slot], near_recv.at[which, slot], {"col": partner}
        )

    def launch(which):
        for side in range(2):

            @pl.when(far_valid(side, 0))
            def _(side=side):
                far(which, side, 0).start()

        near(which, 0).start()

    def pass_on(which, k):
        @pl.when(z >= k)
        def _():
            far_arrival(which, 4 - k).wait_recv()
            if k < 3:

                @pl.when(far_valid(0, k))
                def _():
                    far(which, 0, k).start()

            near(which, 4 - k).start()

        @pl.when(z + k <= 3)
        def _():
            far_arrival(which, k).wait_recv()
            if k < 3:

                @pl.when(far_valid(1, k))
                def _():
                    far(which, 1, k).start()

            near(which, k).start()

    launch(0)
    launch(1)
    for k in range(1, rows):
        square(k).start()
    for copy in factor_loads[:6]:
        copy.wait()
    rank_part[:, 4 * rank :] = cross_shard_total(cot[...], in_rows[2]).astype(bf16)
    own_x = x_buf[slot_rows(core), :]
    rank_part[:, : 2 * rank] = cross_shard_total(own_x, in_rows[0]).astype(bf16)
    rank_part[:, 2 * rank : 4 * rank] = cross_shard_total(own_x, in_rows[1]).astype(bf16)

    def rank_row(k):
        return remote(
            rank_part, rank_in.at[k], rank_sem.at[0, k], rank_sem.at[1, k], row_peer(k)
        )

    for k in range(1, rows):
        rank_row(k).start()

    def clear():
        total[...] = jnp.zeros_like(total)
        for ref in (gate_q, up_q, low_q, gate_curve, up_curve, down_curve):
            ref[...] = jnp.zeros_like(ref)

    def slot_there(k):
        there = lax.rem(me + k, columns) // 2
        return 2 * lax.rem(z - there + 4, 4) + core

    def slot_from(k):
        origin = lax.rem(me - k + columns, columns)
        return 2 * lax.rem(origin // 2 - z + 4, 4) + lax.rem(origin, 2)

    def spread(buffer, sem, k):
        return remote(
            buffer.at[slot_rows(core)],
            buffer.at[slot_rows(slot_there(k))],
            sem.at[0, k],
            sem.at[1, k],
            col_peer(k),
        )

    def spread_arrival(buffer, sem, k):
        at = buffer.at[slot_rows(slot_from(k))]
        return remote(at, at, sem.at[0, k], sem.at[1, k], col_peer(k))

    partner_step = 7 - 6 * core
    partner_ahead = 1 + 6 * core

    def share_ranks():
        sum_squares = squares[0]
        summed = rank_part[...].astype(f32)
        for k in range(1, rows):
            square(k).wait_recv()
            sum_squares = sum_squares + squares[k]
            rank_row(k).wait_recv()
            summed = summed + rank_in[k].astype(f32)
        inv = lax.rsqrt(sum_squares / (rows * depth) + epsilon)
        inv_all[slot_rows(core), :] = inv
        for index in range(3):
            at = slice(index * 2 * rank, (index + 1) * 2 * rank)
            block = summed[:, at]
            if index < 2:
                block = block * inv
            rank_all[slot_rows(core), at] = block.astype(bf16)

        spread(rank_all, rank_all_sem, partner_ahead).start()
        spread(inv_all, inv_sem, partner_ahead).start()

    def spread_ranks():
        @pl.loop(1, columns)
        def _(k):
            @pl.when(k != partner_ahead)
            def _():
                spread(rank_all, rank_all_sem, k).start()
                spread(inv_all, inv_sem, k).start()


    class Group:
        pass

    mine, others = Group(), Group()
    mine.first, mine.size = 0, chip
    mine.left, mine.flip = own_left, own_flip
    others.first, others.size = chip, count - chip
    others.left, others.flip = rest_left, rest_flip

    def prepare(g):
        low = rank_all[g.first : g.first + g.size, :].astype(f32)
        for index in range(3):
            block = low[:, index * 2 * rank : (index + 1) * 2 * rank] * adapter_scale
            lane = lax.broadcasted_iota(jnp.int32, block.shape, 1)
            turned = pltpu.roll(block, rank, 1)
            g.left[index, 0 : g.size, :] = jnp.where(lane < rank, block, 0.0).astype(bf16)
            g.left[index, g.size :, :] = turned.astype(bf16)
            g.flip[index] = turned.T.astype(bf16)

    friends = (flip_both, flip_low, flip_high)

    def own_sends(c, stage):
        return [
            remote(
                own_parts.at[c, peer] if stage == 0 else own_whole.at[c, row],
                own_first.at[c, index] if stage == 0 else own_whole.at[c, row],
                own_send.at[c, stage],
                own_recv.at[c, stage],
                {"row": peer},
            )
            for index, peer in enumerate(friends)
        ]

    def own_all(c, stage):
        return remote(
            own_first.at[c],
            own_first.at[c],
            own_send.at[c, stage],
            own_recv.at[c, stage],
            {"row": flip_both},
        )

    def ends(path):
        return (flip_low, flip_high) if path == 0 else (flip_high, flip_low)

    def send(src, dst, c, path, k, peer):
        away = rest_send.at[c, 1 if k in (2, 5) else 0]
        landed = rest_recv.at[c, 6] if k > 3 else rest_recv.at[c, 3 * path + max(k - 1, 0)]
        return remote(src, dst, away, landed, {"row": peer})

    def sends(c, path, ks):
        near_end, far_end = ends(path)
        table = [
            (rest_parts.at[c, path, near_end], rest_first.at[c, path, 0], near_end),
            (rest_parts.at[c, path, flip_both], rest_first.at[c, path, 1], near_end),
            (rest_mid_out.at[c, path], rest_mid_in.at[c, path], far_end),
            (rest_whole.at[c, path, row], rest_whole.at[c, path, row], far_end),
            (rest_whole.at[c, path, row], rest_whole.at[c, path, row], near_end),
            (rest_whole.at[c, path, far_end], rest_whole.at[c, path, far_end], near_end),
        ]
        return [send(table[k][0], table[k][1], c, path, k, table[k][2]) for k in ks]

    def landed_pair(c, path):
        at = rest_first.at[c, path]
        return remote(at, at, rest_send.at[c, 0], rest_recv.at[c, 3 * path], {"row": flip_low})

    def landed_one(c, path, k):
        at = rest_mid_in.at[c, path]
        return remote(
            at, at, rest_send.at[c, 0], rest_recv.at[c, 3 * path + k - 1], {"row": flip_low}
        )

    def landed_four(c):
        at = rest_first.at[c]
        return remote(at, at, rest_send.at[c, 1], rest_recv.at[c, 6], {"row": flip_low})

    def sent_eight(c):
        at = rest_parts.at[c]
        return remote(at, at, rest_send.at[c, 0], rest_recv.at[c, 6], {"row": flip_low})

    def project(g, c, s):
        for copy in loads(s):
            copy.wait()

        @pl.when(s + 2 < steps)
        def _():
            for copy in loads(s + 2):
                copy.start()

        slot = lax.rem(s, slots)
        span = slice(g.first, g.first + g.size)
        quarter = g.size // 4

        def put(at, value):
            for start in range(0, width, half):
                piece = value[:, start : start + half].reshape(4, quarter, half)
                lane = at * width + start
                if g is mine:
                    own_parts[c, :, :, lane : lane + half] = piece
                else:
                    path, lane = lane // (3 * half), lane % (3 * half)
                    rest_parts[c, path, :, :, lane : lane + half] = piece

        put(0, curvature_product(x_buf[span, :], wide_buf[slot, 0]).astype(bf16))
        put(1, curvature_product(x_buf[span, :], wide_buf[slot, 1]).astype(bf16))
        if g is others:
            for copy in sends(c, 0, (0, 1)):
                copy.start()
        put(2, cross_shard_total(cot_buf[span, :], down_buf[lax.rem(s, sides)]).astype(bf16))
        for copy in own_sends(c, 0) if g is mine else sends(c, 1, (0, 1)):
            copy.start()

    def reduce(g, c, s):
        own_all(c, 0).wait_recv()
        summed = own_parts[c, row].astype(f32)
        for index in range(3):
            summed = summed + own_first[c, index].astype(f32)
        own_whole[c, row] = summed.astype(bf16)
        for copy in own_sends(c, 1):
            copy.start()

    def relay(g, c, s):
        for path in range(2):
            near_end, far_end = ends(path)
            landed_pair(c, path).wait_recv()
            rest_mid_out[c, path] = (
                rest_parts[c, path, far_end].astype(f32) + rest_first[c, path, 1].astype(f32)
            ).astype(bf16)
            sends(c, path, (2,))[0].start()

    def settle(g, c, s):
        for path in range(2):
            landed_one(c, path, 2).wait_recv()
            rest_whole[c, path, row] = (
                rest_parts[c, path, row].astype(f32)
                + rest_first[c, path, 0].astype(f32)
                + rest_mid_in[c, path].astype(f32)
            ).astype(bf16)
            for copy in sends(c, path, (3, 4)):
                copy.start()

    def forward(g, c, s):
        for path in range(2):
            landed_one(c, path, 3).wait_recv()
            sends(c, path, (5,))[0].start()

    def differentiate(g, c, s):
        if g is mine:
            own_all(c, 1).wait_recv()
        else:
            landed_four(c).wait_recv()
        size = g.size

        def got(at):
            pieces = []
            for start in range(0, width, half):
                lane = at * width + start
                if g is mine:
                    piece = own_whole[c, :, :, lane : lane + half]
                else:
                    path, lane = lane // (3 * half), lane % (3 * half)
                    piece = rest_whole[c, path, :, :, lane : lane + half]
                piece = piece.reshape(size, half).astype(f32)
                if at < 2:
                    piece = piece * inv_all[g.first : g.first + size, :]
                pieces.append(piece)
            return jnp.concatenate(pieces, axis=1)

        gate_w, up_w, down_w = out_rows[0, :, lanes(c)], out_rows[1, :, lanes(c)], out_rows[2, :, lanes(c)]
        gate_low = curvature_product(g.left[0], gate_w)
        up_low = curvature_product(g.left[1], up_w)
        adj_low = curvature_product(g.left[2], down_w)
        hidden, hidden_dir, d_gate, d_up, d_gate_dir, d_up_dir = second_order(
            got(0) + gate_low[:size],
            got(1) + up_low[:size],
            got(2) + adj_low[:size],
            gate_low[size:],
            up_low[size:],
            adj_low[size:],
        )
        gate_d = jnp.concatenate([d_gate, d_gate_dir], axis=0)
        up_d = jnp.concatenate([d_up, d_up_dir], axis=0)
        hidden_d = jnp.concatenate([hidden_dir, hidden], axis=0)
        span = slice(g.first, g.first + size)
        gate_curve[:, lanes(c)] += curvature_product(
            g.flip[0, :rank], d_gate
        ) + curvature_product(g.flip[0, rank:], d_gate_dir)
        up_curve[:, lanes(c)] += curvature_product(g.flip[1, :rank], d_up) + curvature_product(
            g.flip[1, rank:], d_up_dir
        )
        down_curve[:, lanes(c)] += curvature_product(
            g.flip[2, rank:], hidden_dir
        ) + curvature_product(g.flip[2, :rank], hidden)
        for ref, value, weight in (
            (gate_q, gate_d, gate_w),
            (up_q, up_d, up_w),
            (low_q, hidden_d, down_w),
        ):
            product = cross_shard_total(value, weight)
            ref[0, span, :] += product[:size]
            ref[1, span, :] += product[size:]
        slot = lax.rem(s, slots)
        piece = 512 if depth % 512 == 0 else depth
        for start in range(0, depth, piece):
            at = slice(start, start + piece)
            product = cross_shard_total(gate_d, wide_buf[slot, 0, at, :]) + cross_shard_total(
                up_d, wide_buf[slot, 1, at, :]
            )
            total[0, span, at] += product[:size]
            total[1, span, at] += product[size:]

    def q_rows(slot):
        at = slot_rows(slot)
        lane = lax.broadcasted_iota(jnp.int32, (own, 2 * rank), 1)
        low_half = lane < rank
        gate = gate_q[0, at, :] + jnp.where(low_half, 0.0, pltpu.roll(gate_q[1, at, :], rank, 1))
        up = up_q[0, at, :] + jnp.where(low_half, 0.0, pltpu.roll(up_q[1, at, :], rank, 1))
        low = jnp.where(low_half, low_q[0, at, :] + pltpu.roll(low_q[1, at, :], rank, 1), 0.0)
        return jnp.concatenate([gate, up, low], axis=1)

    def pair(src, dst, at):
        return remote(src, dst, pair_sem.at[0, at], pair_sem.at[1, at], {"col": partner})

    def pairs():
        return [pair(pair_out, pair_in, 0), pair(pair_q_out, pair_q_in, 1)]

    def exchange():
        for k in range(1, 4):
            slot = 2 * k + 1 - core
            for kind in range(2):
                pair_out[k - 1, kind] = total[kind, slot_rows(slot), :].astype(bf16)
            pair_q_out[k - 1] = q_rows(slot).astype(bf16)
        for copy in pairs():
            copy.start()

    def line(side, k, kind):
        out = k - 1 if side == 0 else 3 - k
        src = line_out.at[out, kind] if kind < 2 else line_q_out.at[out]
        dst = line_in.at[side, k - 1, kind] if kind < 2 else line_q_in.at[side, k - 1]
        return remote(
            src,
            dst,
            line_sem.at[0, side, k - 1, kind],
            line_sem.at[1, side, k - 1, kind],
            right if side == 0 else left,
        )

    def line_arrival(side, k, kind):
        at = line_in.at[side, k, kind] if kind < 2 else line_q_in.at[side, k]
        return remote(
            at,
            at,
            line_sem.at[0, side, k, kind],
            line_sem.at[1, side, k, kind],
            {"col": partner},
        )

    def line_valid(side, k):
        return z + k <= 3 if side == 0 else z - k >= 0

    def line_fed(side):
        return z >= 1 if side == 0 else z <= 2

    def line_send(side, k, kinds):
        at = k if side == 0 else 4 - k
        slot = 2 * at + core
        for kind in kinds:
            if kind < 2:
                value = total[kind, slot_rows(slot), :] + pair_in[at - 1, kind].astype(f32)
                if k < 3:
                    value = value + line_in[side, k, kind].astype(f32)
                line_out[at - 1, kind] = value.astype(bf16)
            else:
                value = q_rows(slot) + pair_q_in[at - 1].astype(f32)
                if k < 3:
                    value = value + line_q_in[side, k].astype(f32)
                line_q_out[at - 1] = value.astype(bf16)
            line(side, k, kind).start()

    def line_open():
        for copy in pairs():
            copy.wait_recv()
        for side in range(2):
            for k in (3, 2, 1):

                @pl.when(line_valid(side, k) & ((z == 0) if side == 0 else (z == 3)))
                def _(side=side, k=k):
                    line_send(side, k, (2, 0, 1))

    def line_stage(k, kinds):
        for side in range(2):

            @pl.when(line_valid(side, k) & line_fed(side))
            def _(side=side):
                for kind in kinds:
                    line_arrival(side, k, kind).wait_recv()
                line_send(side, k, kinds)

    def line_end(kinds):
        for side in range(2):

            @pl.when(line_fed(side))
            def _(side=side):
                for kind in kinds:
                    line_arrival(side, 0, kind).wait_recv()

    turn = lead + chunks
    resume = turn + gap
    own_lags = (0, 2, 4)
    rest_lags = (0, 1, 2, 3, 4)
    rest_end = turn - 1 + rest_lags[4]
    late = {
        rest_end: exchange,
        rest_end + 1: line_open,
        rest_end + 4: functools.partial(line_stage, 2, (2, 0)),
        rest_end + 5: functools.partial(line_stage, 2, (1,)),
        rest_end + 6: functools.partial(line_stage, 1, (2, 0)),
        rest_end + 8: functools.partial(line_stage, 1, (1,)),
    }
    relays = [(0, 1), (1, 1), (0, 2), (1, 2), (0, 3), (1, 3)]
    relay_at = [2, 3, 4, 5, 6, lead - 1]
    early = sum(step < lead for step in relay_at)

    def share():
        share_ranks()
        clear()

    def arrive():
        for which, k in relays[early:]:
            pass_on(which, k)
        for which in range(2):
            for k in range(1, 4):
                near_arrival(which, k).wait_recv()

    def first_ready():
        for copy in factor_loads[6:]:
            copy.wait()
        spread_arrival(rank_all, rank_all_sem, partner_step).wait_recv()
        spread_arrival(inv_all, inv_sem, partner_step).wait_recv()
        prepare(mine)

    def rest_ready():
        @pl.loop(1, columns)
        def _(k):
            @pl.when(k != partner_step)
            def _():
                spread_arrival(rank_all, rank_all_sem, k).wait_recv()
                spread_arrival(inv_all, inv_sem, k).wait_recv()

        prepare(others)

    for which in range(2):
        near_arrival(which, 0).wait_recv()

    last_step = steps + gap + own_lags[2]

    @pl.loop(0, last_step)
    def _(t):
        def at_step(step, action):
            @pl.when(t == step)
            def _():
                action()

        def own_stage(lag, stage):
            u = t - lag
            after = (u + big - resume) // big
            s = u - gap * after

            @pl.when(((u >= 0) & (u < lead)) | ((u >= resume) & (u < steps + gap)))
            def _():
                stage(mine, s - chunks * after, s)

        def rest_stage(lag, stage):
            s = t - lag

            @pl.when((s >= lead) & (s < turn))
            def _():
                stage(others, s - lead, s)

        at_step(lead, arrive)
        at_step(own_lags[2], first_ready)
        at_step(lead + 1, spread_ranks)
        at_step(lead + rest_lags[4], rest_ready)
        for lag, stage in zip(rest_lags, (project, relay, settle, forward, differentiate)):
            rest_stage(lag, stage)
        for step, action in late.items():
            if step < last_step:
                at_step(step, action)
        own_stage(0, project)
        at_step(2, share)
        own_stage(own_lags[1], reduce)
        own_stage(own_lags[2], differentiate)
        for index, (which, k) in enumerate(relays[:early]):
            at_step(relay_at[index], functools.partial(pass_on, which, k))

    for step, action in late.items():
        if step >= last_step:
            action()

    def outputs(index):
        src, dst = (
            (primal_ref, primal_out),
            (dir_ref, dir_out),
            (gate_curve_in, gate_curve_in_out),
            (gate_curve, gate_curve_hbm),
            (up_curve_in, up_curve_in_out),
            (up_curve, up_curve_hbm),
            (down_curve, down_curve_hbm),
            (down_curve_out, down_curve_out_out),
        )[index]
        return pltpu.make_async_copy(src, dst, out_sem.at[index])

    def lasts():
        return [
            remote(last_out, last_in, last_sem.at[0, 0], last_sem.at[1, 0], {"col": partner}),
            remote(last_q_out, last_q_in, last_sem.at[0, 1], last_sem.at[1, 1], {"col": partner}),
        ]

    last_feature, last_q = lasts()
    last_q_out[...] = q_rows(1 - core).astype(bf16)
    last_q.start()
    for kind in range(2):
        last_out[kind] = total[kind, slot_rows(1 - core), :].astype(bf16)
    last_feature.start()
    for index in (3, 5, 6):
        outputs(index).start()

    @pl.loop(0, chunks)
    def _(c):
        own_all(c, 0).wait_send()
        own_all(c, 1).wait_send()
        sent_eight(c).wait_send()
        landed_four(c).wait_send()

    line_end((2,))
    last_q.wait_recv()
    q_own = (
        q_rows(core)
        + last_q_in[...].astype(f32)
        + line_q_in[0, 0].astype(f32)
        + line_q_in[1, 0].astype(f32)
    )
    lane = lax.broadcasted_iota(jnp.int32, (own, 2 * rank), 1)
    both = jnp.where(
        lane < rank, pltpu.roll(q_own[:, : 2 * rank], rank, 1), q_own[:, 2 * rank : 4 * rank]
    )
    q_all[slot_rows(core), : 2 * rank] = (
        both * inv_all[slot_rows(core), :] * adapter_scale
    ).astype(bf16)
    q_all[slot_rows(core), 2 * rank :] = (q_own[:, 4 * rank :] * adapter_scale).astype(bf16)

    @pl.loop(1, columns)
    def _(k):
        spread(q_all, q_sem, k).start()

    line_end((0, 1))
    last_feature.wait_recv()
    feature = [
        total[kind, slot_rows(core), :]
        + last_in[kind].astype(f32)
        + line_in[0, 0, kind].astype(f32)
        + line_in[1, 0, kind].astype(f32)
        for kind in range(2)
    ]
    for index in range(2):
        block = q_own[:, index * 2 * rank : (index + 1) * 2 * rank] * adapter_scale
        straight = jnp.where(lane < rank, block, 0.0).astype(bf16)
        turned = pltpu.roll(block, rank, 1).astype(bf16)
        feature[0] = feature[0] + curvature_product(straight, in_rows[index])
        feature[1] = feature[1] + curvature_product(turned, in_rows[index])
    primal_ref[...] = feature[0]
    dir_ref[...] = feature[1]
    for index in (0, 1):
        outputs(index).start()

    @pl.loop(1, columns)
    def _(k):
        spread_arrival(q_all, q_sem, k).wait_recv()

    every = q_all[...].astype(f32)
    both_t = every[:, : 2 * rank].T.astype(bf16)
    low_t = every[:, 2 * rank :].T.astype(bf16)
    down_curve_out[...] = curvature_product(low_t[:rank], cot_buf[...])
    outputs(7).start()
    product = curvature_product(both_t, x_buf[...])
    gate_curve_in[...] = product[:rank]
    up_curve_in[...] = product[rank:]
    for index in (2, 4):
        outputs(index).start()

    for k in range(1, rows):
        square(k).wait_send()
        rank_row(k).wait_send()
    for which in range(2):
        for side in range(2):
            for k in range(3):

                @pl.when(far_valid(side, k))
                def _(which=which, side=side, k=k):
                    far(which, side, k).wait_send()

        for k in range(4):
            near(which, k).wait_send()

    @pl.loop(1, columns)
    def _(k):
        spread(rank_all, rank_all_sem, k).wait_send()
        spread(inv_all, inv_sem, k).wait_send()
        spread(q_all, q_sem, k).wait_send()

    for copy in pairs() + [last_feature, last_q]:
        copy.wait_send()
    for side in range(2):
        for k in range(1, 4):

            @pl.when(line_valid(side, k))
            def _(side=side, k=k):
                for kind in range(3):
                    line(side, k, kind).wait_send()

    for index in range(8):
        outputs(index).wait()


def handover_kernel(*refs):
    sources, targets, held, sem = refs[:8], refs[8:16], refs[16:24], refs[24]
    fetch = [
        pltpu.make_async_copy(sources[i], held[i], sem.at[0, i]) for i in range(len(sources))
    ]
    place = [
        pltpu.make_async_copy(held[i], targets[i], sem.at[1, i]) for i in range(len(sources))
    ]
    for copy in fetch:
        copy.start()
    for arrive, leave in zip(fetch, place):
        arrive.wait()
        leave.start()
    for copy in place:
        copy.wait()


def fused(
    tokens,
    norm_gain,
    cotangent,
    gate_frozen_weight,
    up_frozen_weight,
    down_frozen_weight,
    gate_input_factor,
    gate_output_factor,
    up_input_factor,
    up_output_factor,
    down_input_factor,
    down_b,
    gate_input_factor_direction,
    gate_output_factor_direction,
    up_input_factor_direction,
    up_output_factor_direction,
    down_input_factor_direction,
    down_b_dir,
    width,
):
    own, depth = tokens.shape
    hidden = gate_frozen_weight.shape[1]
    rank = gate_output_factor.shape[0]
    chunks = hidden // width
    chip, rest, count = 2 * own, 6 * own, 8 * own
    lead, gap = (8 * chunks) // 14, 3
    half_panel = 3 * width // 2
    f32, bf16 = jnp.float32, jnp.bfloat16
    vmem = pl.BlockSpec(memory_space=pltpu.VMEM)
    anywhere = pl.BlockSpec(memory_space=pl.ANY)

    def reduce_buffers(size):
        quarter = size // 4
        return [
            pltpu.VMEM((chunks, 2, 4, quarter, half_panel), bf16),
            pltpu.VMEM((chunks, 2, 2, quarter, half_panel), bf16),
            pltpu.VMEM((chunks, 2, quarter, half_panel), bf16),
            pltpu.VMEM((chunks, 2, quarter, half_panel), bf16),
            pltpu.VMEM((chunks, 2, 4, quarter, half_panel), bf16),
        ]

    dma = pltpu.SemaphoreType.DMA
    slots, sides = 7, 3
    shapes = [
        jax.ShapeDtypeStruct((own, depth), f32),
        jax.ShapeDtypeStruct((own, depth), f32),
        jax.ShapeDtypeStruct((rank, depth), f32),
        jax.ShapeDtypeStruct((rank, hidden), f32),
        jax.ShapeDtypeStruct((rank, depth), f32),
        jax.ShapeDtypeStruct((rank, hidden), f32),
        jax.ShapeDtypeStruct((rank, hidden), f32),
        jax.ShapeDtypeStruct((rank, depth), f32),
    ]
    results = pl.pallas_call(
        functools.partial(lora_kernel, lead, gap),
        out_shape=shapes,
        in_specs=[vmem] * 3 + [anywhere] * 15,
        out_specs=[anywhere] * 8,
        scratch_shapes=[pltpu.VMEM(shape.shape, f32) for shape in shapes]
        + [
            pltpu.VMEM((count, depth), bf16),
            pltpu.VMEM((count, depth), bf16),
            pltpu.VMEM((4, own, 2 * rank), f32),
            pltpu.VMEM((own, 6 * rank), bf16),
            pltpu.VMEM((4, own, 6 * rank), bf16),
            pltpu.VMEM((count, 6 * rank), bf16),
            pltpu.VMEM((count, 2 * rank), f32),
            pltpu.VMEM((3, 2 * rank, depth), bf16),
            pltpu.VMEM((3, 2 * rank, hidden), bf16),
            pltpu.VMEM((slots, 2, depth, width), bf16),
            pltpu.VMEM((sides, width, depth), bf16),
        ]
        + [
            pltpu.VMEM((chunks, 4, chip // 4, 3 * width), bf16),
            pltpu.VMEM((chunks, 3, chip // 4, 3 * width), bf16),
            pltpu.VMEM((chunks, 4, chip // 4, 3 * width), bf16),
        ]
        + reduce_buffers(rest)
        + [
            pltpu.VMEM((3, 2 * chip, 2 * rank), bf16),
            pltpu.VMEM((3, 2 * rank, chip), bf16),
            pltpu.VMEM((3, 2 * rest, 2 * rank), bf16),
            pltpu.VMEM((3, 2 * rank, rest), bf16),
            pltpu.VMEM((2, count, depth), f32),
            pltpu.VMEM((2, count, 2 * rank), f32),
            pltpu.VMEM((2, count, 2 * rank), f32),
            pltpu.VMEM((2, count, 2 * rank), f32),
            pltpu.VMEM((3, 2, own, depth), bf16),
            pltpu.VMEM((3, 2, own, depth), bf16),
            pltpu.VMEM((3, own, 6 * rank), bf16),
            pltpu.VMEM((3, own, 6 * rank), bf16),
            pltpu.VMEM((3, 2, own, depth), bf16),
            pltpu.VMEM((2, 3, 2, own, depth), bf16),
            pltpu.VMEM((3, own, 6 * rank), bf16),
            pltpu.VMEM((2, 3, own, 6 * rank), bf16),
            pltpu.VMEM((2, own, depth), bf16),
            pltpu.VMEM((2, own, depth), bf16),
            pltpu.VMEM((own, 6 * rank), bf16),
            pltpu.VMEM((own, 6 * rank), bf16),
            pltpu.VMEM((count, 4 * rank), bf16),
            dma((12,)),
            dma((slots, 2)),
            dma((sides,)),
            dma((2, 4)),
            dma((2, 4)),
            dma((2, 2, 3)),
            dma((2, 4)),
            dma((2, 4)),
            dma((2, 4)),
            dma((2, 8)),
            dma((2, 8)),
            dma((chunks, 2)),
            dma((chunks, 2)),
            dma((chunks, 2)),
            dma((chunks, 7)),
            dma((2, 2)),
            dma((2, 2, 3, 3)),
            dma((2, 2)),
            dma((2, 8)),
            dma((8,)),
        ],
        compiler_params=pltpu.CompilerParams(
            collective_id=2, has_side_effects=True, vmem_limit_bytes=63 * 1024 * 1024
        ),
        name="lora",
    )(
        tokens,
        norm_gain.reshape(1, depth),
        cotangent,
        gate_frozen_weight,
        up_frozen_weight,
        down_frozen_weight,
        gate_input_factor.T,
        gate_input_factor_direction.T,
        up_input_factor.T,
        up_input_factor_direction.T,
        down_b,
        down_b_dir,
        gate_output_factor,
        gate_output_factor_direction,
        up_output_factor,
        up_output_factor_direction,
        down_input_factor.T,
        down_input_factor_direction.T,
    )
    primal, direction, gate_input, gate_output, up_input, up_output, down_input, down_output = (
        pl.pallas_call(
            handover_kernel,
            out_shape=shapes,
            in_specs=[anywhere] * 8,
            out_specs=[anywhere] * 8,
            scratch_shapes=[pltpu.VMEM(shape.shape, f32) for shape in shapes] + [dma((2, 8))],
            name="handover",
        )(*results)
    )
    return (
        primal,
        direction,
        gate_input.T,
        gate_output,
        up_input.T,
        up_output,
        down_input.T,
        down_output,
    )


def gather_kernel(
    tokens,
    gain,
    cot,
    x_all,
    cot_all,
    x_buf,
    cot_buf,
    squares,
    square_send,
    square_recv,
    far_send,
    far_recv,
    near_send,
    near_recv,
):
    rows, columns = lax.axis_size("row"), lax.axis_size("col")
    chips = columns // 2
    my_row, me = lax.axis_index("row"), lax.axis_index("col")
    partner = me + 1 - 2 * lax.rem(me, 2)
    features = rows * tokens.shape[1]
    barrier = pltpu.get_barrier_semaphore()

    def row_peer(k):
        return {"row": lax.rem(my_row + k, rows)}

    def far_peer(k):
        return {"col": lax.rem(me + 2 * k, columns)}

    @pl.loop(1, rows)
    def _(k):
        pl.semaphore_signal(barrier, inc=1, device_id=row_peer(k), device_id_type=MESH)

    @pl.loop(1, chips)
    def _(k):
        pl.semaphore_signal(barrier, inc=1, device_id=far_peer(k), device_id_type=MESH)

    pl.semaphore_signal(barrier, inc=1, device_id={"col": partner}, device_id_type=MESH)

    buffers = (cot_buf, x_buf)

    def origin(k):
        return lax.rem(me - 2 * k + columns, columns)

    def square(k):
        return pltpu.make_async_remote_copy(
            src_ref=squares.at[0],
            dst_ref=squares.at[k],
            send_sem=square_send.at[k],
            recv_sem=square_recv.at[k],
            device_id=row_peer(k),
            device_id_type=MESH,
        )

    def far(which, k, slot):
        return pltpu.make_async_remote_copy(
            src_ref=buffers[which].at[slot],
            dst_ref=buffers[which].at[slot],
            send_sem=far_send.at[which, k],
            recv_sem=far_recv.at[which, k],
            device_id=far_peer(k),
            device_id_type=MESH,
        )

    def near(which, k, slot):
        return pltpu.make_async_remote_copy(
            src_ref=buffers[which].at[slot],
            dst_ref=buffers[which].at[slot],
            send_sem=near_send.at[which, k],
            recv_sem=near_recv.at[which, k],
            device_id={"col": partner},
            device_id_type=MESH,
        )

    def launch(which):
        @pl.loop(1, chips)
        def _(k):
            far(which, k, me).start()

        near(which, 0, me).start()

    values = tokens[...].astype(jnp.float32)
    squares[0] = jnp.broadcast_to(
        jnp.sum(values * values, axis=1, keepdims=True), squares.shape[1:]
    )
    cot_buf[me] = cot[...]
    pl.semaphore_wait(barrier, rows + chips - 1)

    @pl.loop(1, rows)
    def _(k):
        square(k).start()

    launch(0)

    def add(k, total):
        square(k).wait_recv()
        return total + squares[k]

    total = lax.fori_loop(1, rows, add, squares[0])
    scale = lax.rsqrt(total[:, :1] / features + epsilon)
    x_buf[me] = (tokens[...].astype(jnp.float32) * scale * gain[...]).astype(jnp.bfloat16)
    launch(1)
    for which in range(2):

        @pl.loop(1, chips)
        def _(k, which=which):
            far(which, k, origin(k)).wait_recv()
            near(which, k, origin(k)).start()

    for which in range(2):

        @pl.loop(0, chips)
        def _(k, which=which):
            near(which, k, lax.rem(partner - 2 * k + columns, columns)).wait_recv()

    @pl.loop(1, rows)
    def _(k):
        square(k).wait_send()

    for which in range(2):

        @pl.loop(1, chips)
        def _(k, which=which):
            far(which, k, me).wait_send()

        @pl.loop(0, chips)
        def _(k, which=which):
            near(which, k, origin(k)).wait_send()

    cot_all[...] = cot_buf[...]
    x_all[...] = x_buf[...]


def gathered(tokens, gain, cot):
    rows, columns = lax.axis_size("row"), lax.axis_size("col")
    own, depth = tokens.shape
    whole = (columns, own, depth)
    vmem = pl.BlockSpec(memory_space=pltpu.VMEM)
    x, panel = pl.pallas_call(
        gather_kernel,
        out_shape=[jax.ShapeDtypeStruct(whole, jnp.bfloat16)] * 2,
        in_specs=[vmem] * 3,
        out_specs=[vmem] * 2,
        scratch_shapes=[
            pltpu.VMEM(whole, jnp.bfloat16),
            pltpu.VMEM(whole, jnp.bfloat16),
            pltpu.VMEM((rows, own, 128), jnp.float32),
            pltpu.SemaphoreType.DMA((rows,)),
            pltpu.SemaphoreType.DMA((rows,)),
            pltpu.SemaphoreType.DMA((2, columns // 2)),
            pltpu.SemaphoreType.DMA((2, columns // 2)),
            pltpu.SemaphoreType.DMA((2, columns // 2)),
            pltpu.SemaphoreType.DMA((2, columns // 2)),
        ],
        compiler_params=pltpu.CompilerParams(collective_id=3, has_side_effects=True),
        name="gather",
    )(tokens, gain.reshape(1, depth), cot)
    return x.reshape(columns * own, depth), panel.reshape(columns * own, depth)


def chunk_count(width):
    for count in (4, 2):
        if width % (128 * count) == 0:
            return count
    return 1


def on_device(
    tokens,
    norm_gain,
    cotangent,
    gate_frozen_weight,
    up_frozen_weight,
    down_frozen_weight,
    gate_input_factor,
    gate_output_factor,
    up_input_factor,
    up_output_factor,
    down_input_factor,
    down_b,
    gate_input_factor_direction,
    gate_output_factor_direction,
    up_input_factor_direction,
    up_output_factor_direction,
    down_input_factor_direction,
    down_b_dir,
):
    width = 256
    if (
        lax.axis_size("row") == 4
        and lax.axis_size("col") == 8
        and gate_frozen_weight.shape[1] % (14 * width) == 0
        and gate_frozen_weight.shape[0] % 128 == 0
        and gate_input_factor.shape[1] == 64
        and tokens.shape[0] % 32 == 0
    ):
        return fused(
            tokens,
            norm_gain,
            cotangent,
            gate_frozen_weight,
            up_frozen_weight,
            down_frozen_weight,
            gate_input_factor,
            gate_output_factor,
            up_input_factor,
            up_output_factor,
            down_input_factor,
            down_b,
            gate_input_factor_direction,
            gate_output_factor_direction,
            up_input_factor_direction,
            up_output_factor_direction,
            down_input_factor_direction,
            down_b_dir,
            width,
        )
    rank = gate_input_factor.shape[1]
    width_rows, width_columns = gate_frozen_weight.shape
    own_count = tokens.shape[0]
    normed_tokens, cot_panel = gathered(tokens, norm_gain, cotangent)
    count = normed_tokens.shape[0]
    in_factors = jnp.concatenate(
        [
            gate_input_factor,
            up_input_factor,
            gate_input_factor_direction,
            up_input_factor_direction,
        ],
        axis=1,
    )
    out_factors = jnp.concatenate([down_b, down_b_dir], axis=0)

    projected = jnp.concatenate(
        [curvature_product(normed_tokens, in_factors), cross_shard_total(cot_panel, out_factors)],
        axis=1,
    )
    ranks = shard_total(projected, "row", 0)
    gate_out = jnp.concatenate([gate_output_factor, gate_output_factor_direction], axis=0)
    up_out = jnp.concatenate([up_output_factor, up_output_factor_direction], axis=0)
    down_in = jnp.concatenate([down_input_factor, down_input_factor_direction], axis=1)

    chunks = chunk_count(width_columns)
    wide = width_columns // chunks
    spans = [slice(index * wide, (index + 1) * wide) for index in range(chunks)]

    summed_chunks = []
    for span in spans:
        partial = (
            curvature_product(normed_tokens, gate_frozen_weight[:, span]).astype(jnp.bfloat16),
            curvature_product(normed_tokens, up_frozen_weight[:, span]).astype(jnp.bfloat16),
            cross_shard_total(cot_panel, down_frozen_weight[span]).astype(jnp.bfloat16),
        )
        if summed_chunks:
            partial, summed_chunks[-1] = lax.optimization_barrier((partial, summed_chunks[-1]))
        summed_chunks.append(lax.psum(partial, "row"))

    gate_low, up_low, gate_low_dir, up_low_dir, adj_low, adj_low_dir = [
        ranks[:, index * rank : (index + 1) * rank] for index in range(6)
    ]
    gate_pair = jnp.concatenate([gate_low_dir, gate_low], axis=1)
    up_pair = jnp.concatenate([up_low_dir, up_low], axis=1)
    adj_pair = jnp.concatenate([adj_low_dir, adj_low], axis=1)
    gate_stack = jnp.concatenate([gate_low_dir, gate_low], axis=0)
    up_stack = jnp.concatenate([up_low_dir, up_low], axis=0)
    adj_stack = jnp.concatenate([adj_low, adj_low_dir], axis=0)
    feature = 0.0
    gate_q = 0.0
    up_q = 0.0
    low_dir = 0.0
    gate_output, up_output, down_input = [], [], []
    for span, total in zip(spans, summed_chunks):
        gate_sum, up_sum, adj_sum = [value.astype(jnp.float32) for value in total]
        gate_pre = gate_sum + adapter_scale * curvature_product(
            gate_low, gate_output_factor[:, span]
        )
        up_pre = up_sum + adapter_scale * curvature_product(
            up_low, up_output_factor[:, span]
        )
        hidden_adj = adj_sum + adapter_scale * cross_shard_total(
            adj_low, down_input_factor[span]
        )
        gate_tan = adapter_scale * curvature_product(gate_pair, gate_out[:, span])
        up_tan = adapter_scale * curvature_product(up_pair, up_out[:, span])
        adj_tan = adapter_scale * cross_shard_total(adj_pair, down_in[span])
        hidden, hidden_dir, d_gate, d_up, d_gate_dir, d_up_dir = second_order(
            gate_pre, up_pre, hidden_adj, gate_tan, up_tan, adj_tan
        )
        gate_d = jnp.concatenate([d_gate, d_gate_dir], axis=0)
        up_d = jnp.concatenate([d_up, d_up_dir], axis=0)
        hidden_d = jnp.concatenate([hidden_dir, hidden], axis=0)
        gate_output.append(adapter_scale * summed_over_rows(gate_stack, gate_d))
        up_output.append(adapter_scale * summed_over_rows(up_stack, up_d))
        down_input.append(adapter_scale * summed_over_rows(hidden_d, adj_stack))
        gate_q = gate_q + cross_shard_total(gate_d, gate_out[:, span])
        up_q = up_q + cross_shard_total(up_d, up_out[:, span])
        low_dir = (
            low_dir
            + curvature_product(hidden_dir, down_input_factor[span])
            + curvature_product(hidden, down_input_factor_direction[span])
        )
        feature = (
            feature
            + cross_shard_total(gate_d, gate_frozen_weight[:, span])
            + cross_shard_total(up_d, up_frozen_weight[:, span])
        )
    gate_output = jnp.concatenate(gate_output, axis=1)
    up_output = jnp.concatenate(up_output, axis=1)
    down_input = jnp.concatenate(down_input, axis=0)

    summed = lax.psum_scatter(
        feature.astype(jnp.bfloat16).reshape(2, count, width_rows),
        "col",
        scatter_dimension=1,
        tiled=True,
    ).astype(jnp.float32)
    adjoints = shard_total(
        jnp.concatenate(
            [
                gate_q[:count, :rank],
                up_q[:count, :rank],
                gate_q[count:, :rank] + gate_q[:count, rank:],
                up_q[count:, :rank] + up_q[:count, rank:],
                low_dir,
            ],
            axis=1,
        ).astype(jnp.bfloat16),
        "col",
        1,
    )
    piece = lax.dynamic_slice_in_dim(adjoints, lax.axis_index("col") * own_count, own_count, 0)
    normed_feature_adjoint = summed[0] + adapter_scale * cross_shard_total(
        piece[:, : 2 * rank], in_factors[:, : 2 * rank]
    )
    normed_feature_adjoint_direction = summed[1] + adapter_scale * cross_shard_total(
        jnp.concatenate([piece[:, 2 * rank : 4 * rank], piece[:, : 2 * rank]], axis=1), in_factors
    )
    gate_input = adapter_scale * summed_over_rows(
        normed_tokens, adjoints[:, 2 * rank : 3 * rank]
    )
    up_input = adapter_scale * summed_over_rows(normed_tokens, adjoints[:, 3 * rank : 4 * rank])
    down_output = adapter_scale * summed_over_rows(adjoints[:, 4 * rank :], cot_panel)
    return (
        normed_feature_adjoint,
        normed_feature_adjoint_direction,
        gate_input,
        gate_output,
        up_input,
        up_output,
        down_input,
        down_output,
    )


def solution(mesh):
    in_specs = (
        P("col", "row"),
        P("row"),
        P("col", "row"),
        P("row", "col"),
        P("row", "col"),
        P("col", "row"),
        P("row", None),
        P(None, "col"),
        P("row", None),
        P(None, "col"),
        P("col", None),
        P(None, "row"),
        P("row", None),
        P(None, "col"),
        P("row", None),
        P(None, "col"),
        P("col", None),
        P(None, "row"),
    )
    out_specs = (
        P("col", "row"),
        P("col", "row"),
        P("row", None),
        P(None, "col"),
        P("row", None),
        P(None, "col"),
        P("col", None),
        P(None, "row"),
    )
    return jax.shard_map(
        on_device, mesh=mesh, in_specs=in_specs, out_specs=out_specs, check_vma=False
    )
```
